32 devices in a mesh: rep: 1, wide: 16 (over z, y, x), narrow: 2 (over core).
Axes of the slice: x: 2, y: 2, z: 4, core: 2. Of those that a mesh axis runs over, the one named last changes fastest.
Arguments:
- hidden_in: bfloat16 [2048, 2048], P(('rep', 'wide', 'narrow')), may hold values from -6 to 6
- queries: bfloat16 [2048, 2048], P(('rep', 'wide'), 'narrow')
- out_gate: bfloat16 [2048, 2048], P(('rep', 'wide'), 'narrow'), may hold values from -6 to 6
- draft_kv: bfloat16 [2, 2048, 256], P(None, ('rep', 'wide')), may hold values from -6 to 6
- cache_keys: bfloat16 [128, 256, 256], P(('rep', 'wide'))
- cache_values: bfloat16 [128, 256, 256], P(('rep', 'wide')), may hold values from -6 to 6
- draft_len: int32 [128], P(('rep', 'wide')), may hold values from 1 to 16, as said below
- cache_len: int32 [128], P(('rep', 'wide')), may hold values from 1 to 256, as said below
- o_weight: bfloat16 [2048, 2048], P('narrow'), may hold values from -0.125 to 0.125
- norm_gain: float32 [2048], replicated, may hold values from 0.5 to 1.5
- route_ids: int32 [2048, 10], P(('rep', 'wide', 'narrow')), may hold values from 0 to 31, all different within a row; in each aligned block of 64 rows (0 to 63, 64 to 127, ...) at most 30 rows name the same one
- route_weights: float32 [2048, 10], P(('rep', 'wide', 'narrow')), may hold values from 0.05 to 0.4
- w_gate: bfloat16 [32, 2048, 512], P(('wide', 'narrow')), may hold values from -0.125 to 0.125
- w_up: bfloat16 [32, 2048, 512], P(('wide', 'narrow')), may hold values from -0.125 to 0.125
- w_down: bfloat16 [32, 512, 2048], P(('wide', 'narrow')), may hold values from -0.25 to 0.25
Outputs:
- mixed: bfloat16 [2048, 2048], P(('rep', 'wide', 'narrow'))
The draws below stay inside these ranges and needn't reach their ends.
Inputs may be any that keep to these rules, and one draw needn't show every extreme that they name: `route_ids`: in each aligned block of 64 rows (the rows of one device) no expert is named by more than 30 pairs (row, choice), a bound that some block reaches. `draft_len`: some request has all 16 draft rows live. `cache_len`: some request has all 256 cache slots live.
All inputs are finite; a program needn't handle non-finite values.
Results may differ from the reference program's by a relative error of at most 0.0044.
Values may be sent and summed in bfloat16 or wider, within the bound.
A program may use at most 128 MiB of HBM per device.

```python
import math
import jax
import jax.numpy as jnp
import numpy as np
from jax import lax

D = 2048
HD = 256
FF = 512
TOPK = 10
Q_HEADS = 8
DRAFT = 16
CTX = 256
OWN = 64
REQS = 128
ROWS_ALL = 2048
EXPERTS = 32
CAP = 30


def draw_queries(key, part):
    values = jax.random.normal(key, (ROWS_ALL, Q_HEADS * HD), jnp.float32)
    return values.astype(jnp.bfloat16)


def draw_cache_keys(key, part):
    values = jax.random.normal(key, (REQS, CTX, HD), jnp.float32)
    return values.astype(jnp.bfloat16)


def draw_draft_len(key, part):
    lengths = jax.random.randint(key, (REQS,), 1, DRAFT + 1, dtype=jnp.int32)
    return lengths.at[0].set(DRAFT)


def draw_cache_len(key, part):
    lengths = jax.random.randint(key, (REQS,), 1, CTX + 1, dtype=jnp.int32)
    return lengths.at[0].set(CTX)


def shard_levels(stream_key, extent, pieces, least, high):
    factor_of, own = 1.0, jax.random.fold_in(stream_key, 6)
    for dim, parts in pieces:
        steps = jnp.exp(jax.random.uniform(jax.random.fold_in(own, dim), (parts,), jnp.float32, least / len(pieces), high / len(pieces)))
        factor_of = factor_of * jnp.repeat(steps, extent[dim] // parts).reshape([-1 if axis == dim else 1 for axis in range(len(extent))])
    return factor_of


def shared_out(rng, own, number, rows, count, top, reach, lean):
    order = jax.random.permutation(rng, count)
    heavy_load, ordinary = load_shares(count, rows * top, reach, lean, True), load_shares(count, rows * top, reach, lean, False)
    places = jnp.arange(count)

    def named(sizes, offset_by):
        used = int((sizes > 0).sum())
        fixed = max(1, used // 4)
        passed = fixed + (places - fixed + offset_by * (used - fixed)) % max(1, count - fixed)
        return jnp.zeros((count,), jnp.int32).at[order[jnp.where(places < fixed, places, passed)]].set(jnp.asarray(sizes, jnp.int32))

    sizes = jnp.where(number % 4 == 0, named(heavy_load, number // 4), named(ordinary, number - number // 4 - 1))
    mixed = jax.random.permutation(jax.random.fold_in(own, 3), count)
    donor, sink = mixed[0:count // 2 * 2:2], mixed[1:count // 2 * 2:2]
    room = jnp.minimum(sizes[donor] - 1, reach - sizes[sink]) // 2
    room = jnp.where((donor == order[0]) | (sink == order[0]) | (sizes[sink] == 0), 0, jnp.maximum(room, 0))
    passed = jax.random.randint(jax.random.fold_in(own, 4), (count // 2,), 0, 1 << 20) % (room + 1)
    sizes = sizes.at[donor].add(-passed).at[sink].add(passed)
    members = jnp.searchsorted(jnp.cumsum(sizes), jnp.arange(rows * top), side="right").astype(jnp.int32)
    table = members.reshape(top, rows).T
    table = table[jax.random.permutation(jax.random.fold_in(own, 1), rows)]
    offset_by = jax.random.randint(jax.random.fold_in(own, 2), (rows, 1), 0, top)
    return jnp.take_along_axis(table, (jnp.arange(top)[None, :] + offset_by) % top, axis=1)


def load_shares(number_of, total, reach, lean, full):
    weights = [(1 << 20) // math.isqrt(rank ** lean) + 1 for rank in range(1, number_of + 1)]
    largest = reach if full else min(reach, max(-(-total // number_of), total * weights[0] // sum(weights)))
    least = 1 if total - largest >= number_of - 1 else 0
    holding, rest = [largest] + [least] * (number_of - 1), total - largest - least * (number_of - 1)
    while rest > 0:
        free = [i for i in range(1, number_of) if holding[i] < largest] or [i for i in range(1, number_of) if holding[i] < reach]
        mass, left = sum([weights[i] for i in free]), rest
        for i in free:
            more = min(reach - holding[i], max(1, left * weights[i] // mass), rest)
            holding[i] = holding[i] + more
            rest = rest - more
    return np.array(holding)


def normal_values(key, extent, width, limit, shards=(), kind=jnp.bfloat16):
    array = width * jax.random.normal(key, extent, jnp.float32)
    if shards:
        array = array * shard_levels(key, extent, shards, -0.22, 0.18)
    return jnp.clip(array, -limit, limit).astype(kind)


def setup_inputs(seed: int = 0, part: int = 0) -> dict:
    streams_of = jax.random.split(jax.random.key(seed), 16)
    own_keys = jax.random.split(jax.random.fold_in(streams_of[15], part), 16)
    hidden_in = normal_values(own_keys[0], (ROWS_ALL, D), 1.0, 6.0, ((0, 32),))
    queries = draw_queries(jax.random.fold_in(jax.random.fold_in(streams_of[15], part), 71), part)
    out_gate = normal_values(own_keys[2], (ROWS_ALL, Q_HEADS * HD), 1.5, 6.0, ((0, 16), (1, 2)))
    draft_kv = normal_values(own_keys[3], (2, ROWS_ALL, HD), 1.0, 6.0, ((1, 16),))
    cache_keys = draw_cache_keys(jax.random.fold_in(jax.random.fold_in(streams_of[15], part), 71), part)
    cache_values = normal_values(own_keys[5], (REQS, CTX, HD), 1.0, 6.0, ((0, 16),))
    draft_len = draw_draft_len(jax.random.fold_in(jax.random.fold_in(streams_of[15], part), 71), part)
    cache_len = draw_cache_len(jax.random.fold_in(jax.random.fold_in(streams_of[15], part), 71), part)
    o_weight = normal_values(streams_of[8], (Q_HEADS * HD, D), (Q_HEADS * HD) ** -0.5, 0.125, ((0, 2),))
    norm_gain = jnp.clip(1.0 + 0.1 * jax.random.normal(streams_of[9], (D,), jnp.float32), 0.5, 1.5)
    route_ids_keys = jax.random.split(jax.random.fold_in(own_keys[10], 1), ROWS_ALL // OWN)
    route_ids_turns = jax.random.permutation(jax.random.fold_in(own_keys[10], 3), ROWS_ALL // OWN)
    route_ids = jax.vmap(lambda own, number: shared_out(jax.random.fold_in(own_keys[10], 2), own, number, OWN, EXPERTS, TOPK, CAP, 2))(route_ids_keys, route_ids_turns).reshape((ROWS_ALL, TOPK))
    route_weights = jnp.clip(0.05 + 0.35 * jax.random.uniform(own_keys[11], (ROWS_ALL, TOPK), jnp.float32) ** shard_levels(own_keys[11], (ROWS_ALL, TOPK), ((0, 32),), -0.2, 0.2), 0.05, 0.4)
    w_gate = normal_values(streams_of[12], (EXPERTS, D, FF), D ** -0.5, 0.125, ((0, 32),))
    w_up = normal_values(streams_of[13], (EXPERTS, D, FF), D ** -0.5, 0.125, ((0, 32),))
    w_down = normal_values(streams_of[14], (EXPERTS, FF, D), FF ** -0.5, 0.25, ((0, 32),))
    return {"hidden_in": hidden_in, "queries": queries, "out_gate": out_gate, "draft_kv": draft_kv, "cache_keys": cache_keys, "cache_values": cache_values, "draft_len": draft_len, "cache_len": cache_len, "o_weight": o_weight, "norm_gain": norm_gain, "route_ids": route_ids, "route_weights": route_weights, "w_gate": w_gate, "w_up": w_up, "w_down": w_down}


def attention_rows(queries, out_gate, draft_kv, cache_keys, cache_values, draft_len, cache_len):
    query_blocks = queries.reshape(REQS, DRAFT, Q_HEADS, HD).astype(jnp.float32)
    draft_keys = draft_kv[0].reshape(REQS, DRAFT, HD).astype(jnp.float32)
    draft_values = draft_kv[1].reshape(REQS, DRAFT, HD).astype(jnp.float32)
    score_scale = 1.0 / math.sqrt(HD)
    cache_scores = jnp.einsum('rjhd,rcd->rjhc', query_blocks, cache_keys.astype(jnp.float32)) * score_scale
    draft_scores = jnp.einsum('rjhd,rid->rjhi', query_blocks, draft_keys) * score_scale
    slots = jnp.arange(CTX, dtype=jnp.int32)
    cache_live = slots[None, :] < cache_len[:, None]
    cache_scores = jnp.where(cache_live[:, None, None, :], cache_scores, -jnp.inf)
    positions = jnp.arange(DRAFT, dtype=jnp.int32)
    causal = positions[None, :] <= positions[:, None]
    draft_live = causal[None, :, :] & (positions[None, None, :] < draft_len[:, None, None])
    draft_scores = jnp.where(draft_live[:, :, None, :], draft_scores, -jnp.inf)
    row_max = jnp.maximum(lax.optimization_barrier(jnp.max(cache_scores, axis=-1)), lax.optimization_barrier(jnp.max(draft_scores, axis=-1)))
    cache_probs = jnp.exp(cache_scores - row_max[..., None])
    draft_probs = jnp.exp(draft_scores - row_max[..., None])
    denominator = lax.optimization_barrier(jnp.sum(cache_probs, axis=-1)) + lax.optimization_barrier(jnp.sum(draft_probs, axis=-1))
    cache_probs = cache_probs.astype(jnp.bfloat16).astype(jnp.float32)
    draft_probs = draft_probs.astype(jnp.bfloat16).astype(jnp.float32)
    context = jnp.einsum('rjhc,rcd->rjhd', cache_probs, cache_values.astype(jnp.float32))
    context = context + jnp.einsum('rjhi,rid->rjhd', draft_probs, draft_values)
    context = context / denominator[..., None]
    gate_open = jax.nn.sigmoid(out_gate.astype(jnp.float32)).reshape(REQS, DRAFT, Q_HEADS, HD)
    row_live = (positions[None, :] < draft_len[:, None]).astype(jnp.float32)
    attended = context * gate_open * row_live[:, :, None, None]
    return attended.reshape(ROWS_ALL, Q_HEADS * HD).astype(jnp.bfloat16)

def reference(hidden_in, queries, out_gate, draft_kv, cache_keys, cache_values, draft_len, cache_len, o_weight, norm_gain, route_ids, route_weights, w_gate, w_up, w_down):
    attended = attention_rows(queries, out_gate, draft_kv, cache_keys, cache_values, draft_len, cache_len)
    residual = hidden_in.astype(jnp.float32) + jnp.dot(attended, o_weight, preferred_element_type=jnp.float32)
    spread = lax.optimization_barrier(jnp.mean(residual * residual, axis=-1, keepdims=True))
    normed = (residual * lax.rsqrt(spread + 1e-06) * norm_gain).astype(jnp.bfloat16)
    pair_total = ROWS_ALL * TOPK
    expert_rows = EXPERTS * CAP
    flat_ids = route_ids.reshape(-1).astype(jnp.int32)
    order = jnp.argsort(flat_ids, stable=True).astype(jnp.int32)
    sorted_ids = flat_ids[order]
    starts = jnp.searchsorted(sorted_ids, jnp.arange(EXPERTS, dtype=jnp.int32)).astype(jnp.int32)

    def one_expert(inputs):
        index, gate_mat, up_mat, down_mat = inputs
        position = starts[index] + jnp.arange(expert_rows, dtype=jnp.int32)
        clipped = jnp.minimum(position, pair_total - 1)
        inside = (position < pair_total) & (sorted_ids[clipped] == index)
        pair_index = order[clipped]
        row_block = normed[pair_index // TOPK]
        gate_proj = jnp.dot(row_block, gate_mat, preferred_element_type=jnp.float32)
        up_proj = jnp.dot(row_block, up_mat, preferred_element_type=jnp.float32)
        hidden_act = (jax.nn.silu(gate_proj) * up_proj).astype(jnp.bfloat16)
        produced = jnp.dot(hidden_act, down_mat, preferred_element_type=jnp.float32).astype(jnp.bfloat16)
        return (produced, jnp.where(inside, pair_index, pair_total).astype(jnp.int32))
    produced, destinations = lax.map(one_expert, (jnp.arange(EXPERTS, dtype=jnp.int32), w_gate, w_up, w_down))
    expert_out = jnp.zeros((pair_total, D), produced.dtype)
    expert_out = expert_out.at[destinations.reshape(-1)].set(produced.reshape(-1, D), mode='drop')
    expert_out = expert_out.reshape(ROWS_ALL, TOPK, D).astype(jnp.float32)
    expert_mix = lax.optimization_barrier(jnp.sum(route_weights[:, :, None] * expert_out, axis=1))
    return (residual + expert_mix).astype(jnp.bfloat16)
```

```python
import math

import functools

import jax
import jax.numpy as jnp
from jax import lax
from jax.experimental import pallas as pl
from jax.experimental.pallas import tpu as pltpu
from jax.sharding import PartitionSpec as P

MESH = pl.DeviceIdType.MESH


def attention_rows(queries, out_gate, draft_kv, cache_keys, cache_values, draft_len, cache_len):
    req_count, context_len, head_size = cache_keys.shape
    row_count = queries.shape[0]
    drafts = row_count // req_count
    head_count = queries.shape[1] // head_size
    query_blocks = queries.reshape(req_count, drafts, head_count, head_size)
    draft_keys = draft_kv[0].reshape(req_count, drafts, head_size)
    draft_values = draft_kv[1].reshape(req_count, drafts, head_size)
    score_scale = 1.0 / math.sqrt(head_size)
    cache_scores = (
        jnp.einsum("rjhd,rcd->rjhc", query_blocks, cache_keys, preferred_element_type=jnp.float32)
        * score_scale
    )
    draft_scores = (
        jnp.einsum("rjhd,rid->rjhi", query_blocks, draft_keys, preferred_element_type=jnp.float32)
        * score_scale
    )
    slots = jnp.arange(context_len, dtype=jnp.int32)
    cache_live = slots[None, :] < cache_len[:, None]
    cache_scores = jnp.where(cache_live[:, None, None, :], cache_scores, -jnp.inf)
    positions = jnp.arange(drafts, dtype=jnp.int32)
    causal = positions[None, :] <= positions[:, None]
    draft_live = causal[None, :, :] & (positions[None, None, :] < draft_len[:, None, None])
    draft_scores = jnp.where(draft_live[:, :, None, :], draft_scores, -jnp.inf)
    row_max = jnp.maximum(jnp.max(cache_scores, axis=-1), jnp.max(draft_scores, axis=-1))
    cache_probs = jnp.exp(cache_scores - row_max[..., None])
    draft_probs = jnp.exp(draft_scores - row_max[..., None])
    denominator = jnp.sum(cache_probs, axis=-1) + jnp.sum(draft_probs, axis=-1)
    context = jnp.einsum(
        "rjhc,rcd->rjhd",
        cache_probs.astype(jnp.bfloat16),
        cache_values,
        preferred_element_type=jnp.float32,
    )
    context = context + jnp.einsum(
        "rjhi,rid->rjhd",
        draft_probs.astype(jnp.bfloat16),
        draft_values,
        preferred_element_type=jnp.float32,
    )
    context = context / denominator[..., None]
    gate_open = jax.nn.sigmoid(out_gate.astype(jnp.float32)).reshape(
        req_count, drafts, head_count, head_size
    )
    row_live = (positions[None, :] < draft_len[:, None]).astype(jnp.float32)
    attended = context * gate_open * row_live[:, :, None, None]
    return attended.reshape(row_count, head_count * head_size).astype(jnp.bfloat16)


def plane_of(rep_count, wide_count):
    return 2 if rep_count == 1 and wide_count % 4 == 0 else 1


class Place:
    def __init__(self, side, wide_count):
        self.side, self.levels = side, wide_count // (side * side)
        wide = lax.axis_index("wide")
        self.core = lax.axis_index("narrow")
        self.z = wide // (side * side)
        self.y = (wide // side) % side
        self.x = wide % side
        c = self.core
        if side == 2:
            flip_y, flip_x = 1 - 2 * self.y, 1 - 2 * self.x
            self.y2, self.x2 = self.y + c * flip_y, self.x + (1 - c) * flip_x
            self.y3, self.x3 = self.y + (1 - c) * flip_y, self.x + c * flip_x
            self.y4, self.x4 = self.y + flip_y, self.x + flip_x

    def chip(self, z, kind):
        y, x = {
            1: (self.y, self.x),
            2: (getattr(self, "y2", 0), getattr(self, "x2", 0)),
            3: (getattr(self, "y3", 0), getattr(self, "x3", 0)),
            4: (getattr(self, "y4", 0), getattr(self, "x4", 0)),
        }[kind]
        return (z * self.side + y) * self.side + x

    def device(self, chip):
        return {"wide": chip, "narrow": self.core}

    def partner(self):
        return {"wide": self.chip(self.z, 1), "narrow": 1 - self.core}

    def greet(self):
        barrier = pltpu.get_barrier_semaphore()
        pl.semaphore_signal(barrier, inc=1, device_id=self.partner(), device_id_type=MESH)
        count = 1
        if self.side == 2:
            for kind in (2, 3):
                pl.semaphore_signal(
                    barrier,
                    inc=1,
                    device_id=self.device(self.chip(self.z, kind)),
                    device_id_type=MESH,
                )
            count = 3
        has_up, has_down = self.z < self.levels - 1, self.z > 0

        @pl.when(has_up)
        def _():
            pl.semaphore_signal(
                barrier, inc=1, device_id=self.device(self.chip(self.z + 1, 1)), device_id_type=MESH
            )

        @pl.when(has_down)
        def _():
            pl.semaphore_signal(
                barrier, inc=1, device_id=self.device(self.chip(self.z - 1, 1)), device_id_type=MESH
            )

        ends = has_up.astype(jnp.int32) + has_down.astype(jnp.int32)
        pl.semaphore_wait(barrier, count + ends)


def norm_rows(at, chunk, projected, hidden, gain, residual, rows_ref, theirs, meet):
    count = hidden.shape[0]
    swap = pltpu.make_async_remote_copy(
        src_ref=projected.at[1 - at.core],
        dst_ref=theirs,
        send_sem=meet.at[0],
        recv_sem=meet.at[1],
        device_id=at.partner(),
        device_id_type=MESH,
    )
    swap.start()
    swap.wait()

    @pl.loop(0, count, step=chunk)
    def _(row):
        part = pl.ds(pl.multiple_of(row, chunk), chunk)
        total = hidden[part, :].astype(jnp.float32) + (projected[at.core, part, :] + theirs[part, :])
        residual[part, :] = total
        spread = jnp.mean(total * total, axis=-1, keepdims=True)
        rows_ref[part, : total.shape[1]] = (total * lax.rsqrt(spread + 1e-06) * gain[...]).astype(rows_ref.dtype)


def layer_kernel(
    side, wide_count, chunk, slots, projected, hidden, gain, weights, gate_hbm, up_hbm, down_hbm,
    out, rows_all, terms, residual, theirs, gate_w, up_w, down_w, triangle, pick, pick_t, scale, picked, act,
    near, third, second, flow, meet, loads, g_sends, g_recvs, s_sends, s_recvs,
):
    at = Place(side, wide_count)
    z, levels, core = at.z, at.levels, at.core
    count, width = hidden.shape
    chips = side * side
    kinds = (4, 3, 2, 1) if side == 2 else (1,)
    group = 2 * chips
    experts = 2 * wide_count
    expert = at.chip(z, 1) * 2 + core
    fetch = [
        pltpu.make_async_copy(source.at[0], target, loads.at[i])
        for i, (source, target) in enumerate(((gate_hbm, gate_w), (up_hbm, up_w), (down_hbm, down_w)))
    ]
    for copy in fetch:
        copy.start()
    at.greet()
    own = rows_all.at[expert]
    norm_rows(at, chunk, projected, hidden, gain, residual, own, theirs, meet)
    own[:, width:] = weights[...]

    def carry(chip, block_core, lane, target):
        block = rows_all.at[chip * 2 + block_core]
        return pltpu.make_async_remote_copy(
            src_ref=block,
            dst_ref=block,
            send_sem=g_sends.at[chip, lane],
            recv_sem=g_recvs.at[chip * 2 + block_core],
            device_id=target,
            device_id_type=MESH,
        )

    def above():
        return at.device(at.chip(z + 1, 1))

    def below():
        return at.device(at.chip(z - 1, 1))

    def visit(distance, kind):
        for sign in (1, -1):
            level = z + sign * distance
            present = (distance >= 0) & (level >= 0) & (level < levels)
            if sign < 0:
                present = present & (distance > 0)

            @pl.when(present)
            def _():
                chip = at.chip(level, kind)
                if kind == 1:

                    @pl.when(distance > 0)
                    def _():
                        carry(chip, core, 4, at.partner()).wait_recv()

                    go_up = z < levels - 1
                    go_down = z > 0
                    if sign > 0:
                        go_up = go_up & (distance == 0)
                    else:
                        go_down = go_down & (distance == 0)

                    @pl.when(go_up)
                    def _():
                        carry(chip, core, 0, above()).start()

                    @pl.when(go_down)
                    def _():
                        carry(chip, core, 1, below()).start()

                    if side == 2:
                        carry(chip, core, 2, at.device(at.chip(z, 2))).start()
                else:
                    carry(chip, core, 4, at.partner()).wait_recv()
                if side == 2 and kind in (1, 2):
                    carry(chip, core, 3, at.device(at.chip(z, 3))).start()
                carry(chip, core, 4, at.partner()).start()

    def level_of(turn):
        low, high = z, levels - 1 - z
        less = (low < high).astype(jnp.int32)
        span = low * less + high * (1 - less)
        paired = (turn <= 2 * span).astype(jnp.int32)
        distance = paired * ((turn + 1) // 2) + (1 - paired) * (turn - span)
        sign = paired * (2 * (turn % 2) - 1) + (1 - paired) * (2 * less - 1)
        return z + sign * distance

    many = group * count
    tile = 512

    row = lax.broadcasted_iota(jnp.int32, (many, many), 0)
    other = lax.broadcasted_iota(jnp.int32, (many, many), 1)
    triangle[...] = ((other < row) & (other // count == row // count)).astype(jnp.float32).astype(jnp.bfloat16)

    def compute(level):
        base = level * group
        table = rows_all[pl.ds(base, group), :, width:].reshape(many, weights.shape[1])
        lane = lax.broadcasted_iota(jnp.int32, table.shape, 1)
        mine = jnp.where((lane == expert) | (lane == experts + expert), table.astype(jnp.float32), 0.0)
        mine = jnp.sum(mine, axis=1, keepdims=True)
        live = mine > 0.0
        flags = jnp.broadcast_to(live.astype(jnp.float32), (many, 128)).astype(jnp.bfloat16)
        order = jnp.dot(triangle[...], flags, preferred_element_type=jnp.float32)[:, :1]
        start = (lax.broadcasted_iota(jnp.int32, (many, 1), 0) // count * slots).astype(jnp.float32)
        seat = lax.broadcasted_iota(jnp.int32, (many, group * slots), 1).astype(jnp.float32)
        chosen = live & (seat == order + start)
        chosen = chosen.astype(jnp.float32)
        pick[...] = chosen.astype(jnp.bfloat16)
        pick_t[...] = chosen.T.astype(jnp.bfloat16)
        scale[...] = mine

        @pl.loop(0, width, step=tile)
        def _(column):
            part = pl.ds(pl.multiple_of(column, tile), tile)
            rows = rows_all[pl.ds(base, group), :, part].reshape(many, tile)
            picked[:, part] = jnp.dot(
                pick_t[...], rows, preferred_element_type=jnp.float32
            ).astype(jnp.bfloat16)

        gate_proj = jnp.dot(picked[...], gate_w[...], preferred_element_type=jnp.float32)
        up_proj = jnp.dot(picked[...], up_w[...], preferred_element_type=jnp.float32)
        act[...] = (gate_proj / (1.0 + jnp.exp(-gate_proj)) * up_proj).astype(jnp.bfloat16)

        @pl.loop(0, width, step=tile)
        def _(column):
            part = pl.ds(pl.multiple_of(column, tile), tile)
            produced = jnp.dot(act[...], down_w[:, part], preferred_element_type=jnp.float32)
            back = jnp.dot(pick[...], produced.astype(jnp.bfloat16), preferred_element_type=jnp.float32)
            sums = (back * scale[...]).astype(jnp.bfloat16)
            terms[pl.ds(base, group), :, part] = sums.reshape(group, count, tile)

    def copy_of(source, target, index, lane, chip, device):
        return pltpu.make_async_remote_copy(
            src_ref=source,
            dst_ref=target.at[index],
            send_sem=s_sends.at[lane, chip],
            recv_sem=s_recvs.at[lane, chip],
            device_id=device,
            device_id_type=MESH,
        )

    def to_partner(chip, block_core):
        return copy_of(terms.at[chip * 2 + block_core], near, chip, 0, chip, at.partner())

    def hop(kind, chip, level):
        held = terms.at[chip * 2 + core]
        if kind in (3, 4):
            return copy_of(held, third, chip, 1, chip, at.device(at.chip(z, 3)))
        return copy_of(held, second, level, 2, chip, at.device(at.chip(z, 2)))

    def rise(chip, level):
        return copy_of(terms.at[chip * 2 + core], flow, level, 3, chip, above())

    def fall(chip, level):
        ends = (level == z - 1).astype(jnp.int32)
        slot = level * (1 - ends) + levels * ends
        return copy_of(terms.at[chip * 2 + core], flow, slot, 4, chip, below())

    def fallen(chip):
        return copy_of(terms.at[chip * 2 + core], flow, levels, 4, chip, below())

    def add(chip, extra, last=False):
        @pl.loop(0, count, step=chunk)
        def _(row):
            part = pl.ds(pl.multiple_of(row, chunk), chunk)
            total = terms[chip * 2 + core, part, :].astype(jnp.float32)
            for ref, index in extra:
                total = total + ref[index, part, :].astype(jnp.float32)
            if last:
                out[part, :] = (residual[part, :] + total).astype(out.dtype)
            else:
                terms[chip * 2 + core, part, :] = total.astype(terms.dtype)

    def received(level, kind):
        chip = at.chip(level, kind)
        to_partner(chip, core).wait_recv()
        extra = [(near, chip)]
        if side == 2 and kind in (1, 2):
            hop(3, chip, level).wait_recv()
            extra.append((third, chip))
        if side == 2 and kind == 1:
            hop(2, chip, level).wait_recv()
            extra.append((second, level))
        return chip, extra

    def pass_on(level, kind):
        chip, extra = received(level, kind)
        add(chip, extra)
        hop(kind, chip, level).start()

    def first_along(level):
        @pl.when((z == 0) & (level > z))
        def _():
            chip, extra = received(level, 1)
            add(chip, extra)
            rise(chip, level).start()

        @pl.when((z == levels - 1) & (level < z))
        def _():
            chip, extra = received(level, 1)
            add(chip, extra)
            fall(chip, level).start()

    delay = 2 if side == 2 else 0

    @pl.loop(0, levels + delay)
    def _(step):
        visit(step, 1)
        if side == 2:
            visit(step - 1, 2)
            visit(step - 1, 3)
            visit(step - 2, 4)
        turn = step - delay

        @pl.when((turn >= 0) & (turn < levels))
        def _():
            level = level_of(turn)
            for kind in kinds:
                carry(at.chip(level, kind), 1 - core, 4, at.partner()).wait_recv()

            @pl.when(turn == 0)
            def _():
                for copy in fetch:
                    copy.wait()

            compute(level)
            for kind in kinds:
                to_partner(at.chip(level, kind), 1 - core).start()

    def last_along(level):
        first_along(level)

        @pl.when((z > 0) & (level > z))
        def _():
            chip, extra = received(level, 1)
            rise(chip, level).wait_recv()
            add(chip, extra + [(flow, level)])
            rise(chip, level).start()

        @pl.when((z < levels - 1) & (level < z))
        def _():
            chip, extra = received(level, 1)
            fall(chip, level).wait_recv()
            add(chip, extra + [(flow, level)])
            fall(chip, level).start()

    lag = 1 if side == 2 else 0

    @pl.loop(0, levels + 2 * lag)
    def _(step):
        if side == 2:

            @pl.when(step < levels)
            def _():
                level = level_of(levels - 1 - step)
                pass_on(level, 4)
                pass_on(level, 3)

            @pl.when((step >= lag) & (step < levels + lag))
            def _():
                pass_on(level_of(levels - 1 + lag - step), 2)

        @pl.when((step >= 2 * lag) & (step < levels + 2 * lag - 1))
        def _():
            last_along(level_of(levels - 1 + 2 * lag - step))

    chip, extra = received(z, 1)

    @pl.when(z > 0)
    def _():
        rise(chip, z).wait_recv()

    @pl.when(z < levels - 1)
    def _():
        fallen(chip).wait_recv()

    @pl.when((z > 0) & (z < levels - 1))
    def _():
        add(chip, extra + [(flow, z), (flow, levels)], last=True)

    @pl.when((z > 0) & (z == levels - 1))
    def _():
        add(chip, extra + [(flow, z)], last=True)

    @pl.when((z == 0) & (z < levels - 1))
    def _():
        add(chip, extra + [(flow, levels)], last=True)

    if levels == 1:
        add(chip, extra, last=True)

    @pl.loop(0, levels)
    def _(level):
        for kind in kinds:
            chip = at.chip(level, kind)
            carry(chip, core, 4, at.partner()).wait_send()
            if side == 2 and kind in (1, 2):
                carry(chip, core, 3, at.partner()).wait_send()
            to_partner(chip, 1 - core).wait_send()
            if kind != 1:
                hop(kind, chip, level).wait_send()
            else:
                if side == 2:
                    carry(chip, core, 2, at.partner()).wait_send()

                @pl.when((z < levels - 1) & (level <= z))
                def _():
                    carry(chip, core, 0, at.partner()).wait_send()

                @pl.when((z > 0) & (level >= z))
                def _():
                    carry(chip, core, 1, at.partner()).wait_send()

                @pl.when(level > z)
                def _():
                    rise(chip, level).wait_send()

                @pl.when(level < z)
                def _():
                    fall(chip, level).wait_send()


def run_layer(projected, hidden, gain, weights, w_gate, w_up, w_down, slots, side):
    wide_count = lax.axis_size("wide")
    blocks, chips = 2 * wide_count, side * side
    levels = wide_count // chips
    rows, width = hidden.shape
    block, half = (rows, width), jnp.bfloat16
    inner = w_gate.shape[2]
    seats, many = 2 * chips * slots, 2 * chips * rows
    lateral = wide_count if side == 2 else 1
    return pl.pallas_call(
        functools.partial(layer_kernel, side, wide_count, 16, slots),
        out_shape=jax.ShapeDtypeStruct(block, half),
        in_specs=[pl.BlockSpec(memory_space=pltpu.VMEM)] * 4
        + [pl.BlockSpec(memory_space=pl.ANY)] * 3,
        out_specs=pl.BlockSpec(memory_space=pltpu.VMEM),
        scratch_shapes=[
            pltpu.VMEM((blocks, rows, width + weights.shape[1]), half),
            pltpu.VMEM((blocks,) + block, half),
            pltpu.VMEM(block, jnp.float32),
            pltpu.VMEM(block, jnp.float32),
            pltpu.VMEM((width, inner), half),
            pltpu.VMEM((width, inner), half),
            pltpu.VMEM((inner, width), half),
            pltpu.VMEM((many, many), half),
            pltpu.VMEM((many, seats), half),
            pltpu.VMEM((seats, many), half),
            pltpu.VMEM((many, 1), jnp.float32),
            pltpu.VMEM((seats, width), half),
            pltpu.VMEM((seats, inner), half),
            pltpu.VMEM((wide_count,) + block, half),
            pltpu.VMEM((lateral,) + block, half),
            pltpu.VMEM((levels if side == 2 else 1,) + block, half),
            pltpu.VMEM((levels + 1,) + block, half),
            pltpu.SemaphoreType.DMA((2,)),
            pltpu.SemaphoreType.DMA((3,)),
            pltpu.SemaphoreType.DMA((wide_count, 5)),
            pltpu.SemaphoreType.DMA((blocks,)),
            pltpu.SemaphoreType.DMA((5, wide_count)),
            pltpu.SemaphoreType.DMA((5, wide_count)),
        ],
        compiler_params=pltpu.CompilerParams(
            collective_id=0, has_side_effects=True, vmem_limit_bytes=67043328
        ),
        name="run_layer",
    )(projected, hidden, gain, weights, w_gate, w_up, w_down)


class Grid:
    def __init__(self, levels):
        wide = lax.axis_index("wide")
        self.levels, self.core = levels, lax.axis_index("narrow")
        self.z, self.p = wide // 4, wide % 4
        y, x = self.p // 2, self.p % 2
        along_x, along_y = self.p + 1 - 2 * x, self.p + 2 - 4 * y
        c = self.core
        self.a = (1 - c) * along_x + c * along_y
        self.b = c * along_x + (1 - c) * along_y
        self.d = 3 - self.p
        self.has_up, self.has_down = self.z < levels - 1, self.z > 0

    def at(self, level, column):
        return {"wide": level * 4 + column, "narrow": self.core}

    def partner(self):
        return {"wide": self.z * 4 + self.p, "narrow": 1 - self.core}

    def up(self):
        return self.at(self.z + 1, self.p)

    def down(self):
        return self.at(self.z - 1, self.p)

    def greet(self):
        barrier = pltpu.get_barrier_semaphore()

        def hello(device):
            pl.semaphore_signal(barrier, inc=1, device_id=device, device_id_type=MESH)

        hello(self.partner())
        for column in (self.a, self.b, self.d):
            hello(self.at(self.z, column))
        for step in range(1, self.levels):
            hello(self.at(lax.rem(self.z + step, self.levels), self.p))
        pl.semaphore_wait(barrier, 3 + self.levels)

    def level_of(self, turn):
        low, high = self.z, self.levels - 1 - self.z
        less = (low < high).astype(jnp.int32)
        span = low * less + high * (1 - less)
        paired = (turn <= 2 * span).astype(jnp.int32)
        distance = paired * ((turn + 1) // 2) + (1 - paired) * (turn - span)
        sign = paired * (2 * (turn % 2) - 1) + (1 - paired) * (2 * less - 1)
        return self.z + sign * distance


def fast_kernel(
    levels, draft_len, cache_len, gain, ids, ratios, hidden_hbm, query_hbm, open_hbm, kv_hbm, keys_hbm, values_hbm,
    out_hbm, gate_hbm, up_hbm, down_hbm,
    out, rows_all, terms, near, from_b, from_a, from_b_q, from_a_q, flow_m, flow_q, tables, scale,
    hidden, query, opened, kv, keys, values, out_w, gate_w, up_w, down_w, attended, projected, theirs, residual, act,
    loads, meet, meet_in, t_sends, t_recvs, g_sends, g_recvs, s_sends, s_recvs,
):
    g = Grid(levels)
    z, p, core = g.z, g.p, g.core
    half = jnp.bfloat16
    count, width = hidden.shape
    quarter = count // 4
    main = count - quarter
    tail = 4 * main
    lot = 4 * count
    experts = 8 * levels
    expert = (z * 4 + p) * 2 + core
    tile = projected.shape[3]
    reqs, context_len, head_size = keys.shape
    drafts = query.shape[0] // reqs
    heads = query.shape[1] // head_size
    other = 1 - core

    pairs = (
        (query_hbm, query), (kv_hbm, kv), (keys_hbm, keys), (values_hbm, values), (open_hbm, opened),
        (out_hbm, out_w), (hidden_hbm, hidden), (gate_hbm.at[0], gate_w), (up_hbm.at[0], up_w), (down_hbm.at[0], down_w),
    )
    fetch = [pltpu.make_async_copy(source, target, loads.at[i]) for i, (source, target) in enumerate(pairs)]
    for copy in fetch:
        copy.start()

    def dense(part):
        lane = lax.broadcasted_iota(jnp.int32, tables.shape[3:], 1) % experts
        total = jnp.zeros(tables.shape[3:], jnp.float32)
        for k in range(ids.shape[1]):
            total = total + jnp.where(ids[part, k : k + 1] == lane, ratios[part, k : k + 1], 0.0)
        return total

    lane = lax.broadcasted_iota(jnp.int32, tables.shape[3:], 1)
    weight = jnp.where(lane < 2 * experts, dense(slice(0, count // 2)), dense(slice(count // 2, count)))
    high = weight.astype(half)
    low = (weight - high.astype(jnp.float32)).astype(half)
    tables[z, core, p] = jnp.where(lane % (2 * experts) < experts, high.astype(jnp.float32), low.astype(jnp.float32)).astype(half)

    g.greet()

    def send(source, target, send_sem, recv_sem, device):
        return pltpu.make_async_remote_copy(
            src_ref=source, dst_ref=target, send_sem=send_sem, recv_sem=recv_sem, device_id=device, device_id_type=MESH
        )

    def table_near(lane_id, column):
        block = tables.at[z, core, column]
        return send(block, block, t_sends.at[lane_id], t_recvs.at[lane_id], g.at(z, (g.a, g.b, g.d)[lane_id]))

    def table_far(step, level):
        block = tables.at[z, core]
        return send(block, block, t_sends.at[2 + step], t_recvs.at[3 + z], g.at(level, p))

    def table_far_in(level):
        block = tables.at[level, core]
        return send(block, block, t_sends.at[3], t_recvs.at[3 + level], g.at(z, p))

    def table_over(level, lane_core):
        block = tables.at[level, lane_core]
        return send(block, block, t_sends.at[2 + levels + level], t_recvs.at[3 + levels + level], g.partner())

    for i in range(3):
        table_near(i, p).start()

    def attend(first, last):
        for r in range(first, last):
            mine = slice(r * drafts, (r + 1) * drafts)
            q = jnp.concatenate([query[mine, h * head_size : (h + 1) * head_size] for h in range(heads)], axis=0)
            contract = (((1,), (1,)), ((), ()))
            s = lax.dot_general(q, keys[r], contract, preferred_element_type=jnp.float32) * (1.0 / math.sqrt(head_size))
            sd = lax.dot_general(q, kv[0], contract, preferred_element_type=jnp.float32) * (1.0 / math.sqrt(head_size))
            slot = lax.broadcasted_iota(jnp.int32, s.shape, 1)
            column = lax.broadcasted_iota(jnp.int32, sd.shape, 1) - r * drafts
            row = lax.broadcasted_iota(jnp.int32, sd.shape, 0) % drafts
            s = jnp.where(slot < cache_len[r], s, -jnp.inf)
            sd = jnp.where((column >= 0) & (column <= row) & (column < draft_len[r]), sd, -jnp.inf)
            top = jnp.maximum(jnp.max(s, axis=1, keepdims=True), jnp.max(sd, axis=1, keepdims=True))
            probs, probs_d = jnp.exp(s - top), jnp.exp(sd - top)
            total = jnp.sum(probs, axis=1, keepdims=True) + jnp.sum(probs_d, axis=1, keepdims=True)
            context = jnp.dot(probs.astype(half), values[r], preferred_element_type=jnp.float32)
            context = context + jnp.dot(probs_d.astype(half), kv[1], preferred_element_type=jnp.float32)
            context = context / total
            live = lax.broadcasted_iota(jnp.int32, (drafts, head_size), 0) < draft_len[r]
            for h in range(heads):
                part = slice(h * head_size, (h + 1) * head_size)
                shut = 1.0 + jnp.exp(-opened[mine, part].astype(jnp.float32))
                value = context[h * drafts : (h + 1) * drafts] / shut
                attended[mine, part] = jnp.where(live, value, 0.0).astype(half)

    for i in range(5):
        fetch[i].wait()
    attend(0, reqs // 2)
    for i, column in enumerate((g.a, g.b, g.d)):
        table_near(i, column).wait_recv()
    for step in range(1, levels):
        table_far(step, lax.rem(z + step, levels)).start()
    table_over(z, core).start()
    attend(reqs // 2, reqs)
    fetch[5].wait()

    def swap(i):
        return send(projected.at[i, other], theirs.at[i], meet.at[i], meet_in.at[i], g.partner())

    tiles = width // tile
    for i in range(tiles):
        product = jnp.dot(attended[...], out_w[:, i * tile : (i + 1) * tile], preferred_element_type=jnp.float32)
        projected[i] = product.reshape(2, count, tile)
        swap(i).start()
    fetch[6].wait()
    for i in range(tiles):
        swap(i).wait_recv()

    def m_rows(column):
        return pl.ds(pl.multiple_of(column * main, 16), main)

    def q_rows(column):
        return pl.ds(pl.multiple_of(tail + column * quarter, 16), quarter)

    q_all = pl.ds(tail, count)
    UP, DOWN, A, B, OVER = range(5)

    def target(way):
        return (g.up, g.down, lambda: g.at(z, g.a), lambda: g.at(z, g.b), g.partner)[way]()

    def carry(ref, way, level, slot, recv_slot):
        return send(ref, ref, g_sends.at[way, level, slot], g_recvs.at[level, recv_slot], target(way))

    def m_block(way, level, column, lane_core=core):
        return carry(rows_all.at[level, lane_core, m_rows(column)], way, level, column, column + 9 * (way == OVER))

    def q_block(way, level, column):
        return carry(rows_all.at[level, core, q_rows(column)], way, level, 4 + column, 4 + column)

    def q_level(way, level, lane_core=core):
        return carry(rows_all.at[level, lane_core, q_all], way, level, 8, 13 if way == OVER else 8)

    def along(level, copy):
        @pl.when(g.has_up & (level <= z))
        def _():
            copy(UP)

        @pl.when(g.has_down & (level >= z))
        def _():
            copy(DOWN)

    def norm(i):
        part = slice(i * 16, (i + 1) * 16)
        total = hidden[part, :].astype(jnp.float32) + jnp.concatenate(
            [projected[t, core, part, :] + theirs[t, part, :] for t in range(tiles)], axis=1
        )
        residual[part, :] = total
        spread = jnp.mean(total * total, axis=-1, keepdims=True)
        normed = (total * lax.rsqrt(spread + 1e-06) * gain[...]).astype(half)
        if i * 16 >= main:
            place = tail + p * quarter + i * 16 - main
        else:
            place = p * main + i * 16
        rows_all[z, core, pl.ds(pl.multiple_of(place, 16), 16), :] = normed

    for i in range(main // 16, count // 16):
        norm(i)
    q_block(A, z, p).start()
    q_block(B, z, p).start()
    for i in range(main // 16):
        norm(i)
    along(z, lambda way: m_block(way, z, p).start())
    for way in (A, B, OVER):
        m_block(way, z, p).start()

    for step in range(1, levels):
        table_far_in(lax.rem(z + step, levels)).wait_recv()
        table_over(lax.rem(z + step, levels), core).start()

    def m_first(turn):
        level = g.level_of(turn)
        m_block(A, level, p).wait_recv()
        along(level, lambda way: m_block(way, level, p).start())
        for way in (A, B, OVER):
            m_block(way, level, p).start()

    def compute(level):
        for lane_core in range(2):
            for column in range(4):
                block = tables[level, lane_core, column].astype(jnp.float32)
                for part in range(2):
                    first = 2 * part * experts + expert
                    mine = jnp.where((lane == first) | (lane == first + experts), block, 0.0)
                    mine = jnp.broadcast_to(jnp.sum(mine, axis=1, keepdims=True), block.shape)
                    for i in range(count // 2 // 16):
                        row = part * (count // 2) + i * 16
                        place = column * main + row if row < main else tail + column * quarter + row - main
                        scale[lane_core, place : place + 16, :] = mine[i * 16 : (i + 1) * 16]

        @pl.loop(0, 2)
        def _(i):
            lane_core = (1 - i) * other + i * core
            x = rows_all.at[level, lane_core]
            gate_proj = jnp.dot(x[...], gate_w[...], preferred_element_type=jnp.float32)
            up_proj = jnp.dot(x[...], up_w[...], preferred_element_type=jnp.float32)
            act[...] = (gate_proj / (1.0 + jnp.exp(-gate_proj)) * up_proj).astype(half)

            @pl.loop(0, width, step=512)
            def _(column):
                part = pl.ds(pl.multiple_of(column, 512), 512)
                produced = jnp.dot(act[...], down_w[:, part], preferred_element_type=jnp.float32)
                produced = produced.astype(half).astype(jnp.float32) * scale[lane_core, :, 0:1]
                terms[level, lane_core, :, part] = produced.astype(half)

            @pl.when(i == 0)
            def _():
                term_over(level, other).start()

    def term(ref, target_ref, index, level, device):
        return send(ref, target_ref, s_sends.at[index, level], s_recvs.at[index, level], device)

    def term_over(level, lane_core):
        return term(terms.at[level, lane_core], near.at[level], 0, level, g.partner())

    def b_term(level, column, slot):
        return term(terms.at[level, core, m_rows(column)], from_b.at[level, slot], 1 + slot, level, g.at(z, g.b))

    def a_term(level, column):
        return term(terms.at[level, core, m_rows(column)], from_a.at[level], 3, level, g.at(z, g.a))

    def rise_m(level):
        return term(terms.at[level, core, m_rows(p)], flow_m.at[0, level], 4, level, g.up())

    def fall_m(level):
        return term(terms.at[level, core, m_rows(p)], flow_m.at[1, level], 5, level, g.down())

    def rise_q(level):
        return term(terms.at[level, core, q_all], flow_q.at[0, level], 6, level, g.up())

    def fall_q(level):
        return term(terms.at[level, core, q_all], flow_q.at[1, level], 7, level, g.down())

    def b_term_q(column, slot):
        return term(terms.at[z, core, q_rows(column)], from_b_q.at[slot], 8 + slot, z, g.at(z, g.b))

    def a_term_q(column):
        return term(terms.at[z, core, q_rows(column)], from_a_q, 10, z, g.at(z, g.a))

    q_block(A, z, g.a).wait_recv()
    q_block(B, z, g.a).start()
    q_block(B, z, g.b).wait_recv()
    if levels > 1:
        m_first(1)

    @pl.loop(0, levels)
    def _(turn):
        level = g.level_of(turn)
        m_block(A, level, g.a).wait_recv()
        m_block(B, level, g.a).start()
        m_block(OVER, level, g.a).start()
        m_block(B, level, g.b).wait_recv()
        m_block(OVER, level, g.b).start()

        @pl.when(turn + 2 < levels)
        def _():
            m_first(turn + 2)

        @pl.when(turn == 0)
        def _():
            q_block(B, z, g.d).wait_recv()

        @pl.when(turn > 0)
        def _():
            q_level(UP, level).wait_recv()

        along(level, lambda way: q_level(way, level).start())
        q_level(OVER, level).start()
        m_block(B, level, g.d).wait_recv()
        m_block(OVER, level, g.d).start()

        @pl.when(turn == 0)
        def _():
            for copy in fetch[7:]:
                copy.wait()

        for column in range(4):
            m_block(OVER, level, column, other).wait_recv()
        q_level(OVER, level, other).wait_recv()
        table_over(level, other).wait_recv()
        compute(level)

    def add(level, start, size, extra, last=None):
        @pl.loop(0, size, step=16)
        def _(row):
            row = pl.multiple_of(row, 16)
            part = pl.ds(pl.multiple_of(start + row, 16), 16)
            total = terms[level, core, part, :].astype(jnp.float32) + near[level, part, :].astype(jnp.float32)
            for ref in extra:
                total = total + ref[pl.ds(row, 16), :].astype(jnp.float32)
            if last is None:
                terms[level, core, part, :] = total.astype(half)
            else:
                rest = pl.ds(pl.multiple_of(last + row, 16), 16)
                out[rest, :] = (residual[rest, :] + total).astype(half)

    def add_flow(level, start, size, ref):
        @pl.loop(0, size, step=16)
        def _(row):
            row = pl.multiple_of(row, 16)
            part = pl.ds(pl.multiple_of(start + row, 16), 16)
            total = terms[level, core, part, :].astype(jnp.float32) + ref[pl.ds(row, 16), :].astype(jnp.float32)
            terms[level, core, part, :] = total.astype(half)

    def m_start(column):
        return column * main

    def q_start(column):
        return tail + column * quarter

    def stage_1(turn):
        level = g.level_of(turn)
        term_over(level, other).wait_recv()
        add(level, m_start(g.d), main, [])
        b_term(level, g.d, 1).start()
        add(level, m_start(g.b), main, [])
        b_term(level, g.b, 0).start()

    def stage_q(turn):
        level = g.level_of(turn)

        @pl.when((level < z) | (turn == 0))
        def _():
            @pl.when(g.has_up)
            def _():
                fall_q(level).wait_recv()
                add_flow(level, tail, count, flow_q.at[1, level])

        @pl.when((level > z) | (turn == 0))
        def _():
            @pl.when(g.has_down)
            def _():
                rise_q(level).wait_recv()
                add_flow(level, tail, count, flow_q.at[0, level])

        @pl.when(turn > 0)
        def _():
            add(level, tail, count, [])

            @pl.when(level > z)
            def _():
                rise_q(level).start()

            @pl.when(level < z)
            def _():
                fall_q(level).start()

        @pl.when(turn == 0)
        def _():
            add(level, q_start(g.d), quarter, [])
            b_term_q(g.d, 1).start()
            add(level, q_start(g.b), quarter, [])
            b_term_q(g.b, 0).start()

    def stage_2(turn):
        level = g.level_of(turn)
        b_term(level, g.d, 1).wait_recv()
        add(level, m_start(g.a), main, [from_b.at[level, 1]])
        a_term(level, g.a).start()

        @pl.when(turn == 0)
        def _():
            b_term_q(g.d, 1).wait_recv()
            add(level, q_start(g.a), quarter, [from_b_q.at[1]])
            a_term_q(g.a).start()

    def stage_3(turn):
        level = g.level_of(turn)

        @pl.when((level < z) | (turn == 0))
        def _():
            @pl.when(g.has_up)
            def _():
                fall_m(level).wait_recv()
                add_flow(level, m_start(p), main, flow_m.at[1, level])

        @pl.when((level > z) | (turn == 0))
        def _():
            @pl.when(g.has_down)
            def _():
                rise_m(level).wait_recv()
                add_flow(level, m_start(p), main, flow_m.at[0, level])

        b_term(level, g.b, 0).wait_recv()
        a_term(level, g.a).wait_recv()

        @pl.when(turn > 0)
        def _():
            add(level, m_start(p), main, [from_b.at[level, 0], from_a.at[level]])

            @pl.when(level > z)
            def _():
                rise_m(level).start()

            @pl.when(level < z)
            def _():
                fall_m(level).start()

        @pl.when(turn == 0)
        def _():
            add(level, m_start(p), main, [from_b.at[level, 0], from_a.at[level]], last=0)
            b_term_q(g.b, 0).wait_recv()
            a_term_q(g.a).wait_recv()
            add(level, q_start(p), quarter, [from_b_q.at[0], from_a_q], last=main)

    @pl.loop(0, levels + 2)
    def _(step):
        @pl.when(step < levels)
        def _():
            stage_1(levels - 1 - step)

        @pl.when((step >= 1) & (step < levels + 1))
        def _():
            stage_2(levels - step)

        @pl.when(step < levels)
        def _():
            stage_q(levels - 1 - step)

        @pl.when(step >= 2)
        def _():
            stage_3(levels + 1 - step)

    for i in range(3):
        table_near(i, p).wait_send()
    for step in range(1, levels):
        table_far(step, lax.rem(z + step, levels)).wait_send()
    for i in range(tiles):
        swap(i).wait_send()
    q_block(A, z, p).wait_send()
    q_block(B, z, p).wait_send()
    q_block(B, z, g.a).wait_send()
    b_term_q(g.d, 1).wait_send()
    b_term_q(g.b, 0).wait_send()
    a_term_q(g.a).wait_send()

    @pl.loop(0, levels)
    def _(level):
        table_over(level, core).wait_send()
        along(level, lambda way: m_block(way, level, p).wait_send())
        along(level, lambda way: q_level(way, level).wait_send())
        for way in (A, B, OVER):
            m_block(way, level, p).wait_send()
        for way in (B, OVER):
            m_block(way, level, g.a).wait_send()
        m_block(OVER, level, g.b).wait_send()
        m_block(OVER, level, g.d).wait_send()
        q_level(OVER, level).wait_send()
        term_over(level, other).wait_send()
        b_term(level, g.d, 1).wait_send()
        b_term(level, g.b, 0).wait_send()
        a_term(level, g.a).wait_send()

        @pl.when(level > z)
        def _():
            rise_m(level).wait_send()
            rise_q(level).wait_send()

        @pl.when(level < z)
        def _():
            fall_m(level).wait_send()
            fall_q(level).wait_send()


def run_fast(
    hidden, queries, out_gate, draft_kv, cache_keys, cache_values, draft_len, cache_len, o_weight, norm_gain,
    route_ids, route_weights, w_gate, w_up, w_down,
):
    levels = lax.axis_size("wide") // 4
    count, width = hidden.shape
    quarter = count // 4
    main, lot = count - quarter, 4 * count
    inner = w_gate.shape[2]
    half = jnp.bfloat16
    tile = 512
    lanes = max(128, 32 * levels)
    dma = pltpu.SemaphoreType.DMA
    vmem, smem, hbm = (pl.BlockSpec(memory_space=space) for space in (pltpu.VMEM, pltpu.SMEM, pl.ANY))
    return pl.pallas_call(
        functools.partial(fast_kernel, levels),
        out_shape=jax.ShapeDtypeStruct((count, width), half),
        in_specs=[smem] * 2 + [vmem] * 3 + [hbm] * 10,
        out_specs=vmem,
        scratch_shapes=[
            pltpu.VMEM((levels, 2, lot, width), half),
            pltpu.VMEM((levels, 2, lot, width), half),
            pltpu.VMEM((levels, lot, width), half),
            pltpu.VMEM((levels, 2, main, width), half),
            pltpu.VMEM((levels, main, width), half),
            pltpu.VMEM((2, quarter, width), half),
            pltpu.VMEM((quarter, width), half),
            pltpu.VMEM((2, levels, main, width), half),
            pltpu.VMEM((2, levels, count, width), half),
            pltpu.VMEM((levels, 2, 4, count // 2, lanes), half),
            pltpu.VMEM((2, lot, lanes), jnp.float32),
            pltpu.VMEM(hidden.shape, half),
            pltpu.VMEM(queries.shape, half),
            pltpu.VMEM(out_gate.shape, half),
            pltpu.VMEM(draft_kv.shape, half),
            pltpu.VMEM(cache_keys.shape, half),
            pltpu.VMEM(cache_values.shape, half),
            pltpu.VMEM(o_weight.shape, half),
            pltpu.VMEM((width, inner), half),
            pltpu.VMEM((width, inner), half),
            pltpu.VMEM((inner, width), half),
            pltpu.VMEM(queries.shape, half),
            pltpu.VMEM((width // tile, 2, count, tile), jnp.float32),
            pltpu.VMEM((width // tile, count, tile), jnp.float32),
            pltpu.VMEM((count, width), jnp.float32),
            pltpu.VMEM((lot, inner), half),
            dma((10,)),
            dma((width // tile,)),
            dma((width // tile,)),
            dma((2 + 2 * levels,)),
            dma((3 + 2 * levels,)),
            dma((5, levels, 9)),
            dma((levels, 14)),
            dma((11, levels)),
            dma((11, levels)),
        ],
        compiler_params=pltpu.CompilerParams(
            collective_id=0, has_side_effects=True, vmem_limit_bytes=67043328
        ),
        name="run_layer",
    )(
        draft_len, cache_len, norm_gain[None, :], route_ids, route_weights, hidden, queries, out_gate, draft_kv,
        cache_keys, cache_values, o_weight, w_gate, w_up, w_down,
    )


def fits_fast(hidden_in, queries, cache_keys):
    levels = lax.axis_size("wide") // 4
    drafts = queries.shape[0] // cache_keys.shape[0]
    return (
        plane_of(lax.axis_size("rep"), lax.axis_size("wide")) == 2
        and hidden_in.shape[0] % 64 == 0
        and hidden_in.shape[1] % 512 == 0
        and drafts % 16 == 0
        and cache_keys.shape[0] % 2 == 0
        and levels * 32 <= 128
    )


def on_device(
    hidden_in,
    queries,
    out_gate,
    draft_kv,
    cache_keys,
    cache_values,
    draft_len,
    cache_len,
    o_weight,
    norm_gain,
    route_ids,
    route_weights,
    w_gate,
    w_up,
    w_down,
):
    if fits_fast(hidden_in, queries, cache_keys):
        return run_fast(
            hidden_in, queries, out_gate, draft_kv, cache_keys, cache_values, draft_len, cache_len, o_weight,
            norm_gain, route_ids, route_weights, w_gate, w_up, w_down,
        )
    attended = attention_rows(
        queries, out_gate, draft_kv, cache_keys, cache_values, draft_len, cache_len
    )
    own_rows = hidden_in.shape[0]
    width = hidden_in.shape[1]
    projected = jnp.dot(attended, o_weight, preferred_element_type=jnp.float32)
    projected = projected.reshape(2, own_rows, width)
    top_count = route_ids.shape[1]
    experts = lax.axis_size("wide") * lax.axis_size("narrow")
    capacity = max(2, min(own_rows, (3 * own_rows * top_count + 2 * experts - 1) // (2 * experts)))
    slots = -(-capacity // 16) * 16
    chosen = route_ids[:, :, None] == jnp.arange(experts, dtype=jnp.int32)[None, None, :]
    dense = jnp.sum(jnp.where(chosen, route_weights[:, :, None], 0.0), axis=1)
    coarse = lax.reduce_precision(dense, 8, 7)
    weights = jnp.concatenate([coarse, dense - coarse], axis=1).astype(jnp.bfloat16)
    weights = jnp.pad(weights, ((0, 0), (0, -weights.shape[1] % 128)))
    side = plane_of(lax.axis_size("rep"), lax.axis_size("wide"))
    return run_layer(
        projected, hidden_in, norm_gain[None, :], weights, w_gate, w_up, w_down, slots, side
    )


def solution(mesh):
    placed = (
        P(("rep", "wide", "narrow"), None),
        P(("rep", "wide"), "narrow"),
        P(("rep", "wide"), "narrow"),
        P(None, ("rep", "wide"), None),
        P(("rep", "wide"), None, None),
        P(("rep", "wide"), None, None),
        P(("rep", "wide")),
        P(("rep", "wide")),
        P("narrow", None),
        P(),
        P(("rep", "wide", "narrow"), None),
        P(("rep", "wide", "narrow"), None),
        P(("wide", "narrow"), None, None),
        P(("wide", "narrow"), None, None),
        P(("wide", "narrow"), None, None),
    )
    return jax.shard_map(
        on_device,
        mesh=mesh,
        in_specs=placed,
        out_specs=P(("rep", "wide", "narrow"), None),
        check_vma=False,
    )
```

```python
import math

import functools

import jax
import jax.numpy as jnp
from jax import lax
from jax.experimental import pallas as pl
from jax.experimental.pallas import tpu as pltpu
from jax.sharding import PartitionSpec as P

MESH = pl.DeviceIdType.MESH


def attention_rows(queries, out_gate, draft_kv, cache_keys, cache_values, draft_len, cache_len):
    req_count, context_len, head_size = cache_keys.shape
    row_count = queries.shape[0]
    drafts = row_count // req_count
    head_count = queries.shape[1] // head_size
    query_blocks = queries.reshape(req_count, drafts, head_count, head_size)
    draft_keys = draft_kv[0].reshape(req_count, drafts, head_size)
    draft_values = draft_kv[1].reshape(req_count, drafts, head_size)
    score_scale = 1.0 / math.sqrt(head_size)
    cache_scores = (
        jnp.einsum("rjhd,rcd->rjhc", query_blocks, cache_keys, preferred_element_type=jnp.float32)
        * score_scale
    )
    draft_scores = (
        jnp.einsum("rjhd,rid->rjhi", query_blocks, draft_keys, preferred_element_type=jnp.float32)
        * score_scale
    )
    slots = jnp.arange(context_len, dtype=jnp.int32)
    cache_live = slots[None, :] < cache_len[:, None]
    cache_scores = jnp.where(cache_live[:, None, None, :], cache_scores, -jnp.inf)
    positions = jnp.arange(drafts, dtype=jnp.int32)
    causal = positions[None, :] <= positions[:, None]
    draft_live = causal[None, :, :] & (positions[None, None, :] < draft_len[:, None, None])
    draft_scores = jnp.where(draft_live[:, :, None, :], draft_scores, -jnp.inf)
    row_max = jnp.maximum(jnp.max(cache_scores, axis=-1), jnp.max(draft_scores, axis=-1))
    cache_probs = jnp.exp(cache_scores - row_max[..., None])
    draft_probs = jnp.exp(draft_scores - row_max[..., None])
    denominator = jnp.sum(cache_probs, axis=-1) + jnp.sum(draft_probs, axis=-1)
    context = jnp.einsum(
        "rjhc,rcd->rjhd",
        cache_probs.astype(jnp.bfloat16),
        cache_values,
        preferred_element_type=jnp.float32,
    )
    context = context + jnp.einsum(
        "rjhi,rid->rjhd",
        draft_probs.astype(jnp.bfloat16),
        draft_values,
        preferred_element_type=jnp.float32,
    )
    context = context / denominator[..., None]
    gate_open = jax.nn.sigmoid(out_gate.astype(jnp.float32)).reshape(
        req_count, drafts, head_count, head_size
    )
    row_live = (positions[None, :] < draft_len[:, None]).astype(jnp.float32)
    attended = context * gate_open * row_live[:, :, None, None]
    return attended.reshape(row_count, head_count * head_size).astype(jnp.bfloat16)


def plane_of(rep_count, wide_count):
    return 2 if rep_count == 1 and wide_count % 4 == 0 else 1


class Place:
    def __init__(self, side, wide_count):
        self.side, self.levels = side, wide_count // (side * side)
        wide = lax.axis_index("wide")
        self.core = lax.axis_index("narrow")
        self.z = wide // (side * side)
        self.y = (wide // side) % side
        self.x = wide % side
        c = self.core
        if side == 2:
            flip_y, flip_x = 1 - 2 * self.y, 1 - 2 * self.x
            self.y2, self.x2 = self.y + c * flip_y, self.x + (1 - c) * flip_x
            self.y3, self.x3 = self.y + (1 - c) * flip_y, self.x + c * flip_x
            self.y4, self.x4 = self.y + flip_y, self.x + flip_x

    def chip(self, z, kind):
        y, x = {
            1: (self.y, self.x),
            2: (getattr(self, "y2", 0), getattr(self, "x2", 0)),
            3: (getattr(self, "y3", 0), getattr(self, "x3", 0)),
            4: (getattr(self, "y4", 0), getattr(self, "x4", 0)),
        }[kind]
        return (z * self.side + y) * self.side + x

    def device(self, chip):
        return {"wide": chip, "narrow": self.core}

    def partner(self):
        return {"wide": self.chip(self.z, 1), "narrow": 1 - self.core}

    def greet(self):
        barrier = pltpu.get_barrier_semaphore()
        pl.semaphore_signal(barrier, inc=1, device_id=self.partner(), device_id_type=MESH)
        count = 1
        if self.side == 2:
            for kind in (2, 3):
                pl.semaphore_signal(
                    barrier,
                    inc=1,
                    device_id=self.device(self.chip(self.z, kind)),
                    device_id_type=MESH,
                )
            count = 3
        has_up, has_down = self.z < self.levels - 1, self.z > 0

        @pl.when(has_up)
        def _():
            pl.semaphore_signal(
                barrier, inc=1, device_id=self.device(self.chip(self.z + 1, 1)), device_id_type=MESH
            )

        @pl.when(has_down)
        def _():
            pl.semaphore_signal(
                barrier, inc=1, device_id=self.device(self.chip(self.z - 1, 1)), device_id_type=MESH
            )

        ends = has_up.astype(jnp.int32) + has_down.astype(jnp.int32)
        pl.semaphore_wait(barrier, count + ends)


def norm_rows(at, chunk, projected, hidden, gain, residual, rows_ref, theirs, meet):
    count = hidden.shape[0]
    swap = pltpu.make_async_remote_copy(
        src_ref=projected.at[1 - at.core],
        dst_ref=theirs,
        send_sem=meet.at[0],
        recv_sem=meet.at[1],
        device_id=at.partner(),
        device_id_type=MESH,
    )
    swap.start()
    swap.wait()

    @pl.loop(0, count, step=chunk)
    def _(row):
        part = pl.ds(pl.multiple_of(row, chunk), chunk)
        total = hidden[part, :].astype(jnp.float32) + (projected[at.core, part, :] + theirs[part, :])
        residual[part, :] = total
        spread = jnp.mean(total * total, axis=-1, keepdims=True)
        rows_ref[part, : total.shape[1]] = (total * lax.rsqrt(spread + 1e-06) * gain[...]).astype(rows_ref.dtype)


def layer_kernel(
    side, wide_count, chunk, slots, projected, hidden, gain, weights, gate_hbm, up_hbm, down_hbm,
    out, rows_all, terms, residual, theirs, gate_w, up_w, down_w, triangle, pick, pick_t, scale, picked, act,
    near, third, second, flow, meet, loads, g_sends, g_recvs, s_sends, s_recvs,
):
    at = Place(side, wide_count)
    z, levels, core = at.z, at.levels, at.core
    count, width = hidden.shape
    chips = side * side
    kinds = (4, 3, 2, 1) if side == 2 else (1,)
    group = 2 * chips
    experts = 2 * wide_count
    expert = at.chip(z, 1) * 2 + core
    fetch = [
        pltpu.make_async_copy(source.at[0], target, loads.at[i])
        for i, (source, target) in enumerate(((gate_hbm, gate_w), (up_hbm, up_w), (down_hbm, down_w)))
    ]
    for copy in fetch:
        copy.start()
    at.greet()
    own = rows_all.at[expert]
    norm_rows(at, chunk, projected, hidden, gain, residual, own, theirs, meet)
    own[:, width:] = weights[...]

    def carry(chip, block_core, lane, target):
        block = rows_all.at[chip * 2 + block_core]
        return pltpu.make_async_remote_copy(
            src_ref=block,
            dst_ref=block,
            send_sem=g_sends.at[chip, lane],
            recv_sem=g_recvs.at[chip * 2 + block_core],
            device_id=target,
            device_id_type=MESH,
        )

    def above():
        return at.device(at.chip(z + 1, 1))

    def below():
        return at.device(at.chip(z - 1, 1))

    def visit(distance, kind):
        for sign in (1, -1):
            level = z + sign * distance
            present = (distance >= 0) & (level >= 0) & (level < levels)
            if sign < 0:
                present = present & (distance > 0)

            @pl.when(present)
            def _():
                chip = at.chip(level, kind)
                if kind == 1:

                    @pl.when(distance > 0)
                    def _():
                        carry(chip, core, 4, at.partner()).wait_recv()

                    go_up = z < levels - 1
                    go_down = z > 0
                    if sign > 0:
                        go_up = go_up & (distance == 0)
                    else:
                        go_down = go_down & (distance == 0)

                    @pl.when(go_up)
                    def _():
                        carry(chip, core, 0, above()).start()

                    @pl.when(go_down)
                    def _():
                        carry(chip, core, 1, below()).start()

                    if side == 2:
                        carry(chip, core, 2, at.device(at.chip(z, 2))).start()
                else:
                    carry(chip, core, 4, at.partner()).wait_recv()
                if side == 2 and kind in (1, 2):
                    carry(chip, core, 3, at.device(at.chip(z, 3))).start()
                carry(chip, core, 4, at.partner()).start()

    def level_of(turn):
        low, high = z, levels - 1 - z
        less = (low < high).astype(jnp.int32)
        span = low * less + high * (1 - less)
        paired = (turn <= 2 * span).astype(jnp.int32)
        distance = paired * ((turn + 1) // 2) + (1 - paired) * (turn - span)
        sign = paired * (2 * (turn % 2) - 1) + (1 - paired) * (2 * less - 1)
        return z + sign * distance

    many = group * count
    tile = 512

    row = lax.broadcasted_iota(jnp.int32, (many, many), 0)
    other = lax.broadcasted_iota(jnp.int32, (many, many), 1)
    triangle[...] = ((other < row) & (other // count == row // count)).astype(jnp.float32).astype(jnp.bfloat16)

    def compute(level):
        base = level * group
        table = rows_all[pl.ds(base, group), :, width:].reshape(many, weights.shape[1])
        lane = lax.broadcasted_iota(jnp.int32, table.shape, 1)
        mine = jnp.where((lane == expert) | (lane == experts + expert), table.astype(jnp.float32), 0.0)
        mine = jnp.sum(mine, axis=1, keepdims=True)
        live = mine > 0.0
        flags = jnp.broadcast_to(live.astype(jnp.float32), (many, 128)).astype(jnp.bfloat16)
        order = jnp.dot(triangle[...], flags, preferred_element_type=jnp.float32)[:, :1]
        start = (lax.broadcasted_iota(jnp.int32, (many, 1), 0) // count * slots).astype(jnp.float32)
        seat = lax.broadcasted_iota(jnp.int32, (many, group * slots), 1).astype(jnp.float32)
        chosen = live & (seat == order + start)
        chosen = chosen.astype(jnp.float32)
        pick[...] = chosen.astype(jnp.bfloat16)
        pick_t[...] = chosen.T.astype(jnp.bfloat16)
        scale[...] = mine

        @pl.loop(0, width, step=tile)
        def _(column):
            part = pl.ds(pl.multiple_of(column, tile), tile)
            rows = rows_all[pl.ds(base, group), :, part].reshape(many, tile)
            picked[:, part] = jnp.dot(
                pick_t[...], rows, preferred_element_type=jnp.float32
            ).astype(jnp.bfloat16)

        gate_proj = jnp.dot(picked[...], gate_w[...], preferred_element_type=jnp.float32)
        up_proj = jnp.dot(picked[...], up_w[...], preferred_element_type=jnp.float32)
        act[...] = (gate_proj / (1.0 + jnp.exp(-gate_proj)) * up_proj).astype(jnp.bfloat16)

        @pl.loop(0, width, step=tile)
        def _(column):
            part = pl.ds(pl.multiple_of(column, tile), tile)
            produced = jnp.dot(act[...], down_w[:, part], preferred_element_type=jnp.float32)
            back = jnp.dot(pick[...], produced.astype(jnp.bfloat16), preferred_element_type=jnp.float32)
            sums = (back * scale[...]).astype(jnp.bfloat16)
            terms[pl.ds(base, group), :, part] = sums.reshape(group, count, tile)

    def copy_of(source, target, index, lane, chip, device):
        return pltpu.make_async_remote_copy(
            src_ref=source,
            dst_ref=target.at[index],
            send_sem=s_sends.at[lane, chip],
            recv_sem=s_recvs.at[lane, chip],
            device_id=device,
            device_id_type=MESH,
        )

    def to_partner(chip, block_core):
        return copy_of(terms.at[chip * 2 + block_core], near, chip, 0, chip, at.partner())

    def hop(kind, chip, level):
        held = terms.at[chip * 2 + core]
        if kind in (3, 4):
            return copy_of(held, third, chip, 1, chip, at.device(at.chip(z, 3)))
        return copy_of(held, second, level, 2, chip, at.device(at.chip(z, 2)))

    def rise(chip, level):
        return copy_of(terms.at[chip * 2 + core], flow, level, 3, chip, above())

    def fall(chip, level):
        ends = (level == z - 1).astype(jnp.int32)
        slot = level * (1 - ends) + levels * ends
        return copy_of(terms.at[chip * 2 + core], flow, slot, 4, chip, below())

    def fallen(chip):
        return copy_of(terms.at[chip * 2 + core], flow, levels, 4, chip, below())

    def add(chip, extra, last=False):
        @pl.loop(0, count, step=chunk)
        def _(row):
            part = pl.ds(pl.multiple_of(row, chunk), chunk)
            total = terms[chip * 2 + core, part, :].astype(jnp.float32)
            for ref, index in extra:
                total = total + ref[index, part, :].astype(jnp.float32)
            if last:
                out[part, :] = (residual[part, :] + total).astype(out.dtype)
            else:
                terms[chip * 2 + core, part, :] = total.astype(terms.dtype)

    def received(level, kind):
        chip = at.chip(level, kind)
        to_partner(chip, core).wait_recv()
        extra = [(near, chip)]
        if side == 2 and kind in (1, 2):
            hop(3, chip, level).wait_recv()
            extra.append((third, chip))
        if side == 2 and kind == 1:
            hop(2, chip, level).wait_recv()
            extra.append((second, level))
        return chip, extra

    def pass_on(level, kind):
        chip, extra = received(level, kind)
        add(chip, extra)
        hop(kind, chip, level).start()

    def first_along(level):
        @pl.when((z == 0) & (level > z))
        def _():
            chip, extra = received(level, 1)
            add(chip, extra)
            rise(chip, level).start()

        @pl.when((z == levels - 1) & (level < z))
        def _():
            chip, extra = received(level, 1)
            add(chip, extra)
            fall(chip, level).start()

    delay = 2 if side == 2 else 0

    @pl.loop(0, levels + delay)
    def _(step):
        visit(step, 1)
        if side == 2:
            visit(step - 1, 2)
            visit(step - 1, 3)
            visit(step - 2, 4)
        turn = step - delay

        @pl.when((turn >= 0) & (turn < levels))
        def _():
            level = level_of(turn)
            for kind in kinds:
                carry(at.chip(level, kind), 1 - core, 4, at.partner()).wait_recv()

            @pl.when(turn == 0)
            def _():
                for copy in fetch:
                    copy.wait()

            compute(level)
            for kind in kinds:
                to_partner(at.chip(level, kind), 1 - core).start()

    def last_along(level):
        first_along(level)

        @pl.when((z > 0) & (level > z))
        def _():
            chip, extra = received(level, 1)
            rise(chip, level).wait_recv()
            add(chip, extra + [(flow, level)])
            rise(chip, level).start()

        @pl.when((z < levels - 1) & (level < z))
        def _():
            chip, extra = received(level, 1)
            fall(chip, level).wait_recv()
            add(chip, extra + [(flow, level)])
            fall(chip, level).start()

    lag = 1 if side == 2 else 0

    @pl.loop(0, levels + 2 * lag)
    def _(step):
        if side == 2:

            @pl.when(step < levels)
            def _():
                level = level_of(levels - 1 - step)
                pass_on(level, 4)
                pass_on(level, 3)

            @pl.when((step >= lag) & (step < levels + lag))
            def _():
                pass_on(level_of(levels - 1 + lag - step), 2)

        @pl.when((step >= 2 * lag) & (step < levels + 2 * lag - 1))
        def _():
            last_along(level_of(levels - 1 + 2 * lag - step))

    chip, extra = received(z, 1)

    @pl.when(z > 0)
    def _():
        rise(chip, z).wait_recv()

    @pl.when(z < levels - 1)
    def _():
        fallen(chip).wait_recv()

    @pl.when((z > 0) & (z < levels - 1))
    def _():
        add(chip, extra + [(flow, z), (flow, levels)], last=True)

    @pl.when((z > 0) & (z == levels - 1))
    def _():
        add(chip, extra + [(flow, z)], last=True)

    @pl.when((z == 0) & (z < levels - 1))
    def _():
        add(chip, extra + [(flow, levels)], last=True)

    if levels == 1:
        add(chip, extra, last=True)

    @pl.loop(0, levels)
    def _(level):
        for kind in kinds:
            chip = at.chip(level, kind)
            carry(chip, core, 4, at.partner()).wait_send()
            if side == 2 and kind in (1, 2):
                carry(chip, core, 3, at.partner()).wait_send()
            to_partner(chip, 1 - core).wait_send()
            if kind != 1:
                hop(kind, chip, level).wait_send()
            else:
                if side == 2:
                    carry(chip, core, 2, at.partner()).wait_send()

                @pl.when((z < levels - 1) & (level <= z))
                def _():
                    carry(chip, core, 0, at.partner()).wait_send()

                @pl.when((z > 0) & (level >= z))
                def _():
                    carry(chip, core, 1, at.partner()).wait_send()

                @pl.when(level > z)
                def _():
                    rise(chip, level).wait_send()

                @pl.when(level < z)
                def _():
                    fall(chip, level).wait_send()


def run_layer(projected, hidden, gain, weights, w_gate, w_up, w_down, slots, side):
    wide_count = lax.axis_size("wide")
    blocks, chips = 2 * wide_count, side * side
    levels = wide_count // chips
    rows, width = hidden.shape
    block, half = (rows, width), jnp.bfloat16
    inner = w_gate.shape[2]
    seats, many = 2 * chips * slots, 2 * chips * rows
    lateral = wide_count if side == 2 else 1
    return pl.pallas_call(
        functools.partial(layer_kernel, side, wide_count, 16, slots),
        out_shape=jax.ShapeDtypeStruct(block, half),
        in_specs=[pl.BlockSpec(memory_space=pltpu.VMEM)] * 4
        + [pl.BlockSpec(memory_space=pl.ANY)] * 3,
        out_specs=pl.BlockSpec(memory_space=pltpu.VMEM),
        scratch_shapes=[
            pltpu.VMEM((blocks, rows, width + weights.shape[1]), half),
            pltpu.VMEM((blocks,) + block, half),
            pltpu.VMEM(block, jnp.float32),
            pltpu.VMEM(block, jnp.float32),
            pltpu.VMEM((width, inner), half),
            pltpu.VMEM((width, inner), half),
            pltpu.VMEM((inner, width), half),
            pltpu.VMEM((many, many), half),
            pltpu.VMEM((many, seats), half),
            pltpu.VMEM((seats, many), half),
            pltpu.VMEM((many, 1), jnp.float32),
            pltpu.VMEM((seats, width), half),
            pltpu.VMEM((seats, inner), half),
            pltpu.VMEM((wide_count,) + block, half),
            pltpu.VMEM((lateral,) + block, half),
            pltpu.VMEM((levels if side == 2 else 1,) + block, half),
            pltpu.VMEM((levels + 1,) + block, half),
            pltpu.SemaphoreType.DMA((2,)),
            pltpu.SemaphoreType.DMA((3,)),
            pltpu.SemaphoreType.DMA((wide_count, 5)),
            pltpu.SemaphoreType.DMA((blocks,)),
            pltpu.SemaphoreType.DMA((5, wide_count)),
            pltpu.SemaphoreType.DMA((5, wide_count)),
        ],
        compiler_params=pltpu.CompilerParams(
            collective_id=0, has_side_effects=True, vmem_limit_bytes=67043328
        ),
        name="run_layer",
    )(projected, hidden, gain, weights, w_gate, w_up, w_down)


class Grid:
    def __init__(self, levels):
        wide = lax.axis_index("wide")
        self.levels, self.core = levels, lax.axis_index("narrow")
        self.z, self.p = wide // 4, wide % 4
        y, x = self.p // 2, self.p % 2
        along_x, along_y = self.p + 1 - 2 * x, self.p + 2 - 4 * y
        c = self.core
        self.a = (1 - c) * along_x + c * along_y
        self.b = c * along_x + (1 - c) * along_y
        self.d = 3 - self.p
        self.has_up, self.has_down = self.z < levels - 1, self.z > 0

    def at(self, level, column):
        return {"wide": level * 4 + column, "narrow": self.core}

    def partner(self):
        return {"wide": self.z * 4 + self.p, "narrow": 1 - self.core}

    def up(self):
        return self.at(self.z + 1, self.p)

    def down(self):
        return self.at(self.z - 1, self.p)

    def greet(self):
        barrier = pltpu.get_barrier_semaphore()

        def hello(device):
            pl.semaphore_signal(barrier, inc=1, device_id=device, device_id_type=MESH)

        hello(self.partner())
        for column in (self.a, self.b, self.d):
            hello(self.at(self.z, column))
        for step in range(1, self.levels):
            hello(self.at(lax.rem(self.z + step, self.levels), self.p))

    def greeted(self):
        pl.semaphore_wait(pltpu.get_barrier_semaphore(), 3 + self.levels)

    def level_of(self, turn):
        low, high = self.z, self.levels - 1 - self.z
        less = (low < high).astype(jnp.int32)
        span = low * less + high * (1 - less)
        paired = (turn <= 2 * span).astype(jnp.int32)
        distance = paired * ((turn + 1) // 2) + (1 - paired) * (turn - span)
        sign = paired * (2 * (turn % 2) - 1) + (1 - paired) * (2 * less - 1)
        return self.z + sign * distance


def fast_kernel(
    levels, draft_len, cache_len, gain, ids, ratios, hidden_hbm, query_hbm, open_hbm, kv_hbm, keys_hbm, values_hbm,
    out_hbm, gate_hbm, up_hbm, down_hbm,
    out, rows_all, terms, near, from_b, from_a, from_b_q, from_a_q, flow_m, flow_q, tables, scale,
    hidden, query, opened, kv, keys, values, out_w, gate_w, up_w, down_w, attended, projected, theirs, residual, act,
    loads, meet, meet_in, t_sends, t_recvs, g_sends, g_recvs, s_sends, s_recvs,
):
    g = Grid(levels)
    z, p, core = g.z, g.p, g.core
    half = jnp.bfloat16
    count, width = hidden.shape
    quarter = count // 4
    main = count - quarter
    tail = 4 * main
    lot = 4 * count
    experts = 8 * levels
    expert = (z * 4 + p) * 2 + core
    tile = projected.shape[3]
    reqs, context_len, head_size = keys.shape
    drafts = query.shape[0] // reqs
    heads = query.shape[1] // head_size
    other = 1 - core

    pairs = (
        (query_hbm, query), (kv_hbm, kv), (keys_hbm, keys), (values_hbm, values), (open_hbm, opened),
        (out_hbm, out_w), (hidden_hbm, hidden), (gate_hbm.at[0], gate_w), (up_hbm.at[0], up_w), (down_hbm.at[0], down_w),
    )
    fetch = [pltpu.make_async_copy(source, target, loads.at[i]) for i, (source, target) in enumerate(pairs)]
    for copy in fetch:
        copy.start()

    g.greet()

    name = lax.broadcasted_iota(jnp.int32, (experts, count), 0)
    weight = jnp.zeros((experts, count), jnp.float32)
    for k in range(ids.shape[0]):
        weight = weight + jnp.where(ids[k : k + 1, :] == name, ratios[k : k + 1, :], 0.0)
    high = weight.astype(half).astype(jnp.float32)
    both = jnp.concatenate([high, weight - high] * 2, axis=0)
    both = jnp.concatenate([both, both], axis=1).T
    lane = lax.broadcasted_iota(jnp.int32, tables.shape[3:], 1)
    tables[z, core, p] = jnp.where(lane < 2 * experts, both[: count // 2], both[count // 2 : count]).astype(half)

    def send(source, target, send_sem, recv_sem, device):
        return pltpu.make_async_remote_copy(
            src_ref=source, dst_ref=target, send_sem=send_sem, recv_sem=recv_sem, device_id=device, device_id_type=MESH
        )

    def table_near(lane_id, column):
        block = tables.at[z, core, column]
        return send(block, block, t_sends.at[lane_id], t_recvs.at[lane_id], g.at(z, (g.a, g.b, g.d)[lane_id]))

    def table_far(step, level):
        block = tables.at[z, core]
        return send(block, block, t_sends.at[2 + step], t_recvs.at[3 + z], g.at(level, p))

    def table_far_in(level):
        block = tables.at[level, core]
        return send(block, block, t_sends.at[3], t_recvs.at[3 + level], g.at(z, p))

    def table_over(level, lane_core):
        block = tables.at[level, lane_core]
        return send(block, block, t_sends.at[2 + levels + level], t_recvs.at[3 + levels + level], g.partner())

    def attend(first, last):
        for r in range(first, last):
            mine = slice(r * drafts, (r + 1) * drafts)
            q = jnp.concatenate([query[mine, h * head_size : (h + 1) * head_size] for h in range(heads)], axis=0)
            contract = (((1,), (1,)), ((), ()))
            s = lax.dot_general(q, keys[r], contract, preferred_element_type=jnp.float32) * (1.0 / math.sqrt(head_size))
            sd = lax.dot_general(q, kv[0], contract, preferred_element_type=jnp.float32) * (1.0 / math.sqrt(head_size))
            slot = lax.broadcasted_iota(jnp.int32, s.shape, 1)
            column = lax.broadcasted_iota(jnp.int32, sd.shape, 1) - r * drafts
            row = lax.broadcasted_iota(jnp.int32, sd.shape, 0) % drafts
            s = jnp.where(slot < cache_len[r], s, -jnp.inf)
            sd = jnp.where((column >= 0) & (column <= row) & (column < draft_len[r]), sd, -jnp.inf)
            top = jnp.maximum(jnp.max(s, axis=1, keepdims=True), jnp.max(sd, axis=1, keepdims=True))
            probs, probs_d = jnp.exp(s - top), jnp.exp(sd - top)
            total = jnp.sum(probs, axis=1, keepdims=True) + jnp.sum(probs_d, axis=1, keepdims=True)
            context = jnp.dot(probs.astype(half), values[r], preferred_element_type=jnp.float32)
            context = context + jnp.dot(probs_d.astype(half), kv[1], preferred_element_type=jnp.float32)
            context = context / total
            live = lax.broadcasted_iota(jnp.int32, (drafts, head_size), 0) < draft_len[r]
            for h in range(heads):
                part = slice(h * head_size, (h + 1) * head_size)
                shut = 1.0 + jnp.exp(-opened[mine, part].astype(jnp.float32))
                value = context[h * drafts : (h + 1) * drafts] / shut
                attended[mine, part] = jnp.where(live, value, 0.0).astype(half)

    for i in range(5):
        fetch[i].wait()
    attend(0, reqs)
    fetch[5].wait()
    g.greeted()
    for i in range(3):
        table_near(i, p).start()

    def swap(i):
        return send(projected.at[i, other], theirs.at[i], meet.at[i], meet_in.at[i], g.partner())

    tiles = width // tile
    for i in range(tiles):
        product = jnp.dot(attended[...], out_w[:, i * tile : (i + 1) * tile], preferred_element_type=jnp.float32)
        projected[i] = product.reshape(2, count, tile)
        swap(i).start()
    fetch[6].wait()
    for i in range(tiles):
        swap(i).wait_recv()

    def m_rows(column):
        return pl.ds(pl.multiple_of(column * main, 16), main)

    def q_rows(column):
        return pl.ds(pl.multiple_of(tail + column * quarter, 16), quarter)

    q_all = pl.ds(tail, count)
    UP, DOWN, A, B, OVER = range(5)

    def target(way):
        return (g.up, g.down, lambda: g.at(z, g.a), lambda: g.at(z, g.b), g.partner)[way]()

    def carry(ref, way, level, slot, recv_slot):
        return send(ref, ref, g_sends.at[way, level, slot], g_recvs.at[level, recv_slot], target(way))

    def m_block(way, level, column, lane_core=core):
        return carry(rows_all.at[level, lane_core, m_rows(column)], way, level, column, column + 9 * (way == OVER))

    def q_block(way, level, column):
        return carry(rows_all.at[level, core, q_rows(column)], way, level, 4 + column, 4 + column)

    def q_level(way, level, lane_core=core):
        return carry(rows_all.at[level, lane_core, q_all], way, level, 8, 13 if way == OVER else 8)

    def along(level, copy):
        @pl.when(g.has_up & (level <= z))
        def _():
            copy(UP)

        @pl.when(g.has_down & (level >= z))
        def _():
            copy(DOWN)

    def norm(i):
        part = slice(i * 16, (i + 1) * 16)
        total = hidden[part, :].astype(jnp.float32) + jnp.concatenate(
            [projected[t, core, part, :] + theirs[t, part, :] for t in range(tiles)], axis=1
        )
        residual[part, :] = total
        spread = jnp.mean(total * total, axis=-1, keepdims=True)
        normed = (total * lax.rsqrt(spread + 1e-06) * gain[...]).astype(half)
        if i * 16 >= main:
            place = tail + p * quarter + i * 16 - main
        else:
            place = p * main + i * 16
        rows_all[z, core, pl.ds(pl.multiple_of(place, 16), 16), :] = normed

    for i in range(main // 16, count // 16):
        norm(i)
    q_block(A, z, p).start()
    q_block(B, z, p).start()
    for i in range(main // 16):
        norm(i)
    along(z, lambda way: m_block(way, z, p).start())
    for way in (A, B, OVER):
        m_block(way, z, p).start()

    for i, column in enumerate((g.a, g.b, g.d)):
        table_near(i, column).wait_recv()
    for step in range(1, levels):
        table_far(step, lax.rem(z + step, levels)).start()
    table_over(z, core).start()

    def m_first(turn):
        level = g.level_of(turn)
        m_block(A, level, p).wait_recv()
        along(level, lambda way: m_block(way, level, p).start())
        for way in (A, B, OVER):
            m_block(way, level, p).start()

    def compute(level, lane_core):
        for column in range(4):
            block = tables[level, lane_core, column].astype(jnp.float32)
            for part in range(2):
                first = 2 * part * experts + expert
                mine = jnp.where((lane == first) | (lane == first + experts), block, 0.0)
                mine = jnp.broadcast_to(jnp.sum(mine, axis=1, keepdims=True), block.shape)
                for i in range(count // 2 // 16):
                    row = part * (count // 2) + i * 16
                    place = column * main + row if row < main else tail + column * quarter + row - main
                    scale[place : place + 16, :] = mine[i * 16 : (i + 1) * 16]
        x = rows_all.at[level, lane_core]
        gate_proj = jnp.dot(x[...], gate_w[...], preferred_element_type=jnp.float32)
        up_proj = jnp.dot(x[...], up_w[...], preferred_element_type=jnp.float32)
        act[...] = (gate_proj / (1.0 + jnp.exp(-gate_proj)) * up_proj).astype(half)

        @pl.loop(0, width, step=512)
        def _(column):
            part = pl.ds(pl.multiple_of(column, 512), 512)
            produced = jnp.dot(act[...], down_w[:, part], preferred_element_type=jnp.float32)
            produced = produced.astype(half).astype(jnp.float32) * scale[:, 0:1]
            terms[level, lane_core, :, part] = produced.astype(half)

    def compute_other(level):
        for column in range(4):
            m_block(OVER, level, column, other).wait_recv()
        q_level(OVER, level, other).wait_recv()
        table_over(level, other).wait_recv()
        compute(level, other)
        term_over(level, other).start()

    def term(ref, target_ref, index, level, device):
        return send(ref, target_ref, s_sends.at[index, level], s_recvs.at[index, level], device)

    def term_over(level, lane_core):
        return term(terms.at[level, lane_core], near.at[level], 0, level, g.partner())

    def b_term(level, column, slot):
        return term(terms.at[level, core, m_rows(column)], from_b.at[level, slot], 1 + slot, level, g.at(z, g.b))

    def a_term(level, column):
        return term(terms.at[level, core, m_rows(column)], from_a.at[level], 3, level, g.at(z, g.a))

    def rise_m(level):
        return term(terms.at[level, core, m_rows(p)], flow_m.at[0, level], 4, level, g.up())

    def fall_m(level):
        return term(terms.at[level, core, m_rows(p)], flow_m.at[1, level], 5, level, g.down())

    def rise_q(level):
        return term(terms.at[level, core, q_all], flow_q.at[0, level], 6, level, g.up())

    def fall_q(level):
        return term(terms.at[level, core, q_all], flow_q.at[1, level], 7, level, g.down())

    def b_term_q(column, slot):
        return term(terms.at[z, core, q_rows(column)], from_b_q.at[slot], 8 + slot, z, g.at(z, g.b))

    def a_term_q(column):
        return term(terms.at[z, core, q_rows(column)], from_a_q, 10, z, g.at(z, g.a))

    q_block(A, z, g.a).wait_recv()
    q_block(B, z, g.a).start()
    q_block(B, z, g.b).wait_recv()
    m_first(1)
    for step in range(1, levels):
        table_far_in(lax.rem(z + step, levels)).wait_recv()
        table_over(lax.rem(z + step, levels), core).start()

    @pl.loop(0, levels)
    def _(turn):
        level = g.level_of(turn)
        m_block(A, level, g.a).wait_recv()
        m_block(B, level, g.a).start()
        m_block(OVER, level, g.a).start()
        m_block(B, level, g.b).wait_recv()
        m_block(OVER, level, g.b).start()

        @pl.when(turn == 1)
        def _():
            for copy in fetch[7:]:
                copy.wait()

        @pl.when(turn > 0)
        def _():
            compute_other(g.level_of(turn - 1))

        @pl.when(turn + 2 < levels)
        def _():
            m_first(turn + 2)

        @pl.when(turn == 0)
        def _():
            q_block(B, z, g.d).wait_recv()

        @pl.when(turn > 0)
        def _():
            q_level(UP, level).wait_recv()

        along(level, lambda way: q_level(way, level).start())
        q_level(OVER, level).start()
        m_block(B, level, g.d).wait_recv()
        m_block(OVER, level, g.d).start()

        @pl.when(turn > 0)
        def _():
            compute(g.level_of(turn - 1), core)

    def add(level, start, size, extra, last=None):
        @pl.loop(0, size, step=16)
        def _(row):
            row = pl.multiple_of(row, 16)
            part = pl.ds(pl.multiple_of(start + row, 16), 16)
            total = terms[level, core, part, :].astype(jnp.float32) + near[level, part, :].astype(jnp.float32)
            for ref in extra:
                total = total + ref[pl.ds(row, 16), :].astype(jnp.float32)
            if last is None:
                terms[level, core, part, :] = total.astype(half)
            else:
                rest = pl.ds(pl.multiple_of(last + row, 16), 16)
                out[rest, :] = (residual[rest, :] + total).astype(half)

    def add_flow(level, start, size, ref):
        @pl.loop(0, size, step=16)
        def _(row):
            row = pl.multiple_of(row, 16)
            part = pl.ds(pl.multiple_of(start + row, 16), 16)
            total = terms[level, core, part, :].astype(jnp.float32) + ref[pl.ds(row, 16), :].astype(jnp.float32)
            terms[level, core, part, :] = total.astype(half)

    def m_start(column):
        return column * main

    def q_start(column):
        return tail + column * quarter

    def stage_1(turn):
        level = g.level_of(turn)
        term_over(level, other).wait_recv()
        add(level, m_start(g.d), main, [])
        b_term(level, g.d, 1).start()
        add(level, m_start(g.b), main, [])
        b_term(level, g.b, 0).start()

    def stage_q(turn):
        level = g.level_of(turn)

        @pl.when((level < z) if turn else g.has_up)
        def _():
            @pl.when(g.has_up)
            def _():
                fall_q(level).wait_recv()
                add_flow(level, tail, count, flow_q.at[1, level])

        @pl.when((level > z) if turn else g.has_down)
        def _():
            @pl.when(g.has_down)
            def _():
                rise_q(level).wait_recv()
                add_flow(level, tail, count, flow_q.at[0, level])

        if turn > 0:
            add(level, tail, count, [])

            @pl.when(level > z)
            def _():
                rise_q(level).start()

            @pl.when(level < z)
            def _():
                fall_q(level).start()

        if turn == 0:
            add(level, q_start(g.d), quarter, [])
            b_term_q(g.d, 1).start()
            add(level, q_start(g.b), quarter, [])
            b_term_q(g.b, 0).start()

    def stage_2(turn):
        level = g.level_of(turn)
        b_term(level, g.d, 1).wait_recv()
        add(level, m_start(g.a), main, [from_b.at[level, 1]])
        a_term(level, g.a).start()

    def stage_2q():
        b_term_q(g.d, 1).wait_recv()
        add(z, q_start(g.a), quarter, [from_b_q.at[1]])
        a_term_q(g.a).start()

    def stage_3(turn):
        level = g.level_of(turn)

        @pl.when((level < z) if turn else g.has_up)
        def _():
            @pl.when(g.has_up)
            def _():
                fall_m(level).wait_recv()
                add_flow(level, m_start(p), main, flow_m.at[1, level])

        @pl.when((level > z) if turn else g.has_down)
        def _():
            @pl.when(g.has_down)
            def _():
                rise_m(level).wait_recv()
                add_flow(level, m_start(p), main, flow_m.at[0, level])

        b_term(level, g.b, 0).wait_recv()
        a_term(level, g.a).wait_recv()

        if turn > 0:
            add(level, m_start(p), main, [from_b.at[level, 0], from_a.at[level]])

            @pl.when(level > z)
            def _():
                rise_m(level).start()

            @pl.when(level < z)
            def _():
                fall_m(level).start()

        if turn == 0:
            add(level, m_start(p), main, [from_b.at[level, 0], from_a.at[level]], last=0)
            b_term_q(g.b, 0).wait_recv()
            a_term_q(g.a).wait_recv()
            add(level, q_start(p), quarter, [from_b_q.at[0], from_a_q], last=main)

    last = levels - 1
    at_end = (z == 0) | (z == last)

    def ends(stage, turn):
        pl.when(at_end)(lambda: stage(turn))

    def middle(stage, turn):
        pl.when(jnp.logical_not(at_end))(lambda: stage(turn))

    compute_other(g.level_of(last))
    stage_1(last - 1)
    compute(g.level_of(last), core)
    stage_1(last)
    ends(stage_q, last)
    stage_2(last - 1)
    stage_1(last - 2)
    ends(stage_q, last - 1)
    stage_2(last)
    middle(stage_q, last)
    stage_1(0)
    ends(stage_q, last - 2)
    stage_2(last - 2)
    ends(stage_3, last)
    middle(stage_q, last - 1)
    middle(stage_q, last - 2)
    stage_2(0)
    middle(stage_3, last)
    stage_3(last - 1)
    stage_q(0)
    stage_3(last - 2)
    stage_2q()
    stage_3(0)

    for i in range(3):
        table_near(i, p).wait_send()
    for step in range(1, levels):
        table_far(step, lax.rem(z + step, levels)).wait_send()
    for i in range(tiles):
        swap(i).wait_send()
    q_block(A, z, p).wait_send()
    q_block(B, z, p).wait_send()
    q_block(B, z, g.a).wait_send()
    b_term_q(g.d, 1).wait_send()
    b_term_q(g.b, 0).wait_send()
    a_term_q(g.a).wait_send()

    @pl.loop(0, levels)
    def _(level):
        table_over(level, core).wait_send()
        along(level, lambda way: m_block(way, level, p).wait_send())
        along(level, lambda way: q_level(way, level).wait_send())
        for way in (A, B, OVER):
            m_block(way, level, p).wait_send()
        for way in (B, OVER):
            m_block(way, level, g.a).wait_send()
        m_block(OVER, level, g.b).wait_send()
        m_block(OVER, level, g.d).wait_send()
        q_level(OVER, level).wait_send()
        term_over(level, other).wait_send()
        b_term(level, g.d, 1).wait_send()
        b_term(level, g.b, 0).wait_send()
        a_term(level, g.a).wait_send()

        @pl.when(level > z)
        def _():
            rise_m(level).wait_send()
            rise_q(level).wait_send()

        @pl.when(level < z)
        def _():
            fall_m(level).wait_send()
            fall_q(level).wait_send()


def run_fast(
    hidden, queries, out_gate, draft_kv, cache_keys, cache_values, draft_len, cache_len, o_weight, norm_gain,
    route_ids, route_weights, w_gate, w_up, w_down,
):
    levels = lax.axis_size("wide") // 4
    count, width = hidden.shape
    quarter = count // 4
    main, lot = count - quarter, 4 * count
    inner = w_gate.shape[2]
    half = jnp.bfloat16
    tile = 512
    lanes = max(128, 32 * levels)
    dma = pltpu.SemaphoreType.DMA
    vmem, smem, hbm = (pl.BlockSpec(memory_space=space) for space in (pltpu.VMEM, pltpu.SMEM, pl.ANY))
    return pl.pallas_call(
        functools.partial(fast_kernel, levels),
        out_shape=jax.ShapeDtypeStruct((count, width), half),
        in_specs=[smem] * 2 + [vmem] * 3 + [hbm] * 10,
        out_specs=vmem,
        scratch_shapes=[
            pltpu.VMEM((levels, 2, lot, width), half),
            pltpu.VMEM((levels, 2, lot, width), half),
            pltpu.VMEM((levels, lot, width), half),
            pltpu.VMEM((levels, 2, main, width), half),
            pltpu.VMEM((levels, main, width), half),
            pltpu.VMEM((2, quarter, width), half),
            pltpu.VMEM((quarter, width), half),
            pltpu.VMEM((2, levels, main, width), half),
            pltpu.VMEM((2, levels, count, width), half),
            pltpu.VMEM((levels, 2, 4, count // 2, lanes), half),
            pltpu.VMEM((lot, lanes), jnp.float32),
            pltpu.VMEM(hidden.shape, half),
            pltpu.VMEM(queries.shape, half),
            pltpu.VMEM(out_gate.shape, half),
            pltpu.VMEM(draft_kv.shape, half),
            pltpu.VMEM(cache_keys.shape, half),
            pltpu.VMEM(cache_values.shape, half),
            pltpu.VMEM(o_weight.shape, half),
            pltpu.VMEM((width, inner), half),
            pltpu.VMEM((width, inner), half),
            pltpu.VMEM((inner, width), half),
            pltpu.VMEM(queries.shape, half),
            pltpu.VMEM((width // tile, 2, count, tile), jnp.float32),
            pltpu.VMEM((width // tile, count, tile), jnp.float32),
            pltpu.VMEM((count, width), jnp.float32),
            pltpu.VMEM((lot, inner), half),
            dma((10,)),
            dma((width // tile,)),
            dma((width // tile,)),
            dma((2 + 2 * levels,)),
            dma((3 + 2 * levels,)),
            dma((5, levels, 9)),
            dma((levels, 14)),
            dma((11, levels)),
            dma((11, levels)),
        ],
        compiler_params=pltpu.CompilerParams(
            collective_id=0, has_side_effects=True, vmem_limit_bytes=67043328
        ),
        name="run_layer",
    )(
        draft_len, cache_len, norm_gain[None, :], route_ids.T, route_weights.T, hidden, queries, out_gate, draft_kv,
        cache_keys, cache_values, o_weight, w_gate, w_up, w_down,
    )


def fits_fast(hidden_in, queries, cache_keys):
    levels = lax.axis_size("wide") // 4
    drafts = queries.shape[0] // cache_keys.shape[0]
    return (
        plane_of(lax.axis_size("rep"), lax.axis_size("wide")) == 2
        and hidden_in.shape[0] * 2 == 128
        and hidden_in.shape[1] % 512 == 0
        and drafts % 16 == 0
        and cache_keys.shape[0] % 2 == 0
        and levels * 32 == 128
    )


def on_device(
    hidden_in,
    queries,
    out_gate,
    draft_kv,
    cache_keys,
    cache_values,
    draft_len,
    cache_len,
    o_weight,
    norm_gain,
    route_ids,
    route_weights,
    w_gate,
    w_up,
    w_down,
):
    if fits_fast(hidden_in, queries, cache_keys):
        return run_fast(
            hidden_in, queries, out_gate, draft_kv, cache_keys, cache_values, draft_len, cache_len, o_weight,
            norm_gain, route_ids, route_weights, w_gate, w_up, w_down,
        )
    attended = attention_rows(
        queries, out_gate, draft_kv, cache_keys, cache_values, draft_len, cache_len
    )
    own_rows = hidden_in.shape[0]
    width = hidden_in.shape[1]
    projected = jnp.dot(attended, o_weight, preferred_element_type=jnp.float32)
    projected = projected.reshape(2, own_rows, width)
    top_count = route_ids.shape[1]
    experts = lax.axis_size("wide") * lax.axis_size("narrow")
    capacity = max(2, min(own_rows, (3 * own_rows * top_count + 2 * experts - 1) // (2 * experts)))
    slots = -(-capacity // 16) * 16
    chosen = route_ids[:, :, None] == jnp.arange(experts, dtype=jnp.int32)[None, None, :]
    dense = jnp.sum(jnp.where(chosen, route_weights[:, :, None], 0.0), axis=1)
    coarse = lax.reduce_precision(dense, 8, 7)
    weights = jnp.concatenate([coarse, dense - coarse], axis=1).astype(jnp.bfloat16)
    weights = jnp.pad(weights, ((0, 0), (0, -weights.shape[1] % 128)))
    side = plane_of(lax.axis_size("rep"), lax.axis_size("wide"))
    return run_layer(
        projected, hidden_in, norm_gain[None, :], weights, w_gate, w_up, w_down, slots, side
    )


def solution(mesh):
    placed = (
        P(("rep", "wide", "narrow"), None),
        P(("rep", "wide"), "narrow"),
        P(("rep", "wide"), "narrow"),
        P(None, ("rep", "wide"), None),
        P(("rep", "wide"), None, None),
        P(("rep", "wide"), None, None),
        P(("rep", "wide")),
        P(("rep", "wide")),
        P("narrow", None),
        P(),
        P(("rep", "wide", "narrow"), None),
        P(("rep", "wide", "narrow"), None),
        P(("wide", "narrow"), None, None),
        P(("wide", "narrow"), None, None),
        P(("wide", "narrow"), None, None),
    )
    return jax.shard_map(
        on_device,
        mesh=mesh,
        in_specs=placed,
        out_specs=P(("rep", "wide", "narrow"), None),
        check_vma=False,
    )
```

```python
import math

import functools

import jax
import jax.numpy as jnp
from jax import lax
from jax.experimental import pallas as pl
from jax.experimental.pallas import tpu as pltpu
from jax.sharding import PartitionSpec as P

MESH = pl.DeviceIdType.MESH


def attention_rows(queries, out_gate, draft_kv, cache_keys, cache_values, draft_len, cache_len):
    req_count, context_len, head_size = cache_keys.shape
    row_count = queries.shape[0]
    drafts = row_count // req_count
    head_count = queries.shape[1] // head_size
    query_blocks = queries.reshape(req_count, drafts, head_count, head_size)
    draft_keys = draft_kv[0].reshape(req_count, drafts, head_size)
    draft_values = draft_kv[1].reshape(req_count, drafts, head_size)
    score_scale = 1.0 / math.sqrt(head_size)
    cache_scores = (
        jnp.einsum("rjhd,rcd->rjhc", query_blocks, cache_keys, preferred_element_type=jnp.float32)
        * score_scale
    )
    draft_scores = (
        jnp.einsum("rjhd,rid->rjhi", query_blocks, draft_keys, preferred_element_type=jnp.float32)
        * score_scale
    )
    slots = jnp.arange(context_len, dtype=jnp.int32)
    cache_live = slots[None, :] < cache_len[:, None]
    cache_scores = jnp.where(cache_live[:, None, None, :], cache_scores, -jnp.inf)
    positions = jnp.arange(drafts, dtype=jnp.int32)
    causal = positions[None, :] <= positions[:, None]
    draft_live = causal[None, :, :] & (positions[None, None, :] < draft_len[:, None, None])
    draft_scores = jnp.where(draft_live[:, :, None, :], draft_scores, -jnp.inf)
    row_max = jnp.maximum(jnp.max(cache_scores, axis=-1), jnp.max(draft_scores, axis=-1))
    cache_probs = jnp.exp(cache_scores - row_max[..., None])
    draft_probs = jnp.exp(draft_scores - row_max[..., None])
    denominator = jnp.sum(cache_probs, axis=-1) + jnp.sum(draft_probs, axis=-1)
    context = jnp.einsum(
        "rjhc,rcd->rjhd",
        cache_probs.astype(jnp.bfloat16),
        cache_values,
        preferred_element_type=jnp.float32,
    )
    context = context + jnp.einsum(
        "rjhi,rid->rjhd",
        draft_probs.astype(jnp.bfloat16),
        draft_values,
        preferred_element_type=jnp.float32,
    )
    context = context / denominator[..., None]
    gate_open = jax.nn.sigmoid(out_gate.astype(jnp.float32)).reshape(
        req_count, drafts, head_count, head_size
    )
    row_live = (positions[None, :] < draft_len[:, None]).astype(jnp.float32)
    attended = context * gate_open * row_live[:, :, None, None]
    return attended.reshape(row_count, head_count * head_size).astype(jnp.bfloat16)


def plane_of(rep_count, wide_count):
    return 2 if rep_count == 1 and wide_count % 4 == 0 else 1


class Place:
    def __init__(self, side, wide_count):
        self.side, self.levels = side, wide_count // (side * side)
        wide = lax.axis_index("wide")
        self.core = lax.axis_index("narrow")
        self.z = wide // (side * side)
        self.y = (wide // side) % side
        self.x = wide % side
        c = self.core
        if side == 2:
            flip_y, flip_x = 1 - 2 * self.y, 1 - 2 * self.x
            self.y2, self.x2 = self.y + c * flip_y, self.x + (1 - c) * flip_x
            self.y3, self.x3 = self.y + (1 - c) * flip_y, self.x + c * flip_x
            self.y4, self.x4 = self.y + flip_y, self.x + flip_x

    def chip(self, z, kind):
        y, x = {
            1: (self.y, self.x),
            2: (getattr(self, "y2", 0), getattr(self, "x2", 0)),
            3: (getattr(self, "y3", 0), getattr(self, "x3", 0)),
            4: (getattr(self, "y4", 0), getattr(self, "x4", 0)),
        }[kind]
        return (z * self.side + y) * self.side + x

    def device(self, chip):
        return {"wide": chip, "narrow": self.core}

    def partner(self):
        return {"wide": self.chip(self.z, 1), "narrow": 1 - self.core}

    def greet(self):
        barrier = pltpu.get_barrier_semaphore()
        pl.semaphore_signal(barrier, inc=1, device_id=self.partner(), device_id_type=MESH)
        count = 1
        if self.side == 2:
            for kind in (2, 3):
                pl.semaphore_signal(
                    barrier,
                    inc=1,
                    device_id=self.device(self.chip(self.z, kind)),
                    device_id_type=MESH,
                )
            count = 3
        has_up, has_down = self.z < self.levels - 1, self.z > 0

        @pl.when(has_up)
        def _():
            pl.semaphore_signal(
                barrier, inc=1, device_id=self.device(self.chip(self.z + 1, 1)), device_id_type=MESH
            )

        @pl.when(has_down)
        def _():
            pl.semaphore_signal(
                barrier, inc=1, device_id=self.device(self.chip(self.z - 1, 1)), device_id_type=MESH
            )

        ends = has_up.astype(jnp.int32) + has_down.astype(jnp.int32)
        pl.semaphore_wait(barrier, count + ends)


def norm_rows(at, chunk, projected, hidden, gain, residual, rows_ref, theirs, meet):
    count = hidden.shape[0]
    swap = pltpu.make_async_remote_copy(
        src_ref=projected.at[1 - at.core],
        dst_ref=theirs,
        send_sem=meet.at[0],
        recv_sem=meet.at[1],
        device_id=at.partner(),
        device_id_type=MESH,
    )
    swap.start()
    swap.wait()

    @pl.loop(0, count, step=chunk)
    def _(row):
        part = pl.ds(pl.multiple_of(row, chunk), chunk)
        total = hidden[part, :].astype(jnp.float32) + (projected[at.core, part, :] + theirs[part, :])
        residual[part, :] = total
        spread = jnp.mean(total * total, axis=-1, keepdims=True)
        rows_ref[part, : total.shape[1]] = (total * lax.rsqrt(spread + 1e-06) * gain[...]).astype(rows_ref.dtype)


def layer_kernel(
    side, wide_count, chunk, slots, projected, hidden, gain, weights, gate_hbm, up_hbm, down_hbm,
    out, rows_all, terms, residual, theirs, gate_w, up_w, down_w, triangle, pick, pick_t, scale, picked, act,
    near, third, second, flow, meet, loads, g_sends, g_recvs, s_sends, s_recvs,
):
    at = Place(side, wide_count)
    z, levels, core = at.z, at.levels, at.core
    count, width = hidden.shape
    chips = side * side
    kinds = (4, 3, 2, 1) if side == 2 else (1,)
    group = 2 * chips
    experts = 2 * wide_count
    expert = at.chip(z, 1) * 2 + core
    fetch = [
        pltpu.make_async_copy(source.at[0], target, loads.at[i])
        for i, (source, target) in enumerate(((gate_hbm, gate_w), (up_hbm, up_w), (down_hbm, down_w)))
    ]
    for copy in fetch:
        copy.start()
    at.greet()
    own = rows_all.at[expert]
    norm_rows(at, chunk, projected, hidden, gain, residual, own, theirs, meet)
    own[:, width:] = weights[...]

    def carry(chip, block_core, lane, target):
        block = rows_all.at[chip * 2 + block_core]
        return pltpu.make_async_remote_copy(
            src_ref=block,
            dst_ref=block,
            send_sem=g_sends.at[chip, lane],
            recv_sem=g_recvs.at[chip * 2 + block_core],
            device_id=target,
            device_id_type=MESH,
        )

    def above():
        return at.device(at.chip(z + 1, 1))

    def below():
        return at.device(at.chip(z - 1, 1))

    def visit(distance, kind):
        for sign in (1, -1):
            level = z + sign * distance
            present = (distance >= 0) & (level >= 0) & (level < levels)
            if sign < 0:
                present = present & (distance > 0)

            @pl.when(present)
            def _():
                chip = at.chip(level, kind)
                if kind == 1:

                    @pl.when(distance > 0)
                    def _():
                        carry(chip, core, 4, at.partner()).wait_recv()

                    go_up = z < levels - 1
                    go_down = z > 0
                    if sign > 0:
                        go_up = go_up & (distance == 0)
                    else:
                        go_down = go_down & (distance == 0)

                    @pl.when(go_up)
                    def _():
                        carry(chip, core, 0, above()).start()

                    @pl.when(go_down)
                    def _():
                        carry(chip, core, 1, below()).start()

                    if side == 2:
                        carry(chip, core, 2, at.device(at.chip(z, 2))).start()
                else:
                    carry(chip, core, 4, at.partner()).wait_recv()
                if side == 2 and kind in (1, 2):
                    carry(chip, core, 3, at.device(at.chip(z, 3))).start()
                carry(chip, core, 4, at.partner()).start()

    def level_of(turn):
        low, high = z, levels - 1 - z
        less = (low < high).astype(jnp.int32)
        span = low * less + high * (1 - less)
        paired = (turn <= 2 * span).astype(jnp.int32)
        distance = paired * ((turn + 1) // 2) + (1 - paired) * (turn - span)
        sign = paired * (2 * (turn % 2) - 1) + (1 - paired) * (2 * less - 1)
        return z + sign * distance

    many = group * count
    tile = 512

    row = lax.broadcasted_iota(jnp.int32, (many, many), 0)
    other = lax.broadcasted_iota(jnp.int32, (many, many), 1)
    triangle[...] = ((other < row) & (other // count == row // count)).astype(jnp.float32).astype(jnp.bfloat16)

    def compute(level):
        base = level * group
        table = rows_all[pl.ds(base, group), :, width:].reshape(many, weights.shape[1])
        lane = lax.broadcasted_iota(jnp.int32, table.shape, 1)
        mine = jnp.where((lane == expert) | (lane == experts + expert), table.astype(jnp.float32), 0.0)
        mine = jnp.sum(mine, axis=1, keepdims=True)
        live = mine > 0.0
        flags = jnp.broadcast_to(live.astype(jnp.float32), (many, 128)).astype(jnp.bfloat16)
        order = jnp.dot(triangle[...], flags, preferred_element_type=jnp.float32)[:, :1]
        start = (lax.broadcasted_iota(jnp.int32, (many, 1), 0) // count * slots).astype(jnp.float32)
        seat = lax.broadcasted_iota(jnp.int32, (many, group * slots), 1).astype(jnp.float32)
        chosen = live & (seat == order + start)
        chosen = chosen.astype(jnp.float32)
        pick[...] = chosen.astype(jnp.bfloat16)
        pick_t[...] = chosen.T.astype(jnp.bfloat16)
        scale[...] = mine

        @pl.loop(0, width, step=tile)
        def _(column):
            part = pl.ds(pl.multiple_of(column, tile), tile)
            rows = rows_all[pl.ds(base, group), :, part].reshape(many, tile)
            picked[:, part] = jnp.dot(
                pick_t[...], rows, preferred_element_type=jnp.float32
            ).astype(jnp.bfloat16)

        gate_proj = jnp.dot(picked[...], gate_w[...], preferred_element_type=jnp.float32)
        up_proj = jnp.dot(picked[...], up_w[...], preferred_element_type=jnp.float32)
        act[...] = (gate_proj / (1.0 + jnp.exp(-gate_proj)) * up_proj).astype(jnp.bfloat16)

        @pl.loop(0, width, step=tile)
        def _(column):
            part = pl.ds(pl.multiple_of(column, tile), tile)
            produced = jnp.dot(act[...], down_w[:, part], preferred_element_type=jnp.float32)
            back = jnp.dot(pick[...], produced.astype(jnp.bfloat16), preferred_element_type=jnp.float32)
            sums = (back * scale[...]).astype(jnp.bfloat16)
            terms[pl.ds(base, group), :, part] = sums.reshape(group, count, tile)

    def copy_of(source, target, index, lane, chip, device):
        return pltpu.make_async_remote_copy(
            src_ref=source,
            dst_ref=target.at[index],
            send_sem=s_sends.at[lane, chip],
            recv_sem=s_recvs.at[lane, chip],
            device_id=device,
            device_id_type=MESH,
        )

    def to_partner(chip, block_core):
        return copy_of(terms.at[chip * 2 + block_core], near, chip, 0, chip, at.partner())

    def hop(kind, chip, level):
        held = terms.at[chip * 2 + core]
        if kind in (3, 4):
            return copy_of(held, third, chip, 1, chip, at.device(at.chip(z, 3)))
        return copy_of(held, second, level, 2, chip, at.device(at.chip(z, 2)))

    def rise(chip, level):
        return copy_of(terms.at[chip * 2 + core], flow, level, 3, chip, above())

    def fall(chip, level):
        ends = (level == z - 1).astype(jnp.int32)
        slot = level * (1 - ends) + levels * ends
        return copy_of(terms.at[chip * 2 + core], flow, slot, 4, chip, below())

    def fallen(chip):
        return copy_of(terms.at[chip * 2 + core], flow, levels, 4, chip, below())

    def add(chip, extra, last=False):
        @pl.loop(0, count, step=chunk)
        def _(row):
            part = pl.ds(pl.multiple_of(row, chunk), chunk)
            total = terms[chip * 2 + core, part, :].astype(jnp.float32)
            for ref, index in extra:
                total = total + ref[index, part, :].astype(jnp.float32)
            if last:
                out[part, :] = (residual[part, :] + total).astype(out.dtype)
            else:
                terms[chip * 2 + core, part, :] = total.astype(terms.dtype)

    def received(level, kind):
        chip = at.chip(level, kind)
        to_partner(chip, core).wait_recv()
        extra = [(near, chip)]
        if side == 2 and kind in (1, 2):
            hop(3, chip, level).wait_recv()
            extra.append((third, chip))
        if side == 2 and kind == 1:
            hop(2, chip, level).wait_recv()
            extra.append((second, level))
        return chip, extra

    def pass_on(level, kind):
        chip, extra = received(level, kind)
        add(chip, extra)
        hop(kind, chip, level).start()

    def first_along(level):
        @pl.when((z == 0) & (level > z))
        def _():
            chip, extra = received(level, 1)
            add(chip, extra)
            rise(chip, level).start()

        @pl.when((z == levels - 1) & (level < z))
        def _():
            chip, extra = received(level, 1)
            add(chip, extra)
            fall(chip, level).start()

    delay = 2 if side == 2 else 0

    @pl.loop(0, levels + delay)
    def _(step):
        visit(step, 1)
        if side == 2:
            visit(step - 1, 2)
            visit(step - 1, 3)
            visit(step - 2, 4)
        turn = step - delay

        @pl.when((turn >= 0) & (turn < levels))
        def _():
            level = level_of(turn)
            for kind in kinds:
                carry(at.chip(level, kind), 1 - core, 4, at.partner()).wait_recv()

            @pl.when(turn == 0)
            def _():
                for copy in fetch:
                    copy.wait()

            compute(level)
            for kind in kinds:
                to_partner(at.chip(level, kind), 1 - core).start()

    def last_along(level):
        first_along(level)

        @pl.when((z > 0) & (level > z))
        def _():
            chip, extra = received(level, 1)
            rise(chip, level).wait_recv()
            add(chip, extra + [(flow, level)])
            rise(chip, level).start()

        @pl.when((z < levels - 1) & (level < z))
        def _():
            chip, extra = received(level, 1)
            fall(chip, level).wait_recv()
            add(chip, extra + [(flow, level)])
            fall(chip, level).start()

    lag = 1 if side == 2 else 0

    @pl.loop(0, levels + 2 * lag)
    def _(step):
        if side == 2:

            @pl.when(step < levels)
            def _():
                level = level_of(levels - 1 - step)
                pass_on(level, 4)
                pass_on(level, 3)

            @pl.when((step >= lag) & (step < levels + lag))
            def _():
                pass_on(level_of(levels - 1 + lag - step), 2)

        @pl.when((step >= 2 * lag) & (step < levels + 2 * lag - 1))
        def _():
            last_along(level_of(levels - 1 + 2 * lag - step))

    chip, extra = received(z, 1)

    @pl.when(z > 0)
    def _():
        rise(chip, z).wait_recv()

    @pl.when(z < levels - 1)
    def _():
        fallen(chip).wait_recv()

    @pl.when((z > 0) & (z < levels - 1))
    def _():
        add(chip, extra + [(flow, z), (flow, levels)], last=True)

    @pl.when((z > 0) & (z == levels - 1))
    def _():
        add(chip, extra + [(flow, z)], last=True)

    @pl.when((z == 0) & (z < levels - 1))
    def _():
        add(chip, extra + [(flow, levels)], last=True)

    if levels == 1:
        add(chip, extra, last=True)

    @pl.loop(0, levels)
    def _(level):
        for kind in kinds:
            chip = at.chip(level, kind)
            carry(chip, core, 4, at.partner()).wait_send()
            if side == 2 and kind in (1, 2):
                carry(chip, core, 3, at.partner()).wait_send()
            to_partner(chip, 1 - core).wait_send()
            if kind != 1:
                hop(kind, chip, level).wait_send()
            else:
                if side == 2:
                    carry(chip, core, 2, at.partner()).wait_send()

                @pl.when((z < levels - 1) & (level <= z))
                def _():
                    carry(chip, core, 0, at.partner()).wait_send()

                @pl.when((z > 0) & (level >= z))
                def _():
                    carry(chip, core, 1, at.partner()).wait_send()

                @pl.when(level > z)
                def _():
                    rise(chip, level).wait_send()

                @pl.when(level < z)
                def _():
                    fall(chip, level).wait_send()


def run_layer(projected, hidden, gain, weights, w_gate, w_up, w_down, slots, side):
    wide_count = lax.axis_size("wide")
    blocks, chips = 2 * wide_count, side * side
    levels = wide_count // chips
    rows, width = hidden.shape
    block, half = (rows, width), jnp.bfloat16
    inner = w_gate.shape[2]
    seats, many = 2 * chips * slots, 2 * chips * rows
    lateral = wide_count if side == 2 else 1
    return pl.pallas_call(
        functools.partial(layer_kernel, side, wide_count, 16, slots),
        out_shape=jax.ShapeDtypeStruct(block, half),
        in_specs=[pl.BlockSpec(memory_space=pltpu.VMEM)] * 4
        + [pl.BlockSpec(memory_space=pl.ANY)] * 3,
        out_specs=pl.BlockSpec(memory_space=pltpu.VMEM),
        scratch_shapes=[
            pltpu.VMEM((blocks, rows, width + weights.shape[1]), half),
            pltpu.VMEM((blocks,) + block, half),
            pltpu.VMEM(block, jnp.float32),
            pltpu.VMEM(block, jnp.float32),
            pltpu.VMEM((width, inner), half),
            pltpu.VMEM((width, inner), half),
            pltpu.VMEM((inner, width), half),
            pltpu.VMEM((many, many), half),
            pltpu.VMEM((many, seats), half),
            pltpu.VMEM((seats, many), half),
            pltpu.VMEM((many, 1), jnp.float32),
            pltpu.VMEM((seats, width), half),
            pltpu.VMEM((seats, inner), half),
            pltpu.VMEM((wide_count,) + block, half),
            pltpu.VMEM((lateral,) + block, half),
            pltpu.VMEM((levels if side == 2 else 1,) + block, half),
            pltpu.VMEM((levels + 1,) + block, half),
            pltpu.SemaphoreType.DMA((2,)),
            pltpu.SemaphoreType.DMA((3,)),
            pltpu.SemaphoreType.DMA((wide_count, 5)),
            pltpu.SemaphoreType.DMA((blocks,)),
            pltpu.SemaphoreType.DMA((5, wide_count)),
            pltpu.SemaphoreType.DMA((5, wide_count)),
        ],
        compiler_params=pltpu.CompilerParams(
            collective_id=0, has_side_effects=True, vmem_limit_bytes=67043328
        ),
        name="run_layer",
    )(projected, hidden, gain, weights, w_gate, w_up, w_down)


END_PLAN = (
    ("t", 0), ("q2", 0), ("m1", 1), ("qh", 0), ("m3", 0), ("m2", 0), ("m1", 2), ("m4", 0), ("m2", 1), ("co", 0),
    ("t", 1), ("m2", 2), ("q", 1), ("cw", 0), ("m1", 3), ("m3", 1), ("m4", 1), ("co", 1), ("m3", 2), ("m4", 2),
    ("cw", 1), ("q", 2), ("m2", 3), ("t", 2), ("nw", 1), ("m3", 3), ("sq", 1), ("s1", 1), ("co", 2), ("cw", 2),
    ("m4", 3), ("t", 3), ("q", 3), ("nw", 2), ("sq", 2), ("s1", 2), ("co", 3), ("s2", 1), ("cw", 3), ("nw", 3),
    ("sq", 3), ("s1", 3), ("nw", 0), ("s2", 3), ("s2", 2), ("s3", 3), ("s1", 0), ("s3", 2), ("s2", 0), ("s3", 1),
    ("sq", 0), ("s2q", 0), ("s3", 0), ("s3q", 0),
)
MIDDLE_PLAN = (
    ("q2", 0), ("t", 0), ("m1", 1), ("t", 2), ("m2", 0), ("m1", 2), ("qh", 0), ("m3", 0), ("m1", 3), ("m2", 1),
    ("q", 2), ("m3", 1), ("q", 1), ("m2", 2), ("m4", 0), ("m2", 3), ("co", 0), ("t", 3), ("t", 1), ("cw", 0),
    ("m4", 1), ("nw", 0), ("q", 3), ("m4", 2), ("s1", 0), ("co", 1), ("cw", 1), ("m3", 2), ("m4", 3), ("m3", 3),
    ("s2", 0), ("co", 3), ("nw", 1), ("s1", 1), ("cw", 3), ("co", 2), ("sq", 1), ("nw", 2), ("nw", 3), ("s1", 3),
    ("sq", 3), ("s2", 3), ("cw", 2), ("sq", 0), ("s1", 2), ("s2q", 0), ("sq", 2), ("s3", 3), ("s2", 2), ("s2", 1),
    ("s3", 2), ("s3", 1), ("s3q", 0), ("s3", 0),
)


class Grid:
    def __init__(self, levels):
        wide = lax.axis_index("wide")
        self.levels, self.core = levels, lax.axis_index("narrow")
        self.z, self.p = wide // 4, wide % 4
        y, x = self.p // 2, self.p % 2
        along_x, along_y = self.p + 1 - 2 * x, self.p + 2 - 4 * y
        c = self.core
        self.a = (1 - c) * along_x + c * along_y
        self.b = c * along_x + (1 - c) * along_y
        self.d = 3 - self.p
        self.has_up, self.has_down = self.z < levels - 1, self.z > 0

    def at(self, level, column):
        return {"wide": level * 4 + column, "narrow": self.core}

    def partner(self):
        return {"wide": self.z * 4 + self.p, "narrow": 1 - self.core}

    def up(self):
        return self.at(self.z + 1, self.p)

    def down(self):
        return self.at(self.z - 1, self.p)

    def greet(self):
        barrier = pltpu.get_barrier_semaphore()

        def hello(device):
            pl.semaphore_signal(barrier, inc=1, device_id=device, device_id_type=MESH)

        hello(self.partner())
        hello(self.at(self.z, self.a))
        hello(self.at(self.z, self.b))
        pl.when(self.has_up)(lambda: hello(self.up()))
        pl.when(self.has_down)(lambda: hello(self.down()))

    def greeted(self):
        ends = self.has_up.astype(jnp.int32) + self.has_down.astype(jnp.int32)
        pl.semaphore_wait(pltpu.get_barrier_semaphore(), 3 + ends)

    def level_of(self, turn):
        low, high = self.z, self.levels - 1 - self.z
        less = (low < high).astype(jnp.int32)
        span = low * less + high * (1 - less)
        paired = (turn <= 2 * span).astype(jnp.int32)
        distance = paired * ((turn + 1) // 2) + (1 - paired) * (turn - span)
        toward = 2 * less - 1
        sign = paired * (2 * (turn % 2) - 1) * toward + (1 - paired) * toward
        return self.z + sign * distance


def fast_kernel(
    levels, draft_len, cache_len, gain, ids, ratios, hidden_hbm, query_hbm, open_hbm, kv_hbm, keys_hbm, values_hbm,
    out_hbm, gate_hbm, up_hbm, down_hbm,
    out, rows_all, terms, near, from_b, from_a, from_b_q, from_a_q, flow_m, flow_q, tables, scale,
    hidden, query, opened, kv, keys, values, out_w, gate_w, up_w, down_w, attended, projected, theirs, residual, act,
    loads, meet, meet_in, t_sends, t_recvs, g_sends, g_recvs, s_sends, s_recvs,
):
    g = Grid(levels)
    z, p, core = g.z, g.p, g.core
    half = jnp.bfloat16
    count, width = hidden.shape
    quarter = count // 4
    main = count - quarter
    tail = 4 * main
    lot = 4 * count
    experts = 8 * levels
    expert = (z * 4 + p) * 2 + core
    tile = projected.shape[3]
    reqs, context_len, head_size = keys.shape
    drafts = query.shape[0] // reqs
    heads = query.shape[1] // head_size
    other = 1 - core

    pairs = (
        (query_hbm, query), (kv_hbm, kv), (keys_hbm, keys), (values_hbm, values), (open_hbm, opened),
        (out_hbm, out_w), (hidden_hbm, hidden), (gate_hbm.at[0], gate_w), (up_hbm.at[0], up_w), (down_hbm.at[0], down_w),
    )
    fetch = [pltpu.make_async_copy(source, target, loads.at[i]) for i, (source, target) in enumerate(pairs)]
    for copy in fetch:
        copy.start()

    g.greet()

    name = lax.broadcasted_iota(jnp.int32, (experts, count), 0)
    weight = jnp.zeros((experts, count), jnp.float32)
    for k in range(ids.shape[0]):
        weight = weight + jnp.where(ids[k : k + 1, :] == name, ratios[k : k + 1, :], 0.0)
    high = weight.astype(half).astype(jnp.float32)
    both = jnp.concatenate([high, weight - high] * 2, axis=0)
    both = jnp.concatenate([both, both], axis=1).T
    lane = lax.broadcasted_iota(jnp.int32, tables.shape[3:], 1)
    tables[z, core, p] = jnp.where(lane < 2 * experts, both[: count // 2], both[count // 2 : count]).astype(half)

    def send(source, target, send_sem, recv_sem, device):
        return pltpu.make_async_remote_copy(
            src_ref=source, dst_ref=target, send_sem=send_sem, recv_sem=recv_sem, device_id=device, device_id_type=MESH
        )

    def table(source, index, recv_index, device):
        return send(source, source, t_sends.at[index], t_recvs.at[recv_index], device)

    def table_near(index, column):
        return table(tables.at[z, core, column], index, index, g.at(z, (g.a, g.b, g.b)[index]))

    def table_far(way, level):
        device = (g.up, g.down, g.partner)[way]()
        return table(tables.at[level, core], 3 + way * levels + level, 3 + (way // 2) * levels + level, device)

    def table_over(level, lane_core):
        return table(tables.at[level, lane_core], 3 + 2 * levels + level, 3 + levels + level, g.partner())

    def attend(first, last):
        for r in range(first, last):
            mine = slice(r * drafts, (r + 1) * drafts)
            q = jnp.concatenate([query[mine, h * head_size : (h + 1) * head_size] for h in range(heads)], axis=0)
            contract = (((1,), (1,)), ((), ()))
            s = lax.dot_general(q, keys[r], contract, preferred_element_type=jnp.float32) * (1.0 / math.sqrt(head_size))
            sd = lax.dot_general(q, kv[0], contract, preferred_element_type=jnp.float32) * (1.0 / math.sqrt(head_size))
            slot = lax.broadcasted_iota(jnp.int32, s.shape, 1)
            column = lax.broadcasted_iota(jnp.int32, sd.shape, 1) - r * drafts
            row = lax.broadcasted_iota(jnp.int32, sd.shape, 0) % drafts
            s = jnp.where(slot < cache_len[r], s, -jnp.inf)
            sd = jnp.where((column >= 0) & (column <= row) & (column < draft_len[r]), sd, -jnp.inf)
            top = jnp.maximum(jnp.max(s, axis=1, keepdims=True), jnp.max(sd, axis=1, keepdims=True))
            probs, probs_d = jnp.exp(s - top), jnp.exp(sd - top)
            total = jnp.sum(probs, axis=1, keepdims=True) + jnp.sum(probs_d, axis=1, keepdims=True)
            context = jnp.dot(probs.astype(half), values[r], preferred_element_type=jnp.float32)
            context = context + jnp.dot(probs_d.astype(half), kv[1], preferred_element_type=jnp.float32)
            context = context / total
            live = lax.broadcasted_iota(jnp.int32, (drafts, head_size), 0) < draft_len[r]
            for h in range(heads):
                part = slice(h * head_size, (h + 1) * head_size)
                shut = 1.0 + jnp.exp(-opened[mine, part].astype(jnp.float32))
                value = context[h * drafts : (h + 1) * drafts] / shut
                attended[mine, part] = jnp.where(live, value, 0.0).astype(half)

    for i in range(5):
        fetch[i].wait()
    attend(0, reqs)
    fetch[5].wait()
    g.greeted()
    table_near(0, p).start()
    table_near(1, p).start()

    def swap(i):
        return send(projected.at[i, other], theirs.at[i], meet.at[i], meet_in.at[i], g.partner())

    tiles = width // tile
    for i in range(tiles):
        product = jnp.dot(attended[...], out_w[:, i * tile : (i + 1) * tile], preferred_element_type=jnp.float32)
        projected[i] = product.reshape(2, count, tile)
        swap(i).start()
    fetch[6].wait()
    table_near(0, g.a).wait_recv()
    table_near(2, g.a).start()
    for i in range(tiles):
        swap(i).wait_recv()

    def m_rows(column):
        return pl.ds(pl.multiple_of(column * main, 16), main)

    def q_rows(column):
        return pl.ds(pl.multiple_of(tail + column * quarter, 16), quarter)

    q_all = pl.ds(tail, count)
    UP, DOWN, A, B, OVER = range(5)

    def target(way):
        return (g.up, g.down, lambda: g.at(z, g.a), lambda: g.at(z, g.b), g.partner)[way]()

    def carry(ref, way, level, slot, recv_slot):
        return send(ref, ref, g_sends.at[way, level, slot], g_recvs.at[level, recv_slot], target(way))

    def m_block(way, level, column, lane_core=core):
        return carry(rows_all.at[level, lane_core, m_rows(column)], way, level, column, column + 9 * (way == OVER))

    def q_block(way, level, column):
        return carry(rows_all.at[level, core, q_rows(column)], way, level, 4 + column, 4 + column)

    def q_level(way, level, lane_core=core):
        return carry(rows_all.at[level, lane_core, q_all], way, level, 8, 13 if way == OVER else 8)

    def along(level, copy):
        @pl.when(g.has_up & (level <= z))
        def _():
            copy(UP)

        @pl.when(g.has_down & (level >= z))
        def _():
            copy(DOWN)

    def norm(i):
        part = slice(i * 16, (i + 1) * 16)
        total = hidden[part, :].astype(jnp.float32) + jnp.concatenate(
            [projected[t, core, part, :] + theirs[t, part, :] for t in range(tiles)], axis=1
        )
        residual[part, :] = total
        spread = jnp.mean(total * total, axis=-1, keepdims=True)
        normed = (total * lax.rsqrt(spread + 1e-06) * gain[...]).astype(half)
        if i * 16 >= main:
            place = tail + p * quarter + i * 16 - main
        else:
            place = p * main + i * 16
        rows_all[z, core, pl.ds(pl.multiple_of(place, 16), 16), :] = normed

    for i in range(main // 16, count // 16):
        norm(i)
    q_block(A, z, p).start()
    q_block(B, z, p).start()
    for i in range(main // 16):
        norm(i)
    along(z, lambda way: m_block(way, z, p).start())
    for way in (A, B, OVER):
        m_block(way, z, p).start()

    def m_first(turn):
        level = g.level_of(turn)
        m_block(A, level, p).wait_recv()
        along(level, lambda way: m_block(way, level, p).start())
        for way in (A, B, OVER):
            m_block(way, level, p).start()

    def compute(level, lane_core):
        for column in range(4):
            block = tables[level, lane_core, column].astype(jnp.float32)
            for part in range(2):
                first = 2 * part * experts + expert
                mine = jnp.where((lane == first) | (lane == first + experts), block, 0.0)
                mine = jnp.broadcast_to(jnp.sum(mine, axis=1, keepdims=True), block.shape)
                for i in range(count // 2 // 16):
                    row = part * (count // 2) + i * 16
                    place = column * main + row if row < main else tail + column * quarter + row - main
                    scale[place : place + 16, :] = mine[i * 16 : (i + 1) * 16]
        x = rows_all.at[level, lane_core]
        gate_proj = jnp.dot(x[...], gate_w[...], preferred_element_type=jnp.float32)
        up_proj = jnp.dot(x[...], up_w[...], preferred_element_type=jnp.float32)
        act[...] = (gate_proj / (1.0 + jnp.exp(-gate_proj)) * up_proj).astype(half)

        @pl.loop(0, width, step=512)
        def _(column):
            part = pl.ds(pl.multiple_of(column, 512), 512)
            produced = jnp.dot(act[...], down_w[:, part], preferred_element_type=jnp.float32)
            produced = produced.astype(half).astype(jnp.float32) * scale[:, 0:1]
            terms[level, lane_core, :, part] = produced.astype(half)

    def term(ref, target_ref, index, level, device):
        return send(ref, target_ref, s_sends.at[index, level], s_recvs.at[index, level], device)

    def term_over(level, lane_core):
        return term(terms.at[level, lane_core], near.at[level], 0, level, g.partner())

    def b_term(level, column, slot):
        return term(terms.at[level, core, m_rows(column)], from_b.at[level, slot], 1 + slot, level, g.at(z, g.b))

    def a_term(level, column):
        return term(terms.at[level, core, m_rows(column)], from_a.at[level], 3, level, g.at(z, g.a))

    def rise_m(level):
        return term(terms.at[level, core, m_rows(p)], flow_m.at[0, level], 4, level, g.up())

    def fall_m(level):
        return term(terms.at[level, core, m_rows(p)], flow_m.at[1, level], 5, level, g.down())

    def rise_q(level):
        return term(terms.at[level, core, q_all], flow_q.at[0, level], 6, level, g.up())

    def fall_q(level):
        return term(terms.at[level, core, q_all], flow_q.at[1, level], 7, level, g.down())

    def b_term_q(column, slot):
        return term(terms.at[z, core, q_rows(column)], from_b_q.at[slot], 8 + slot, z, g.at(z, g.b))

    def a_term_q(column):
        return term(terms.at[z, core, q_rows(column)], from_a_q, 10, z, g.at(z, g.a))

    def table_first(turn):
        level = g.level_of(turn)
        if turn == 0:
            table_near(1, g.b).wait_recv()
            table_near(2, g.d).wait_recv()
        else:
            table_far(0, level).wait_recv()
        along(level, lambda way: table_far(way, level).start())
        table_over(level, core).start()

    def q_second(turn):
        q_block(A, z, g.a).wait_recv()
        q_block(B, z, g.a).start()

    def q_home(turn):
        q_block(B, z, g.b).wait_recv()
        q_block(B, z, g.d).wait_recv()
        along(z, lambda way: q_level(way, z).start())
        q_level(OVER, z).start()

    def q_next(turn):
        level = g.level_of(turn)
        q_level(UP, level).wait_recv()
        along(level, lambda way: q_level(way, level).start())
        q_level(OVER, level).start()

    def m_second(turn):
        level = g.level_of(turn)
        m_block(A, level, g.a).wait_recv()
        m_block(B, level, g.a).start()
        m_block(OVER, level, g.a).start()

    def m_third(turn):
        level = g.level_of(turn)
        m_block(B, level, g.b).wait_recv()
        m_block(OVER, level, g.b).start()

    def m_fourth(turn):
        level = g.level_of(turn)
        m_block(B, level, g.d).wait_recv()
        m_block(OVER, level, g.d).start()

    def rows_over(turn):
        level = g.level_of(turn)
        for column in range(4):
            m_block(OVER, level, column, other).wait_recv()
        q_level(OVER, level, other).wait_recv()
        table_over(level, other).wait_recv()

    def near_in(turn):
        term_over(g.level_of(turn), other).wait_recv()

    def add(level, start, size, extra, last=None):
        @pl.loop(0, size, step=16)
        def _(row):
            row = pl.multiple_of(row, 16)
            part = pl.ds(pl.multiple_of(start + row, 16), 16)
            total = terms[level, core, part, :].astype(jnp.float32) + near[level, part, :].astype(jnp.float32)
            for ref in extra:
                total = total + ref[pl.ds(row, 16), :].astype(jnp.float32)
            if last is None:
                terms[level, core, part, :] = total.astype(half)
            else:
                rest = pl.ds(pl.multiple_of(last + row, 16), 16)
                out[rest, :] = (residual[rest, :] + total).astype(half)

    def add_flow(level, start, size, ref):
        @pl.loop(0, size, step=16)
        def _(row):
            row = pl.multiple_of(row, 16)
            part = pl.ds(pl.multiple_of(start + row, 16), 16)
            total = terms[level, core, part, :].astype(jnp.float32) + ref[pl.ds(row, 16), :].astype(jnp.float32)
            terms[level, core, part, :] = total.astype(half)

    def m_start(column):
        return column * main

    def q_start(column):
        return tail + column * quarter

    def stage_1(turn):
        level = g.level_of(turn)
        add(level, m_start(g.d), main, [])
        b_term(level, g.d, 1).start()
        add(level, m_start(g.b), main, [])
        b_term(level, g.b, 0).start()

    def stage_q(turn):
        level = g.level_of(turn)

        @pl.when((level < z) if turn else g.has_up)
        def _():
            @pl.when(g.has_up)
            def _():
                fall_q(level).wait_recv()
                add_flow(level, tail, count, flow_q.at[1, level])

        @pl.when((level > z) if turn else g.has_down)
        def _():
            @pl.when(g.has_down)
            def _():
                rise_q(level).wait_recv()
                add_flow(level, tail, count, flow_q.at[0, level])

        if turn > 0:
            add(level, tail, count, [])

            @pl.when(level > z)
            def _():
                rise_q(level).start()

            @pl.when(level < z)
            def _():
                fall_q(level).start()

        if turn == 0:
            add(level, q_start(g.d), quarter, [])
            b_term_q(g.d, 1).start()
            add(level, q_start(g.b), quarter, [])
            b_term_q(g.b, 0).start()

    def stage_2(turn):
        level = g.level_of(turn)
        b_term(level, g.d, 1).wait_recv()
        add(level, m_start(g.a), main, [from_b.at[level, 1]])
        a_term(level, g.a).start()

    def stage_2q(turn):
        b_term_q(g.d, 1).wait_recv()
        add(z, q_start(g.a), quarter, [from_b_q.at[1]])
        a_term_q(g.a).start()

    def stage_3(turn):
        level = g.level_of(turn)

        @pl.when((level < z) if turn else g.has_up)
        def _():
            @pl.when(g.has_up)
            def _():
                fall_m(level).wait_recv()
                add_flow(level, m_start(p), main, flow_m.at[1, level])

        @pl.when((level > z) if turn else g.has_down)
        def _():
            @pl.when(g.has_down)
            def _():
                rise_m(level).wait_recv()
                add_flow(level, m_start(p), main, flow_m.at[0, level])

        b_term(level, g.b, 0).wait_recv()
        a_term(level, g.a).wait_recv()

        if turn > 0:
            add(level, m_start(p), main, [from_b.at[level, 0], from_a.at[level]])

            @pl.when(level > z)
            def _():
                rise_m(level).start()

            @pl.when(level < z)
            def _():
                fall_m(level).start()

        if turn == 0:
            add(level, m_start(p), main, [from_b.at[level, 0], from_a.at[level]], last=0)

    def stage_3q(turn):
        b_term_q(g.b, 0).wait_recv()
        a_term_q(g.a).wait_recv()
        add(z, q_start(p), quarter, [from_b_q.at[0], from_a_q], last=main)

    steps = {
        "t": table_first, "q2": q_second, "qh": q_home, "q": q_next, "m1": m_first, "m2": m_second, "m3": m_third,
        "m4": m_fourth, "co": rows_over, "nw": near_in, "s1": stage_1, "sq": stage_q, "s2": stage_2, "s2q": stage_2q,
        "s3": stage_3, "s3q": stage_3q,
    }
    at_end = (z == 0) | (z == levels - 1)
    is_end = at_end.astype(jnp.int32)

    def parts_of(plan):
        parts, pieces = [[]], []
        for entry in plan:
            if entry[0] == "co":
                parts[-1].append(entry)
            if entry[0] in ("co", "cw"):
                pieces.append(2 * entry[1] + (entry[0] == "cw"))
                parts.append([])
            else:
                parts[-1].append(entry)
        return parts, pieces

    def play(part):
        def run():
            for name, turn in part:
                steps[name](turn)

        return run

    (end_parts, end_pieces), (middle_parts, middle_pieces) = parts_of(END_PLAN), parts_of(MIDDLE_PLAN)

    @pl.loop(0, len(end_parts))
    def _(step):
        piece = 0
        for i in range(len(end_parts)):
            pl.when((step == i) & at_end)(play(end_parts[i]))
            pl.when((step == i) & jnp.logical_not(at_end))(play(middle_parts[i]))
            if i < len(end_pieces):
                chosen = is_end * end_pieces[i] + (1 - is_end) * middle_pieces[i]
                piece = piece + (step == i).astype(jnp.int32) * chosen

        @pl.when(step == 0)
        def _():
            for copy in fetch[7:]:
                copy.wait()

        @pl.when(step < len(end_pieces))
        def _():
            level = g.level_of(piece // 2)
            mine = piece % 2
            compute(level, mine * core + (1 - mine) * other)

            @pl.when(mine == 0)
            def _():
                term_over(level, other).start()

    for i in range(3):
        table_near(i, p).wait_send()
    for i in range(tiles):
        swap(i).wait_send()
    q_block(A, z, p).wait_send()
    q_block(B, z, p).wait_send()
    q_block(B, z, g.a).wait_send()
    b_term_q(g.d, 1).wait_send()
    b_term_q(g.b, 0).wait_send()
    a_term_q(g.a).wait_send()

    @pl.loop(0, levels)
    def _(level):
        table_over(level, core).wait_send()
        along(level, lambda way: table_far(way, level).wait_send())
        along(level, lambda way: m_block(way, level, p).wait_send())
        along(level, lambda way: q_level(way, level).wait_send())
        for way in (A, B, OVER):
            m_block(way, level, p).wait_send()
        for way in (B, OVER):
            m_block(way, level, g.a).wait_send()
        m_block(OVER, level, g.b).wait_send()
        m_block(OVER, level, g.d).wait_send()
        q_level(OVER, level).wait_send()
        term_over(level, other).wait_send()
        b_term(level, g.d, 1).wait_send()
        b_term(level, g.b, 0).wait_send()
        a_term(level, g.a).wait_send()

        @pl.when(level > z)
        def _():
            rise_m(level).wait_send()
            rise_q(level).wait_send()

        @pl.when(level < z)
        def _():
            fall_m(level).wait_send()
            fall_q(level).wait_send()


def run_fast(
    hidden, queries, out_gate, draft_kv, cache_keys, cache_values, draft_len, cache_len, o_weight, norm_gain,
    route_ids, route_weights, w_gate, w_up, w_down,
):
    levels = lax.axis_size("wide") // 4
    count, width = hidden.shape
    quarter = count // 4
    main, lot = count - quarter, 4 * count
    inner = w_gate.shape[2]
    half = jnp.bfloat16
    tile = 512
    lanes = max(128, 32 * levels)
    dma = pltpu.SemaphoreType.DMA
    vmem, smem, hbm = (pl.BlockSpec(memory_space=space) for space in (pltpu.VMEM, pltpu.SMEM, pl.ANY))
    return pl.pallas_call(
        functools.partial(fast_kernel, levels),
        out_shape=jax.ShapeDtypeStruct((count, width), half),
        in_specs=[smem] * 2 + [vmem] * 3 + [hbm] * 10,
        out_specs=vmem,
        scratch_shapes=[
            pltpu.VMEM((levels, 2, lot, width), half),
            pltpu.VMEM((levels, 2, lot, width), half),
            pltpu.VMEM((levels, lot, width), half),
            pltpu.VMEM((levels, 2, main, width), half),
            pltpu.VMEM((levels, main, width), half),
            pltpu.VMEM((2, quarter, width), half),
            pltpu.VMEM((quarter, width), half),
            pltpu.VMEM((2, levels, main, width), half),
            pltpu.VMEM((2, levels, count, width), half),
            pltpu.VMEM((levels, 2, 4, count // 2, lanes), half),
            pltpu.VMEM((lot, lanes), jnp.float32),
            pltpu.VMEM(hidden.shape, half),
            pltpu.VMEM(queries.shape, half),
            pltpu.VMEM(out_gate.shape, half),
            pltpu.VMEM(draft_kv.shape, half),
            pltpu.VMEM(cache_keys.shape, half),
            pltpu.VMEM(cache_values.shape, half),
            pltpu.VMEM(o_weight.shape, half),
            pltpu.VMEM((width, inner), half),
            pltpu.VMEM((width, inner), half),
            pltpu.VMEM((inner, width), half),
            pltpu.VMEM(queries.shape, half),
            pltpu.VMEM((width // tile, 2, count, tile), jnp.float32),
            pltpu.VMEM((width // tile, count, tile), jnp.float32),
            pltpu.VMEM((count, width), jnp.float32),
            pltpu.VMEM((lot, inner), half),
            dma((10,)),
            dma((width // tile,)),
            dma((width // tile,)),
            dma((3 + 3 * levels,)),
            dma((3 + 2 * levels,)),
            dma((5, levels, 9)),
            dma((levels, 14)),
            dma((11, levels)),
            dma((11, levels)),
        ],
        compiler_params=pltpu.CompilerParams(
            collective_id=0, has_side_effects=True, vmem_limit_bytes=67043328
        ),
        name="run_layer",
    )(
        draft_len, cache_len, norm_gain[None, :], route_ids.T, route_weights.T, hidden, queries, out_gate, draft_kv,
        cache_keys, cache_values, o_weight, w_gate, w_up, w_down,
    )


def fits_fast(hidden_in, queries, cache_keys):
    levels = lax.axis_size("wide") // 4
    drafts = queries.shape[0] // cache_keys.shape[0]
    return (
        plane_of(lax.axis_size("rep"), lax.axis_size("wide")) == 2
        and hidden_in.shape[0] * 2 == 128
        and hidden_in.shape[1] % 512 == 0
        and drafts % 16 == 0
        and cache_keys.shape[0] % 2 == 0
        and levels * 32 == 128
    )


def on_device(
    hidden_in,
    queries,
    out_gate,
    draft_kv,
    cache_keys,
    cache_values,
    draft_len,
    cache_len,
    o_weight,
    norm_gain,
    route_ids,
    route_weights,
    w_gate,
    w_up,
    w_down,
):
    if fits_fast(hidden_in, queries, cache_keys):
        return run_fast(
            hidden_in, queries, out_gate, draft_kv, cache_keys, cache_values, draft_len, cache_len, o_weight,
            norm_gain, route_ids, route_weights, w_gate, w_up, w_down,
        )
    attended = attention_rows(
        queries, out_gate, draft_kv, cache_keys, cache_values, draft_len, cache_len
    )
    own_rows = hidden_in.shape[0]
    width = hidden_in.shape[1]
    projected = jnp.dot(attended, o_weight, preferred_element_type=jnp.float32)
    projected = projected.reshape(2, own_rows, width)
    top_count = route_ids.shape[1]
    experts = lax.axis_size("wide") * lax.axis_size("narrow")
    capacity = max(2, min(own_rows, (3 * own_rows * top_count + 2 * experts - 1) // (2 * experts)))
    slots = -(-capacity // 16) * 16
    chosen = route_ids[:, :, None] == jnp.arange(experts, dtype=jnp.int32)[None, None, :]
    dense = jnp.sum(jnp.where(chosen, route_weights[:, :, None], 0.0), axis=1)
    coarse = lax.reduce_precision(dense, 8, 7)
    weights = jnp.concatenate([coarse, dense - coarse], axis=1).astype(jnp.bfloat16)
    weights = jnp.pad(weights, ((0, 0), (0, -weights.shape[1] % 128)))
    side = plane_of(lax.axis_size("rep"), lax.axis_size("wide"))
    return run_layer(
        projected, hidden_in, norm_gain[None, :], weights, w_gate, w_up, w_down, slots, side
    )


def solution(mesh):
    placed = (
        P(("rep", "wide", "narrow"), None),
        P(("rep", "wide"), "narrow"),
        P(("rep", "wide"), "narrow"),
        P(None, ("rep", "wide"), None),
        P(("rep", "wide"), None, None),
        P(("rep", "wide"), None, None),
        P(("rep", "wide")),
        P(("rep", "wide")),
        P("narrow", None),
        P(),
        P(("rep", "wide", "narrow"), None),
        P(("rep", "wide", "narrow"), None),
        P(("wide", "narrow"), None, None),
        P(("wide", "narrow"), None, None),
        P(("wide", "narrow"), None, None),
    )
    return jax.shard_map(
        on_device,
        mesh=mesh,
        in_specs=placed,
        out_specs=P(("rep", "wide", "narrow"), None),
        check_vma=False,
    )
```

```python
import math

import functools

import jax
import jax.numpy as jnp
from jax import lax
from jax.experimental import pallas as pl
from jax.experimental.pallas import tpu as pltpu
from jax.sharding import PartitionSpec as P

MESH = pl.DeviceIdType.MESH


def attention_rows(queries, out_gate, draft_kv, cache_keys, cache_values, draft_len, cache_len):
    req_count, context_len, head_size = cache_keys.shape
    row_count = queries.shape[0]
    drafts = row_count // req_count
    head_count = queries.shape[1] // head_size
    query_blocks = queries.reshape(req_count, drafts, head_count, head_size)
    draft_keys = draft_kv[0].reshape(req_count, drafts, head_size)
    draft_values = draft_kv[1].reshape(req_count, drafts, head_size)
    score_scale = 1.0 / math.sqrt(head_size)
    cache_scores = (
        jnp.einsum("rjhd,rcd->rjhc", query_blocks, cache_keys, preferred_element_type=jnp.float32)
        * score_scale
    )
    draft_scores = (
        jnp.einsum("rjhd,rid->rjhi", query_blocks, draft_keys, preferred_element_type=jnp.float32)
        * score_scale
    )
    slots = jnp.arange(context_len, dtype=jnp.int32)
    cache_live = slots[None, :] < cache_len[:, None]
    cache_scores = jnp.where(cache_live[:, None, None, :], cache_scores, -jnp.inf)
    positions = jnp.arange(drafts, dtype=jnp.int32)
    causal = positions[None, :] <= positions[:, None]
    draft_live = causal[None, :, :] & (positions[None, None, :] < draft_len[:, None, None])
    draft_scores = jnp.where(draft_live[:, :, None, :], draft_scores, -jnp.inf)
    row_max = jnp.maximum(jnp.max(cache_scores, axis=-1), jnp.max(draft_scores, axis=-1))
    cache_probs = jnp.exp(cache_scores - row_max[..., None])
    draft_probs = jnp.exp(draft_scores - row_max[..., None])
    denominator = jnp.sum(cache_probs, axis=-1) + jnp.sum(draft_probs, axis=-1)
    context = jnp.einsum(
        "rjhc,rcd->rjhd",
        cache_probs.astype(jnp.bfloat16),
        cache_values,
        preferred_element_type=jnp.float32,
    )
    context = context + jnp.einsum(
        "rjhi,rid->rjhd",
        draft_probs.astype(jnp.bfloat16),
        draft_values,
        preferred_element_type=jnp.float32,
    )
    context = context / denominator[..., None]
    gate_open = jax.nn.sigmoid(out_gate.astype(jnp.float32)).reshape(
        req_count, drafts, head_count, head_size
    )
    row_live = (positions[None, :] < draft_len[:, None]).astype(jnp.float32)
    attended = context * gate_open * row_live[:, :, None, None]
    return attended.reshape(row_count, head_count * head_size).astype(jnp.bfloat16)


def plane_of(rep_count, wide_count):
    return 2 if rep_count == 1 and wide_count % 4 == 0 else 1


class Place:
    def __init__(self, side, wide_count):
        self.side, self.levels = side, wide_count // (side * side)
        wide = lax.axis_index("wide")
        self.core = lax.axis_index("narrow")
        self.z = wide // (side * side)
        self.y = (wide // side) % side
        self.x = wide % side
        c = self.core
        if side == 2:
            flip_y, flip_x = 1 - 2 * self.y, 1 - 2 * self.x
            self.y2, self.x2 = self.y + c * flip_y, self.x + (1 - c) * flip_x
            self.y3, self.x3 = self.y + (1 - c) * flip_y, self.x + c * flip_x
            self.y4, self.x4 = self.y + flip_y, self.x + flip_x

    def chip(self, z, kind):
        y, x = {
            1: (self.y, self.x),
            2: (getattr(self, "y2", 0), getattr(self, "x2", 0)),
            3: (getattr(self, "y3", 0), getattr(self, "x3", 0)),
            4: (getattr(self, "y4", 0), getattr(self, "x4", 0)),
        }[kind]
        return (z * self.side + y) * self.side + x

    def device(self, chip):
        return {"wide": chip, "narrow": self.core}

    def partner(self):
        return {"wide": self.chip(self.z, 1), "narrow": 1 - self.core}

    def greet(self):
        barrier = pltpu.get_barrier_semaphore()
        pl.semaphore_signal(barrier, inc=1, device_id=self.partner(), device_id_type=MESH)
        count = 1
        if self.side == 2:
            for kind in (2, 3):
                pl.semaphore_signal(
                    barrier,
                    inc=1,
                    device_id=self.device(self.chip(self.z, kind)),
                    device_id_type=MESH,
                )
            count = 3
        has_up, has_down = self.z < self.levels - 1, self.z > 0

        @pl.when(has_up)
        def _():
            pl.semaphore_signal(
                barrier, inc=1, device_id=self.device(self.chip(self.z + 1, 1)), device_id_type=MESH
            )

        @pl.when(has_down)
        def _():
            pl.semaphore_signal(
                barrier, inc=1, device_id=self.device(self.chip(self.z - 1, 1)), device_id_type=MESH
            )

        ends = has_up.astype(jnp.int32) + has_down.astype(jnp.int32)
        pl.semaphore_wait(barrier, count + ends)


def norm_rows(at, chunk, projected, hidden, gain, residual, rows_ref, theirs, meet):
    count = hidden.shape[0]
    swap = pltpu.make_async_remote_copy(
        src_ref=projected.at[1 - at.core],
        dst_ref=theirs,
        send_sem=meet.at[0],
        recv_sem=meet.at[1],
        device_id=at.partner(),
        device_id_type=MESH,
    )
    swap.start()
    swap.wait()

    @pl.loop(0, count, step=chunk)
    def _(row):
        part = pl.ds(pl.multiple_of(row, chunk), chunk)
        total = hidden[part, :].astype(jnp.float32) + (projected[at.core, part, :] + theirs[part, :])
        residual[part, :] = total
        spread = jnp.mean(total * total, axis=-1, keepdims=True)
        rows_ref[part, : total.shape[1]] = (total * lax.rsqrt(spread + 1e-06) * gain[...]).astype(rows_ref.dtype)


def layer_kernel(
    side, wide_count, chunk, slots, projected, hidden, gain, weights, gate_hbm, up_hbm, down_hbm,
    out, rows_all, terms, residual, theirs, gate_w, up_w, down_w, triangle, pick, pick_t, scale, picked, act,
    near, third, second, flow, meet, loads, g_sends, g_recvs, s_sends, s_recvs,
):
    at = Place(side, wide_count)
    z, levels, core = at.z, at.levels, at.core
    count, width = hidden.shape
    chips = side * side
    kinds = (4, 3, 2, 1) if side == 2 else (1,)
    group = 2 * chips
    experts = 2 * wide_count
    expert = at.chip(z, 1) * 2 + core
    fetch = [
        pltpu.make_async_copy(source.at[0], target, loads.at[i])
        for i, (source, target) in enumerate(((gate_hbm, gate_w), (up_hbm, up_w), (down_hbm, down_w)))
    ]
    for copy in fetch:
        copy.start()
    at.greet()
    own = rows_all.at[expert]
    norm_rows(at, chunk, projected, hidden, gain, residual, own, theirs, meet)
    own[:, width:] = weights[...]

    def carry(chip, block_core, lane, target):
        block = rows_all.at[chip * 2 + block_core]
        return pltpu.make_async_remote_copy(
            src_ref=block,
            dst_ref=block,
            send_sem=g_sends.at[chip, lane],
            recv_sem=g_recvs.at[chip * 2 + block_core],
            device_id=target,
            device_id_type=MESH,
        )

    def above():
        return at.device(at.chip(z + 1, 1))

    def below():
        return at.device(at.chip(z - 1, 1))

    def visit(distance, kind):
        for sign in (1, -1):
            level = z + sign * distance
            present = (distance >= 0) & (level >= 0) & (level < levels)
            if sign < 0:
                present = present & (distance > 0)

            @pl.when(present)
            def _():
                chip = at.chip(level, kind)
                if kind == 1:

                    @pl.when(distance > 0)
                    def _():
                        carry(chip, core, 4, at.partner()).wait_recv()

                    go_up = z < levels - 1
                    go_down = z > 0
                    if sign > 0:
                        go_up = go_up & (distance == 0)
                    else:
                        go_down = go_down & (distance == 0)

                    @pl.when(go_up)
                    def _():
                        carry(chip, core, 0, above()).start()

                    @pl.when(go_down)
                    def _():
                        carry(chip, core, 1, below()).start()

                    if side == 2:
                        carry(chip, core, 2, at.device(at.chip(z, 2))).start()
                else:
                    carry(chip, core, 4, at.partner()).wait_recv()
                if side == 2 and kind in (1, 2):
                    carry(chip, core, 3, at.device(at.chip(z, 3))).start()
                carry(chip, core, 4, at.partner()).start()

    def level_of(turn):
        low, high = z, levels - 1 - z
        less = (low < high).astype(jnp.int32)
        span = low * less + high * (1 - less)
        paired = (turn <= 2 * span).astype(jnp.int32)
        distance = paired * ((turn + 1) // 2) + (1 - paired) * (turn - span)
        sign = paired * (2 * (turn % 2) - 1) + (1 - paired) * (2 * less - 1)
        return z + sign * distance

    many = group * count
    tile = 512

    row = lax.broadcasted_iota(jnp.int32, (many, many), 0)
    other = lax.broadcasted_iota(jnp.int32, (many, many), 1)
    triangle[...] = ((other < row) & (other // count == row // count)).astype(jnp.float32).astype(jnp.bfloat16)

    def compute(level):
        base = level * group
        table = rows_all[pl.ds(base, group), :, width:].reshape(many, weights.shape[1])
        lane = lax.broadcasted_iota(jnp.int32, table.shape, 1)
        mine = jnp.where((lane == expert) | (lane == experts + expert), table.astype(jnp.float32), 0.0)
        mine = jnp.sum(mine, axis=1, keepdims=True)
        live = mine > 0.0
        flags = jnp.broadcast_to(live.astype(jnp.float32), (many, 128)).astype(jnp.bfloat16)
        order = jnp.dot(triangle[...], flags, preferred_element_type=jnp.float32)[:, :1]
        start = (lax.broadcasted_iota(jnp.int32, (many, 1), 0) // count * slots).astype(jnp.float32)
        seat = lax.broadcasted_iota(jnp.int32, (many, group * slots), 1).astype(jnp.float32)
        chosen = live & (seat == order + start)
        chosen = chosen.astype(jnp.float32)
        pick[...] = chosen.astype(jnp.bfloat16)
        pick_t[...] = chosen.T.astype(jnp.bfloat16)
        scale[...] = mine

        @pl.loop(0, width, step=tile)
        def _(column):
            part = pl.ds(pl.multiple_of(column, tile), tile)
            rows = rows_all[pl.ds(base, group), :, part].reshape(many, tile)
            picked[:, part] = jnp.dot(
                pick_t[...], rows, preferred_element_type=jnp.float32
            ).astype(jnp.bfloat16)

        gate_proj = jnp.dot(picked[...], gate_w[...], preferred_element_type=jnp.float32)
        up_proj = jnp.dot(picked[...], up_w[...], preferred_element_type=jnp.float32)
        act[...] = (gate_proj / (1.0 + jnp.exp(-gate_proj)) * up_proj).astype(jnp.bfloat16)

        @pl.loop(0, width, step=tile)
        def _(column):
            part = pl.ds(pl.multiple_of(column, tile), tile)
            produced = jnp.dot(act[...], down_w[:, part], preferred_element_type=jnp.float32)
            back = jnp.dot(pick[...], produced.astype(jnp.bfloat16), preferred_element_type=jnp.float32)
            sums = (back * scale[...]).astype(jnp.bfloat16)
            terms[pl.ds(base, group), :, part] = sums.reshape(group, count, tile)

    def copy_of(source, target, index, lane, chip, device):
        return pltpu.make_async_remote_copy(
            src_ref=source,
            dst_ref=target.at[index],
            send_sem=s_sends.at[lane, chip],
            recv_sem=s_recvs.at[lane, chip],
            device_id=device,
            device_id_type=MESH,
        )

    def to_partner(chip, block_core):
        return copy_of(terms.at[chip * 2 + block_core], near, chip, 0, chip, at.partner())

    def hop(kind, chip, level):
        held = terms.at[chip * 2 + core]
        if kind in (3, 4):
            return copy_of(held, third, chip, 1, chip, at.device(at.chip(z, 3)))
        return copy_of(held, second, level, 2, chip, at.device(at.chip(z, 2)))

    def rise(chip, level):
        return copy_of(terms.at[chip * 2 + core], flow, level, 3, chip, above())

    def fall(chip, level):
        ends = (level == z - 1).astype(jnp.int32)
        slot = level * (1 - ends) + levels * ends
        return copy_of(terms.at[chip * 2 + core], flow, slot, 4, chip, below())

    def fallen(chip):
        return copy_of(terms.at[chip * 2 + core], flow, levels, 4, chip, below())

    def add(chip, extra, last=False):
        @pl.loop(0, count, step=chunk)
        def _(row):
            part = pl.ds(pl.multiple_of(row, chunk), chunk)
            total = terms[chip * 2 + core, part, :].astype(jnp.float32)
            for ref, index in extra:
                total = total + ref[index, part, :].astype(jnp.float32)
            if last:
                out[part, :] = (residual[part, :] + total).astype(out.dtype)
            else:
                terms[chip * 2 + core, part, :] = total.astype(terms.dtype)

    def received(level, kind):
        chip = at.chip(level, kind)
        to_partner(chip, core).wait_recv()
        extra = [(near, chip)]
        if side == 2 and kind in (1, 2):
            hop(3, chip, level).wait_recv()
            extra.append((third, chip))
        if side == 2 and kind == 1:
            hop(2, chip, level).wait_recv()
            extra.append((second, level))
        return chip, extra

    def pass_on(level, kind):
        chip, extra = received(level, kind)
        add(chip, extra)
        hop(kind, chip, level).start()

    def first_along(level):
        @pl.when((z == 0) & (level > z))
        def _():
            chip, extra = received(level, 1)
            add(chip, extra)
            rise(chip, level).start()

        @pl.when((z == levels - 1) & (level < z))
        def _():
            chip, extra = received(level, 1)
            add(chip, extra)
            fall(chip, level).start()

    delay = 2 if side == 2 else 0

    @pl.loop(0, levels + delay)
    def _(step):
        visit(step, 1)
        if side == 2:
            visit(step - 1, 2)
            visit(step - 1, 3)
            visit(step - 2, 4)
        turn = step - delay

        @pl.when((turn >= 0) & (turn < levels))
        def _():
            level = level_of(turn)
            for kind in kinds:
                carry(at.chip(level, kind), 1 - core, 4, at.partner()).wait_recv()

            @pl.when(turn == 0)
            def _():
                for copy in fetch:
                    copy.wait()

            compute(level)
            for kind in kinds:
                to_partner(at.chip(level, kind), 1 - core).start()

    def last_along(level):
        first_along(level)

        @pl.when((z > 0) & (level > z))
        def _():
            chip, extra = received(level, 1)
            rise(chip, level).wait_recv()
            add(chip, extra + [(flow, level)])
            rise(chip, level).start()

        @pl.when((z < levels - 1) & (level < z))
        def _():
            chip, extra = received(level, 1)
            fall(chip, level).wait_recv()
            add(chip, extra + [(flow, level)])
            fall(chip, level).start()

    lag = 1 if side == 2 else 0

    @pl.loop(0, levels + 2 * lag)
    def _(step):
        if side == 2:

            @pl.when(step < levels)
            def _():
                level = level_of(levels - 1 - step)
                pass_on(level, 4)
                pass_on(level, 3)

            @pl.when((step >= lag) & (step < levels + lag))
            def _():
                pass_on(level_of(levels - 1 + lag - step), 2)

        @pl.when((step >= 2 * lag) & (step < levels + 2 * lag - 1))
        def _():
            last_along(level_of(levels - 1 + 2 * lag - step))

    chip, extra = received(z, 1)

    @pl.when(z > 0)
    def _():
        rise(chip, z).wait_recv()

    @pl.when(z < levels - 1)
    def _():
        fallen(chip).wait_recv()

    @pl.when((z > 0) & (z < levels - 1))
    def _():
        add(chip, extra + [(flow, z), (flow, levels)], last=True)

    @pl.when((z > 0) & (z == levels - 1))
    def _():
        add(chip, extra + [(flow, z)], last=True)

    @pl.when((z == 0) & (z < levels - 1))
    def _():
        add(chip, extra + [(flow, levels)], last=True)

    if levels == 1:
        add(chip, extra, last=True)

    @pl.loop(0, levels)
    def _(level):
        for kind in kinds:
            chip = at.chip(level, kind)
            carry(chip, core, 4, at.partner()).wait_send()
            if side == 2 and kind in (1, 2):
                carry(chip, core, 3, at.partner()).wait_send()
            to_partner(chip, 1 - core).wait_send()
            if kind != 1:
                hop(kind, chip, level).wait_send()
            else:
                if side == 2:
                    carry(chip, core, 2, at.partner()).wait_send()

                @pl.when((z < levels - 1) & (level <= z))
                def _():
                    carry(chip, core, 0, at.partner()).wait_send()

                @pl.when((z > 0) & (level >= z))
                def _():
                    carry(chip, core, 1, at.partner()).wait_send()

                @pl.when(level > z)
                def _():
                    rise(chip, level).wait_send()

                @pl.when(level < z)
                def _():
                    fall(chip, level).wait_send()


def run_layer(projected, hidden, gain, weights, w_gate, w_up, w_down, slots, side):
    wide_count = lax.axis_size("wide")
    blocks, chips = 2 * wide_count, side * side
    levels = wide_count // chips
    rows, width = hidden.shape
    block, half = (rows, width), jnp.bfloat16
    inner = w_gate.shape[2]
    seats, many = 2 * chips * slots, 2 * chips * rows
    lateral = wide_count if side == 2 else 1
    return pl.pallas_call(
        functools.partial(layer_kernel, side, wide_count, 16, slots),
        out_shape=jax.ShapeDtypeStruct(block, half),
        in_specs=[pl.BlockSpec(memory_space=pltpu.VMEM)] * 4
        + [pl.BlockSpec(memory_space=pl.ANY)] * 3,
        out_specs=pl.BlockSpec(memory_space=pltpu.VMEM),
        scratch_shapes=[
            pltpu.VMEM((blocks, rows, width + weights.shape[1]), half),
            pltpu.VMEM((blocks,) + block, half),
            pltpu.VMEM(block, jnp.float32),
            pltpu.VMEM(block, jnp.float32),
            pltpu.VMEM((width, inner), half),
            pltpu.VMEM((width, inner), half),
            pltpu.VMEM((inner, width), half),
            pltpu.VMEM((many, many), half),
            pltpu.VMEM((many, seats), half),
            pltpu.VMEM((seats, many), half),
            pltpu.VMEM((many, 1), jnp.float32),
            pltpu.VMEM((seats, width), half),
            pltpu.VMEM((seats, inner), half),
            pltpu.VMEM((wide_count,) + block, half),
            pltpu.VMEM((lateral,) + block, half),
            pltpu.VMEM((levels if side == 2 else 1,) + block, half),
            pltpu.VMEM((levels + 1,) + block, half),
            pltpu.SemaphoreType.DMA((2,)),
            pltpu.SemaphoreType.DMA((3,)),
            pltpu.SemaphoreType.DMA((wide_count, 5)),
            pltpu.SemaphoreType.DMA((blocks,)),
            pltpu.SemaphoreType.DMA((5, wide_count)),
            pltpu.SemaphoreType.DMA((5, wide_count)),
        ],
        compiler_params=pltpu.CompilerParams(
            collective_id=0, has_side_effects=True, vmem_limit_bytes=67043328
        ),
        name="run_layer",
    )(projected, hidden, gain, weights, w_gate, w_up, w_down)


END_PLAN = (
    ("t", 0), ("m1", 4), ("q2", 0), ("m1", 5), ("m1", 8), ("m1", 6), ("m2", 0), ("m2", 1), ("m2", 4), ("qh", 0),
    ("m2", 2), ("m3", 1), ("m2", 5), ("m1", 12), ("q", 4), ("m2", 6), ("q", 5), ("m2", 8), ("m1", 9), ("m2", 12),
    ("m3", 0), ("t", 1), ("m1", 13), ("m4", 1), ("q", 6), ("q", 7), ("m1", 14), ("m2", 9), ("m4", 0), ("m1", 10),
    ("co", 1), ("t", 3), ("m2", 13), ("m2", 14), ("cw", 1), ("q", 12), ("nw", 1), ("q", 13), ("sq", 5), ("m3", 3),
    ("m4", 3), ("sq", 7), ("m3", 2), ("q", 14), ("q", 8), ("q", 15), ("m2", 10), ("sq", 4), ("sq", 6), ("s1", 1),
    ("t", 2), ("co", 3), ("m4", 2), ("cw", 3), ("nw", 3), ("sq", 12), ("q", 9), ("q", 10), ("q", 11), ("sq", 14),
    ("s2", 4), ("s1", 3), ("sq", 13), ("s2", 6), ("sq", 15), ("co", 2), ("cw", 2), ("nw", 2), ("s2", 13), ("sq", 11),
    ("sq", 8), ("s1", 2), ("s2", 12), ("sq", 10), ("co", 0), ("sq", 9), ("s3", 13), ("s2", 14), ("cw", 0), ("s2", 8),
    ("s2", 9), ("nw", 0), ("s2", 5), ("s3", 12), ("s3", 14), ("s2", 10), ("s1", 0), ("s3", 8), ("s3", 9), ("s3", 10),
    ("s3", 4), ("s3", 5), ("sq", 0), ("s3", 6), ("s2", 2), ("s2", 1), ("s2q", 0), ("s2", 0), ("s3q", 0), ("s3", 1),
    ("s3", 2), ("s3", 0),
)
MIDDLE_PLAN = (
    ("q2", 0), ("m1", 8), ("m1", 4), ("t", 0), ("m1", 9), ("m2", 0), ("m2", 1), ("m1", 5), ("t", 2), ("m2", 2),
    ("m1", 10), ("m1", 12), ("qh", 0), ("m2", 8), ("m2", 9), ("q", 8), ("m1", 13), ("m2", 10), ("m2", 4), ("m1", 14),
    ("q", 9), ("m2", 12), ("m1", 6), ("t", 3), ("m4", 0), ("q", 10), ("q", 4), ("m3", 0), ("q", 12), ("q", 11),
    ("co", 0), ("m3", 2), ("q", 13), ("m2", 13), ("q", 14), ("cw", 0), ("nw", 0), ("m4", 2), ("m2", 14), ("q", 15),
    ("t", 1), ("s1", 0), ("m3", 3), ("m2", 5), ("m2", 6), ("co", 2), ("m4", 3), ("q", 5), ("q", 6), ("cw", 2),
    ("q", 7), ("co", 3), ("nw", 2), ("s1", 2), ("m3", 1), ("m4", 1), ("cw", 3), ("nw", 3), ("s1", 3), ("co", 1),
    ("sq", 12), ("cw", 1), ("sq", 13), ("nw", 1), ("s2", 9), ("s1", 1), ("sq", 14), ("sq", 15), ("sq", 7), ("s2", 12),
    ("sq", 8), ("s2", 8), ("sq", 9), ("sq", 4), ("s2", 13), ("s2", 1), ("s2", 10), ("s2", 14), ("sq", 10), ("s2", 4),
    ("s2", 0), ("sq", 6), ("s2", 5), ("sq", 11), ("sq", 5), ("s3", 13), ("s3", 12), ("s3", 14), ("s2", 6), ("sq", 0),
    ("s3", 9), ("s3", 4), ("s3", 8), ("s3", 5), ("s2", 2), ("s2q", 0), ("s3", 10), ("s3", 6), ("s3", 1), ("s3", 0),
    ("s3q", 0), ("s3", 2),
)


class Grid:
    def __init__(self, levels):
        wide = lax.axis_index("wide")
        self.levels, self.core = levels, lax.axis_index("narrow")
        self.z, self.p = wide // 4, wide % 4
        y, x = self.p // 2, self.p % 2
        along_x, along_y = self.p + 1 - 2 * x, self.p + 2 - 4 * y
        c = self.core
        self.a = (1 - c) * along_x + c * along_y
        self.b = c * along_x + (1 - c) * along_y
        self.d = 3 - self.p
        self.has_up, self.has_down = self.z < levels - 1, self.z > 0

    def at(self, level, column):
        return {"wide": level * 4 + column, "narrow": self.core}

    def partner(self):
        return {"wide": self.z * 4 + self.p, "narrow": 1 - self.core}

    def up(self):
        return self.at(self.z + 1, self.p)

    def down(self):
        return self.at(self.z - 1, self.p)

    def greet(self):
        barrier = pltpu.get_barrier_semaphore()

        def hello(device):
            pl.semaphore_signal(barrier, inc=1, device_id=device, device_id_type=MESH)

        hello(self.partner())
        hello(self.at(self.z, self.a))
        hello(self.at(self.z, self.b))
        pl.when(self.has_up)(lambda: hello(self.up()))
        pl.when(self.has_down)(lambda: hello(self.down()))

    def greeted(self):
        ends = self.has_up.astype(jnp.int32) + self.has_down.astype(jnp.int32)
        pl.semaphore_wait(pltpu.get_barrier_semaphore(), 3 + ends)

    def level_of(self, turn):
        low, high = self.z, self.levels - 1 - self.z
        less = (low < high).astype(jnp.int32)
        span = low * less + high * (1 - less)
        paired = (turn <= 2 * span).astype(jnp.int32)
        distance = paired * ((turn + 1) // 2) + (1 - paired) * (turn - span)
        toward = 2 * less - 1
        sign = paired * (2 * (turn % 2) - 1) * toward + (1 - paired) * toward
        return self.z + sign * distance


def fast_kernel(
    levels, draft_len, cache_len, gain, ids, ratios, hidden_hbm, query_hbm, open_hbm, kv_hbm, keys_hbm, values_hbm,
    out_hbm, gate_hbm, up_hbm, down_hbm,
    out, rows_all, terms, near, from_b, from_a, from_b_q, from_a_q, flow_m, flow_q, tables, scale,
    hidden, query, opened, kv, keys, values, out_w, gate_w, up_w, down_w, attended, projected, theirs, residual, act,
    loads, meet, meet_in, t_sends, t_recvs, g_sends, g_recvs, s_sends, s_recvs,
):
    g = Grid(levels)
    z, p, core = g.z, g.p, g.core
    half = jnp.bfloat16
    count, width = hidden.shape
    quarter = count // 4
    main = count - quarter
    tail = 4 * main
    lot = 4 * count
    experts = 8 * levels
    expert = (z * 4 + p) * 2 + core
    tile = projected.shape[3]
    reqs, context_len, head_size = keys.shape
    drafts = query.shape[0] // reqs
    heads = query.shape[1] // head_size
    other = 1 - core

    pairs = (
        (query_hbm, query), (kv_hbm, kv), (keys_hbm, keys), (values_hbm, values), (open_hbm, opened),
        (out_hbm, out_w), (hidden_hbm, hidden), (gate_hbm.at[0], gate_w), (up_hbm.at[0], up_w), (down_hbm.at[0], down_w),
    )
    fetch = [pltpu.make_async_copy(source, target, loads.at[i]) for i, (source, target) in enumerate(pairs)]
    for copy in fetch:
        copy.start()

    g.greet()

    name = lax.broadcasted_iota(jnp.int32, (experts, count), 0)
    weight = jnp.zeros((experts, count), jnp.float32)
    for k in range(ids.shape[0]):
        weight = weight + jnp.where(ids[k : k + 1, :] == name, ratios[k : k + 1, :], 0.0)
    high = weight.astype(half).astype(jnp.float32)
    both = jnp.concatenate([high, weight - high] * 2, axis=0)
    both = jnp.concatenate([both, both], axis=1).T
    lane = lax.broadcasted_iota(jnp.int32, tables.shape[3:], 1)
    tables[z, core, p] = jnp.where(lane < 2 * experts, both[: count // 2], both[count // 2 : count]).astype(half)

    def send(source, target, send_sem, recv_sem, device):
        return pltpu.make_async_remote_copy(
            src_ref=source, dst_ref=target, send_sem=send_sem, recv_sem=recv_sem, device_id=device, device_id_type=MESH
        )

    def table(source, index, recv_index, device):
        return send(source, source, t_sends.at[index], t_recvs.at[recv_index], device)

    def table_near(index, column):
        return table(tables.at[z, core, column], index, index, g.at(z, (g.a, g.b, g.b)[index]))

    def table_far(way, level):
        device = (g.up, g.down, g.partner)[way]()
        return table(tables.at[level, core], 3 + way * levels + level, 3 + (way // 2) * levels + level, device)

    def table_over(level, lane_core):
        return table(tables.at[level, lane_core], 3 + 2 * levels + level, 3 + levels + level, g.partner())

    def attend(first, last):
        for r in range(first, last):
            mine = slice(r * drafts, (r + 1) * drafts)
            q = jnp.concatenate([query[mine, h * head_size : (h + 1) * head_size] for h in range(heads)], axis=0)
            contract = (((1,), (1,)), ((), ()))
            s = lax.dot_general(q, keys[r], contract, preferred_element_type=jnp.float32) * (1.0 / math.sqrt(head_size))
            sd = lax.dot_general(q, kv[0], contract, preferred_element_type=jnp.float32) * (1.0 / math.sqrt(head_size))
            slot = lax.broadcasted_iota(jnp.int32, s.shape, 1)
            column = lax.broadcasted_iota(jnp.int32, sd.shape, 1) - r * drafts
            row = lax.broadcasted_iota(jnp.int32, sd.shape, 0) % drafts
            s = jnp.where(slot < cache_len[r], s, -jnp.inf)
            sd = jnp.where((column >= 0) & (column <= row) & (column < draft_len[r]), sd, -jnp.inf)
            top = jnp.maximum(jnp.max(s, axis=1, keepdims=True), jnp.max(sd, axis=1, keepdims=True))
            probs, probs_d = jnp.exp(s - top), jnp.exp(sd - top)
            total = jnp.sum(probs, axis=1, keepdims=True) + jnp.sum(probs_d, axis=1, keepdims=True)
            context = jnp.dot(probs.astype(half), values[r], preferred_element_type=jnp.float32)
            context = context + jnp.dot(probs_d.astype(half), kv[1], preferred_element_type=jnp.float32)
            context = context / total
            live = lax.broadcasted_iota(jnp.int32, (drafts, head_size), 0) < draft_len[r]
            for h in range(heads):
                part = slice(h * head_size, (h + 1) * head_size)
                shut = 1.0 + jnp.exp(-opened[mine, part].astype(jnp.float32))
                value = context[h * drafts : (h + 1) * drafts] / shut
                attended[mine, part] = jnp.where(live, value, 0.0).astype(half)

    for i in range(5):
        fetch[i].wait()
    attend(0, reqs)
    fetch[5].wait()
    g.greeted()
    table_near(0, p).start()
    table_near(1, p).start()

    def swap(i):
        return send(projected.at[i, other], theirs.at[i], meet.at[i], meet_in.at[i], g.partner())

    tiles = width // tile
    for i in range(tiles):
        product = jnp.dot(attended[...], out_w[:, i * tile : (i + 1) * tile], preferred_element_type=jnp.float32)
        projected[i] = product.reshape(2, count, tile)
        swap(i).start()
    fetch[6].wait()
    table_near(0, g.a).wait_recv()
    table_near(2, g.a).start()
    for i in range(tiles):
        swap(i).wait_recv()

    thirds = main // 16

    def m_rows(column):
        return pl.ds(pl.multiple_of(column * main, 16), main)

    def m_part(column, i):
        return pl.ds(pl.multiple_of(column * main + i * 16, 16), 16)

    def q_rows(column):
        return pl.ds(pl.multiple_of(tail + column * quarter, 16), quarter)

    q_all = pl.ds(tail, count)
    UP, DOWN, A, B, OVER = range(5)
    from_a_slot, from_b_slot, q_slot, over_slot = thirds, 2 * thirds, 2 * thirds + 2, 2 * thirds + 6

    def target(way):
        return (g.up, g.down, lambda: g.at(z, g.a), lambda: g.at(z, g.b), g.partner)[way]()

    def carry(ref, way, level, slot):
        return send(ref, ref, g_sends.at[way, level], g_recvs.at[level, slot], target(way))

    def m_piece(way, level, column, i, slot):
        return carry(rows_all.at[level, core, m_part(column, i)], way, level, slot)

    def m_z(way, level, i):
        return m_piece(way, level, p, i, i)

    def m_a(level, i):
        return m_piece(A, level, p, i, from_a_slot + i)

    def m_b(level, i, passed):
        return m_piece(B, level, g.a if passed else p, i, from_b_slot + passed)

    def m_b_all(level, column, passed):
        return carry(rows_all.at[level, core, m_rows(column)], B, level, from_b_slot + passed)

    def m_over(level, column):
        return carry(rows_all.at[level, core, m_rows(column)], OVER, level, over_slot)

    def q_block(way, column, slot):
        return carry(rows_all.at[z, core, q_rows(column)], way, z, q_slot + slot)

    def q_piece(way, level, i):
        return carry(rows_all.at[level, core, q_rows(i)], way, level, q_slot + i)

    def q_over(level):
        return carry(rows_all.at[level, core, q_all], OVER, level, over_slot)

    def over_all(level, lane_core):
        return carry(rows_all.at[level, lane_core], OVER, level, over_slot)

    def along(level, copy):
        @pl.when(g.has_up & (level <= z))
        def _():
            copy(UP)

        @pl.when(g.has_down & (level >= z))
        def _():
            copy(DOWN)

    def norm(i):
        part = slice(i * 16, (i + 1) * 16)
        total = hidden[part, :].astype(jnp.float32) + jnp.concatenate(
            [projected[t, core, part, :] + theirs[t, part, :] for t in range(tiles)], axis=1
        )
        residual[part, :] = total
        spread = jnp.mean(total * total, axis=-1, keepdims=True)
        normed = (total * lax.rsqrt(spread + 1e-06) * gain[...]).astype(half)
        if i * 16 >= main:
            place = tail + p * quarter + i * 16 - main
        else:
            place = p * main + i * 16
        rows_all[z, core, pl.ds(pl.multiple_of(place, 16), 16), :] = normed

    for i in range(main // 16, count // 16):
        norm(i)
    q_block(A, p, 0).start()
    q_block(B, p, 1).start()
    for i in range(thirds):
        norm(i)
        along(z, lambda way: m_z(way, z, i).start())
        m_a(z, i).start()
        m_b(z, i, 0).start()
    m_over(z, p).start()

    def compute(level, lane_core):
        for column in range(4):
            block = tables[level, lane_core, column].astype(jnp.float32)
            for part in range(2):
                first = 2 * part * experts + expert
                mine = jnp.where((lane == first) | (lane == first + experts), block, 0.0)
                mine = jnp.broadcast_to(jnp.sum(mine, axis=1, keepdims=True), block.shape)
                for i in range(count // 2 // 16):
                    row = part * (count // 2) + i * 16
                    place = column * main + row if row < main else tail + column * quarter + row - main
                    scale[place : place + 16, :] = mine[i * 16 : (i + 1) * 16]
        x = rows_all.at[level, lane_core]
        gate_proj = jnp.dot(x[...], gate_w[...], preferred_element_type=jnp.float32)
        up_proj = jnp.dot(x[...], up_w[...], preferred_element_type=jnp.float32)
        act[...] = (gate_proj / (1.0 + jnp.exp(-gate_proj)) * up_proj).astype(half)

        @pl.loop(0, width, step=512)
        def _(column):
            part = pl.ds(pl.multiple_of(column, 512), 512)
            produced = jnp.dot(act[...], down_w[:, part], preferred_element_type=jnp.float32)
            produced = produced.astype(half).astype(jnp.float32) * scale[:, 0:1]
            terms[level, lane_core, :, part] = produced.astype(half)

    plane_slot, q_in = 1 + thirds, 1 + 2 * thirds

    def term(ref, target_ref, way, slot, level, device):
        return send(ref, target_ref, s_sends.at[way, level], s_recvs.at[level, slot], device)

    def term_over(level, lane_core):
        return term(terms.at[level, lane_core], near.at[level], 0, 0, level, g.partner())

    def piece(i):
        return pl.ds(pl.multiple_of(i * 16, 16), 16)

    def b_term(level, column, slot, i):
        source = terms.at[level, core, m_part(column, i)]
        counted = 1 + i if slot else plane_slot + i
        return term(source, from_b.at[level, slot, piece(i)], 1, counted, level, g.at(z, g.b))

    def a_term(level, column, i):
        source = terms.at[level, core, m_part(column, i)]
        return term(source, from_a.at[level, piece(i)], 2, plane_slot + i, level, g.at(z, g.a))

    def flow_m_term(way, level, i, device):
        source = terms.at[level, core, m_part(p, i)]
        return term(source, flow_m.at[way, level, piece(i)], 3, plane_slot + i, level, device)

    def flow_q_term(way, level, i, device):
        source = terms.at[level, core, q_rows(i)]
        return term(source, flow_q.at[way, level, piece(i)], 3, q_in + i, level, device)

    def b_term_q(column, slot):
        source = terms.at[z, core, q_rows(column)]
        return term(source, from_b_q.at[slot], 1, q_in + 4 + slot, z, g.at(z, g.b))

    def a_term_q(column):
        return term(terms.at[z, core, q_rows(column)], from_a_q, 2, q_in + 4, z, g.at(z, g.a))

    def arrived(level, slot, rows):
        ref = near.at[level, pl.ds(0, rows)]
        term(ref, ref, 0, slot, level, g.partner()).wait_recv()

    def left(sems, way, level, rows):
        ref = rows_all.at[level, core, pl.ds(0, rows)]
        send(ref, ref, sems.at[way, level], s_recvs.at[level, 0], g.partner()).wait_send()

    def table_first(turn, mid):
        level = g.level_of(turn)
        if turn == 0:
            table_near(1, g.b).wait_recv()
            table_near(2, g.d).wait_recv()
        else:
            table_far(0, level).wait_recv()
        along(level, lambda way: table_far(way, level).start())
        table_over(level, core).start()

    def q_second(turn, mid):
        q_block(A, g.a, 0).wait_recv()
        q_block(B, g.a, 2).start()

    def q_home(turn, mid):
        q_block(B, g.b, 1).wait_recv()
        q_block(B, g.d, 2).wait_recv()

        @pl.loop(0, 4)
        def _(i):
            along(z, lambda way: q_piece(way, z, i).start())

        q_over(z).start()

    def q_next(turn, mid):
        turn, i = turn // 4, turn % 4
        level = g.level_of(turn)
        q_piece(UP, level, i).wait_recv()
        along(level, lambda way: q_piece(way, level, i).start())
        if i == 3:
            q_over(level).start()

    def m_first(turn, mid):
        turn, i = turn // 4, turn % 4
        level = g.level_of(turn)
        m_z(UP, level, i).wait_recv()
        along(level, lambda way: m_z(way, level, i).start())
        m_a(level, i).start()
        m_b(level, i, 0).start()
        if i == thirds - 1:
            m_over(level, p).start()

    def m_second(turn, mid):
        turn, i = turn // 4, turn % 4
        level = g.level_of(turn)
        m_a(level, i).wait_recv()
        m_b(level, i, 1).start()
        if i == thirds - 1:
            m_over(level, g.a).start()

    def m_third(turn, mid):
        level = g.level_of(turn)
        m_b_all(level, g.b, 0).wait_recv()
        m_over(level, g.b).start()

    def m_fourth(turn, mid):
        level = g.level_of(turn)
        m_b_all(level, g.d, 1).wait_recv()
        m_over(level, g.d).start()

    def rows_over(turn, mid):
        level = g.level_of(turn)
        over_all(level, other).wait_recv()
        table_over(level, other).wait_recv()

    def near_in(turn, mid):
        term_over(g.level_of(turn), other).wait_recv()

    def add(level, start, extra, last=None):
        part = pl.ds(pl.multiple_of(start, 16), 16)

        @pl.loop(0, width, step=512)
        def _(column):
            part_of = pl.ds(pl.multiple_of(column, 512), 512)
            total = terms[level, core, part, part_of].astype(jnp.float32) + near[level, part, part_of].astype(jnp.float32)
            for ref in extra:
                total = total + ref[:, part_of].astype(jnp.float32)
            if last is None:
                terms[level, core, part, part_of] = total.astype(half)
            else:
                rest = slice(last, last + 16)
                out[rest, part_of] = (residual[rest, part_of] + total).astype(half)

    def m_start(column, i):
        return column * main + i * 16

    def q_start(column):
        return tail + column * quarter

    def rising(level):
        return (level > z).astype(jnp.int32)

    def ways_in(turn, mid):
        if turn == 0:
            return (0, 1) if mid else ((z == 0).astype(jnp.int32),)
        return (1 - rising(g.level_of(turn)),) if mid else ()

    def stage_1(turn, mid):
        level = g.level_of(turn)

        @pl.loop(0, thirds)
        def _(i):
            add(level, m_start(g.d, i), [])
            b_term(level, g.d, 1, i).start()
            add(level, m_start(g.b, i), [])
            b_term(level, g.b, 0, i).start()

    def stage_2(turn, mid):
        turn, i = turn // 4, turn % 4
        level = g.level_of(turn)
        b_term(level, g.d, 1, i).wait_recv()
        add(level, m_start(g.a, i), [from_b.at[level, 1, piece(i)]])
        a_term(level, g.a, i).start()

    def stage_q(turn, mid):
        turn, i = turn // 4, turn % 4
        level = g.level_of(turn)
        ways = ways_in(turn, mid)

        def arrive(i):
            if ways:
                arrived(level, q_in + i, 16 * len(ways))

        def sum_of(i):
            add(level, q_start(i), [flow_q.at[way, level, piece(i)] for way in ways])

        if turn == 0:

            @pl.loop(0, 4)
            def _(column):
                arrive(column)
                pl.when((column != p) & (column != g.a))(lambda: sum_of(column))

            b_term_q(g.d, 1).start()
            b_term_q(g.b, 0).start()
        else:
            arrive(i)
            sum_of(i)
            pl.when(level > z)(lambda: flow_q_term(0, level, i, g.up()).start())
            pl.when(level < z)(lambda: flow_q_term(1, level, i, g.down()).start())

    def stage_2q(turn, mid):
        b_term_q(g.d, 1).wait_recv()
        add(z, q_start(g.a), [from_b_q.at[1]] + [flow_q.at[way, z, piece(g.a)] for way in ways_in(0, mid)])
        a_term_q(g.a).start()

    def stage_3q(turn, mid):
        arrived(z, q_in + 4, 2 * quarter)
        add(z, q_start(p), [from_b_q.at[0], from_a_q] + [flow_q.at[way, z, piece(p)] for way in ways_in(0, mid)], last=main)

    def stage_3(turn, mid):
        turn, i = turn // 4, turn % 4
        level = g.level_of(turn)
        ways = ways_in(turn, mid)
        arrived(level, plane_slot + i, 16 * (2 + len(ways)))
        extra = [from_b.at[level, 0, piece(i)], from_a.at[level, piece(i)]]
        extra = extra + [flow_m.at[way, level, piece(i)] for way in ways]
        if turn == 0:
            add(level, m_start(p, i), extra, last=i * 16)
        else:
            add(level, m_start(p, i), extra)
            pl.when(level > z)(lambda: flow_m_term(0, level, i, g.up()).start())
            pl.when(level < z)(lambda: flow_m_term(1, level, i, g.down()).start())

    steps = {
        "t": table_first, "q2": q_second, "qh": q_home, "q": q_next, "m1": m_first, "m2": m_second, "m3": m_third,
        "m4": m_fourth, "co": rows_over, "nw": near_in, "s1": stage_1, "sq": stage_q, "s2": stage_2, "s2q": stage_2q,
        "s3": stage_3, "s3q": stage_3q,
    }
    at_end = (z == 0) | (z == levels - 1)
    is_end = at_end.astype(jnp.int32)

    def parts_of(plan):
        parts, pieces = [[]], []
        for entry in plan:
            if entry[0] == "co":
                parts[-1].append(entry)
            if entry[0] in ("co", "cw"):
                pieces.append(2 * entry[1] + (entry[0] == "cw"))
                parts.append([])
            else:
                parts[-1].append(entry)
        return parts, pieces

    def play(part, mid):
        def run():
            for name, turn in part:
                steps[name](turn, mid)

        return run

    (end_parts, end_pieces), (middle_parts, middle_pieces) = parts_of(END_PLAN), parts_of(MIDDLE_PLAN)

    @pl.loop(0, len(end_parts))
    def _(step):
        piece = 0
        for i in range(len(end_parts)):
            pl.when((step == i) & at_end)(play(end_parts[i], False))
            pl.when((step == i) & jnp.logical_not(at_end))(play(middle_parts[i], True))
            if i < len(end_pieces):
                chosen = is_end * end_pieces[i] + (1 - is_end) * middle_pieces[i]
                piece = piece + (step == i).astype(jnp.int32) * chosen

        @pl.when(step == 0)
        def _():
            for copy in fetch[7:]:
                copy.wait()

        @pl.when(step < len(end_pieces))
        def _():
            level = g.level_of(piece // 2)
            mine = piece % 2
            compute(level, mine * core + (1 - mine) * other)

            @pl.when(mine == 0)
            def _():
                term_over(level, other).start()

    for i in range(3):
        table_near(i, p).wait_send()
    for i in range(tiles):
        swap(i).wait_send()
    @pl.loop(0, levels)
    def _(level):
        table_over(level, core).wait_send()
        along(level, lambda way: table_far(way, level).wait_send())
        along(level, lambda way: left(g_sends, way, level, main + count))
        left(g_sends, OVER, level, lot)
        left(s_sends, 0, level, lot)

        @pl.when(level == z)
        def _():
            for sems, a_way, b_way in ((g_sends, A, B), (s_sends, 2, 1)):
                left(sems, a_way, level, count)
                left(sems, b_way, level, 2 * count)

        @pl.when(level != z)
        def _():
            for sems, a_way, b_way in ((g_sends, A, B), (s_sends, 2, 1)):
                left(sems, a_way, level, main)
                left(sems, b_way, level, 2 * main)
            left(s_sends, 3, level, main + count)


def run_fast(
    hidden, queries, out_gate, draft_kv, cache_keys, cache_values, draft_len, cache_len, o_weight, norm_gain,
    route_ids, route_weights, w_gate, w_up, w_down,
):
    levels = lax.axis_size("wide") // 4
    count, width = hidden.shape
    quarter = count // 4
    main, lot = count - quarter, 4 * count
    inner = w_gate.shape[2]
    half = jnp.bfloat16
    tile = 512
    lanes = max(128, 32 * levels)
    dma = pltpu.SemaphoreType.DMA
    vmem, smem, hbm = (pl.BlockSpec(memory_space=space) for space in (pltpu.VMEM, pltpu.SMEM, pl.ANY))
    return pl.pallas_call(
        functools.partial(fast_kernel, levels),
        out_shape=jax.ShapeDtypeStruct((count, width), half),
        in_specs=[smem] * 2 + [vmem] * 3 + [hbm] * 10,
        out_specs=vmem,
        scratch_shapes=[
            pltpu.VMEM((levels, 2, lot, width), half),
            pltpu.VMEM((levels, 2, lot, width), half),
            pltpu.VMEM((levels, lot, width), half),
            pltpu.VMEM((levels, 2, main, width), half),
            pltpu.VMEM((levels, main, width), half),
            pltpu.VMEM((2, quarter, width), half),
            pltpu.VMEM((quarter, width), half),
            pltpu.VMEM((2, levels, main, width), half),
            pltpu.VMEM((2, levels, count, width), half),
            pltpu.VMEM((levels, 2, 4, count // 2, lanes), half),
            pltpu.VMEM((lot, lanes), jnp.float32),
            pltpu.VMEM(hidden.shape, half),
            pltpu.VMEM(queries.shape, half),
            pltpu.VMEM(out_gate.shape, half),
            pltpu.VMEM(draft_kv.shape, half),
            pltpu.VMEM(cache_keys.shape, half),
            pltpu.VMEM(cache_values.shape, half),
            pltpu.VMEM(o_weight.shape, half),
            pltpu.VMEM((width, inner), half),
            pltpu.VMEM((width, inner), half),
            pltpu.VMEM((inner, width), half),
            pltpu.VMEM(queries.shape, half),
            pltpu.VMEM((width // tile, 2, count, tile), jnp.float32),
            pltpu.VMEM((width // tile, count, tile), jnp.float32),
            pltpu.VMEM((count, width), jnp.float32),
            pltpu.VMEM((lot, inner), half),
            dma((10,)),
            dma((width // tile,)),
            dma((width // tile,)),
            dma((3 + 3 * levels,)),
            dma((3 + 2 * levels,)),
            dma((5, levels)),
            dma((levels, 7 + main // 8)),
            dma((4, levels)),
            dma((levels, 7 + main // 8)),
        ],
        compiler_params=pltpu.CompilerParams(
            collective_id=0, has_side_effects=True, vmem_limit_bytes=67043328
        ),
        name="run_layer",
    )(
        draft_len, cache_len, norm_gain[None, :], route_ids.T, route_weights.T, hidden, queries, out_gate, draft_kv,
        cache_keys, cache_values, o_weight, w_gate, w_up, w_down,
    )


def fits_fast(hidden_in, queries, cache_keys):
    levels = lax.axis_size("wide") // 4
    drafts = queries.shape[0] // cache_keys.shape[0]
    return (
        plane_of(lax.axis_size("rep"), lax.axis_size("wide")) == 2
        and hidden_in.shape[0] * 2 == 128
        and hidden_in.shape[1] % 512 == 0
        and drafts % 16 == 0
        and cache_keys.shape[0] % 2 == 0
        and levels * 32 == 128
    )


def on_device(
    hidden_in,
    queries,
    out_gate,
    draft_kv,
    cache_keys,
    cache_values,
    draft_len,
    cache_len,
    o_weight,
    norm_gain,
    route_ids,
    route_weights,
    w_gate,
    w_up,
    w_down,
):
    if fits_fast(hidden_in, queries, cache_keys):
        return run_fast(
            hidden_in, queries, out_gate, draft_kv, cache_keys, cache_values, draft_len, cache_len, o_weight,
            norm_gain, route_ids, route_weights, w_gate, w_up, w_down,
        )
    attended = attention_rows(
        queries, out_gate, draft_kv, cache_keys, cache_values, draft_len, cache_len
    )
    own_rows = hidden_in.shape[0]
    width = hidden_in.shape[1]
    projected = jnp.dot(attended, o_weight, preferred_element_type=jnp.float32)
    projected = projected.reshape(2, own_rows, width)
    top_count = route_ids.shape[1]
    experts = lax.axis_size("wide") * lax.axis_size("narrow")
    capacity = max(2, min(own_rows, (3 * own_rows * top_count + 2 * experts - 1) // (2 * experts)))
    slots = -(-capacity // 16) * 16
    chosen = route_ids[:, :, None] == jnp.arange(experts, dtype=jnp.int32)[None, None, :]
    dense = jnp.sum(jnp.where(chosen, route_weights[:, :, None], 0.0), axis=1)
    coarse = lax.reduce_precision(dense, 8, 7)
    weights = jnp.concatenate([coarse, dense - coarse], axis=1).astype(jnp.bfloat16)
    weights = jnp.pad(weights, ((0, 0), (0, -weights.shape[1] % 128)))
    side = plane_of(lax.axis_size("rep"), lax.axis_size("wide"))
    return run_layer(
        projected, hidden_in, norm_gain[None, :], weights, w_gate, w_up, w_down, slots, side
    )


def solution(mesh):
    placed = (
        P(("rep", "wide", "narrow"), None),
        P(("rep", "wide"), "narrow"),
        P(("rep", "wide"), "narrow"),
        P(None, ("rep", "wide"), None),
        P(("rep", "wide"), None, None),
        P(("rep", "wide"), None, None),
        P(("rep", "wide")),
        P(("rep", "wide")),
        P("narrow", None),
        P(),
        P(("rep", "wide", "narrow"), None),
        P(("rep", "wide", "narrow"), None),
        P(("wide", "narrow"), None, None),
        P(("wide", "narrow"), None, None),
        P(("wide", "narrow"), None, None),
    )
    return jax.shard_map(
        on_device,
        mesh=mesh,
        in_specs=placed,
        out_specs=P(("rep", "wide", "narrow"), None),
        check_vma=False,
    )
```

```python
import math

import functools

import jax
import jax.numpy as jnp
from jax import lax
from jax.experimental import pallas as pl
from jax.experimental.pallas import tpu as pltpu
from jax.sharding import PartitionSpec as P

MESH = pl.DeviceIdType.MESH


def attention_rows(queries, out_gate, draft_kv, cache_keys, cache_values, draft_len, cache_len):
    req_count, context_len, head_size = cache_keys.shape
    row_count = queries.shape[0]
    drafts = row_count // req_count
    head_count = queries.shape[1] // head_size
    query_blocks = queries.reshape(req_count, drafts, head_count, head_size)
    draft_keys = draft_kv[0].reshape(req_count, drafts, head_size)
    draft_values = draft_kv[1].reshape(req_count, drafts, head_size)
    score_scale = 1.0 / math.sqrt(head_size)
    cache_scores = (
        jnp.einsum("rjhd,rcd->rjhc", query_blocks, cache_keys, preferred_element_type=jnp.float32)
        * score_scale
    )
    draft_scores = (
        jnp.einsum("rjhd,rid->rjhi", query_blocks, draft_keys, preferred_element_type=jnp.float32)
        * score_scale
    )
    slots = jnp.arange(context_len, dtype=jnp.int32)
    cache_live = slots[None, :] < cache_len[:, None]
    cache_scores = jnp.where(cache_live[:, None, None, :], cache_scores, -jnp.inf)
    positions = jnp.arange(drafts, dtype=jnp.int32)
    causal = positions[None, :] <= positions[:, None]
    draft_live = causal[None, :, :] & (positions[None, None, :] < draft_len[:, None, None])
    draft_scores = jnp.where(draft_live[:, :, None, :], draft_scores, -jnp.inf)
    row_max = jnp.maximum(jnp.max(cache_scores, axis=-1), jnp.max(draft_scores, axis=-1))
    cache_probs = jnp.exp(cache_scores - row_max[..., None])
    draft_probs = jnp.exp(draft_scores - row_max[..., None])
    denominator = jnp.sum(cache_probs, axis=-1) + jnp.sum(draft_probs, axis=-1)
    context = jnp.einsum(
        "rjhc,rcd->rjhd",
        cache_probs.astype(jnp.bfloat16),
        cache_values,
        preferred_element_type=jnp.float32,
    )
    context = context + jnp.einsum(
        "rjhi,rid->rjhd",
        draft_probs.astype(jnp.bfloat16),
        draft_values,
        preferred_element_type=jnp.float32,
    )
    context = context / denominator[..., None]
    gate_open = jax.nn.sigmoid(out_gate.astype(jnp.float32)).reshape(
        req_count, drafts, head_count, head_size
    )
    row_live = (positions[None, :] < draft_len[:, None]).astype(jnp.float32)
    attended = context * gate_open * row_live[:, :, None, None]
    return attended.reshape(row_count, head_count * head_size).astype(jnp.bfloat16)


def plane_of(rep_count, wide_count):
    return 2 if rep_count == 1 and wide_count % 4 == 0 else 1


class Place:
    def __init__(self, side, wide_count):
        self.side, self.levels = side, wide_count // (side * side)
        wide = lax.axis_index("wide")
        self.core = lax.axis_index("narrow")
        self.z = wide // (side * side)
        self.y = (wide // side) % side
        self.x = wide % side
        c = self.core
        if side == 2:
            flip_y, flip_x = 1 - 2 * self.y, 1 - 2 * self.x
            self.y2, self.x2 = self.y + c * flip_y, self.x + (1 - c) * flip_x
            self.y3, self.x3 = self.y + (1 - c) * flip_y, self.x + c * flip_x
            self.y4, self.x4 = self.y + flip_y, self.x + flip_x

    def chip(self, z, kind):
        y, x = {
            1: (self.y, self.x),
            2: (getattr(self, "y2", 0), getattr(self, "x2", 0)),
            3: (getattr(self, "y3", 0), getattr(self, "x3", 0)),
            4: (getattr(self, "y4", 0), getattr(self, "x4", 0)),
        }[kind]
        return (z * self.side + y) * self.side + x

    def device(self, chip):
        return {"wide": chip, "narrow": self.core}

    def partner(self):
        return {"wide": self.chip(self.z, 1), "narrow": 1 - self.core}

    def greet(self):
        barrier = pltpu.get_barrier_semaphore()
        pl.semaphore_signal(barrier, inc=1, device_id=self.partner(), device_id_type=MESH)
        count = 1
        if self.side == 2:
            for kind in (2, 3):
                pl.semaphore_signal(
                    barrier,
                    inc=1,
                    device_id=self.device(self.chip(self.z, kind)),
                    device_id_type=MESH,
                )
            count = 3
        has_up, has_down = self.z < self.levels - 1, self.z > 0

        @pl.when(has_up)
        def _():
            pl.semaphore_signal(
                barrier, inc=1, device_id=self.device(self.chip(self.z + 1, 1)), device_id_type=MESH
            )

        @pl.when(has_down)
        def _():
            pl.semaphore_signal(
                barrier, inc=1, device_id=self.device(self.chip(self.z - 1, 1)), device_id_type=MESH
            )

        ends = has_up.astype(jnp.int32) + has_down.astype(jnp.int32)
        pl.semaphore_wait(barrier, count + ends)


def norm_rows(at, chunk, projected, hidden, gain, residual, rows_ref, theirs, meet):
    count = hidden.shape[0]
    swap = pltpu.make_async_remote_copy(
        src_ref=projected.at[1 - at.core],
        dst_ref=theirs,
        send_sem=meet.at[0],
        recv_sem=meet.at[1],
        device_id=at.partner(),
        device_id_type=MESH,
    )
    swap.start()
    swap.wait()

    @pl.loop(0, count, step=chunk)
    def _(row):
        part = pl.ds(pl.multiple_of(row, chunk), chunk)
        total = hidden[part, :].astype(jnp.float32) + (projected[at.core, part, :] + theirs[part, :])
        residual[part, :] = total
        spread = jnp.mean(total * total, axis=-1, keepdims=True)
        rows_ref[part, : total.shape[1]] = (total * lax.rsqrt(spread + 1e-06) * gain[...]).astype(rows_ref.dtype)


def layer_kernel(
    side, wide_count, chunk, slots, projected, hidden, gain, weights, gate_hbm, up_hbm, down_hbm,
    out, rows_all, terms, residual, theirs, gate_w, up_w, down_w, triangle, pick, pick_t, scale, picked, act,
    near, third, second, flow, meet, loads, g_sends, g_recvs, s_sends, s_recvs,
):
    at = Place(side, wide_count)
    z, levels, core = at.z, at.levels, at.core
    count, width = hidden.shape
    chips = side * side
    kinds = (4, 3, 2, 1) if side == 2 else (1,)
    group = 2 * chips
    experts = 2 * wide_count
    expert = at.chip(z, 1) * 2 + core
    fetch = [
        pltpu.make_async_copy(source.at[0], target, loads.at[i])
        for i, (source, target) in enumerate(((gate_hbm, gate_w), (up_hbm, up_w), (down_hbm, down_w)))
    ]
    for copy in fetch:
        copy.start()
    at.greet()
    own = rows_all.at[expert]
    norm_rows(at, chunk, projected, hidden, gain, residual, own, theirs, meet)
    own[:, width:] = weights[...]

    def carry(chip, block_core, lane, target):
        block = rows_all.at[chip * 2 + block_core]
        return pltpu.make_async_remote_copy(
            src_ref=block,
            dst_ref=block,
            send_sem=g_sends.at[chip, lane],
            recv_sem=g_recvs.at[chip * 2 + block_core],
            device_id=target,
            device_id_type=MESH,
        )

    def above():
        return at.device(at.chip(z + 1, 1))

    def below():
        return at.device(at.chip(z - 1, 1))

    def visit(distance, kind):
        for sign in (1, -1):
            level = z + sign * distance
            present = (distance >= 0) & (level >= 0) & (level < levels)
            if sign < 0:
                present = present & (distance > 0)

            @pl.when(present)
            def _():
                chip = at.chip(level, kind)
                if kind == 1:

                    @pl.when(distance > 0)
                    def _():
                        carry(chip, core, 4, at.partner()).wait_recv()

                    go_up = z < levels - 1
                    go_down = z > 0
                    if sign > 0:
                        go_up = go_up & (distance == 0)
                    else:
                        go_down = go_down & (distance == 0)

                    @pl.when(go_up)
                    def _():
                        carry(chip, core, 0, above()).start()

                    @pl.when(go_down)
                    def _():
                        carry(chip, core, 1, below()).start()

                    if side == 2:
                        carry(chip, core, 2, at.device(at.chip(z, 2))).start()
                else:
                    carry(chip, core, 4, at.partner()).wait_recv()
                if side == 2 and kind in (1, 2):
                    carry(chip, core, 3, at.device(at.chip(z, 3))).start()
                carry(chip, core, 4, at.partner()).start()

    def level_of(turn):
        low, high = z, levels - 1 - z
        less = (low < high).astype(jnp.int32)
        span = low * less + high * (1 - less)
        paired = (turn <= 2 * span).astype(jnp.int32)
        distance = paired * ((turn + 1) // 2) + (1 - paired) * (turn - span)
        sign = paired * (2 * (turn % 2) - 1) + (1 - paired) * (2 * less - 1)
        return z + sign * distance

    many = group * count
    tile = 512

    row = lax.broadcasted_iota(jnp.int32, (many, many), 0)
    other = lax.broadcasted_iota(jnp.int32, (many, many), 1)
    triangle[...] = ((other < row) & (other // count == row // count)).astype(jnp.float32).astype(jnp.bfloat16)

    def compute(level):
        base = level * group
        table = rows_all[pl.ds(base, group), :, width:].reshape(many, weights.shape[1])
        lane = lax.broadcasted_iota(jnp.int32, table.shape, 1)
        mine = jnp.where((lane == expert) | (lane == experts + expert), table.astype(jnp.float32), 0.0)
        mine = jnp.sum(mine, axis=1, keepdims=True)
        live = mine > 0.0
        flags = jnp.broadcast_to(live.astype(jnp.float32), (many, 128)).astype(jnp.bfloat16)
        order = jnp.dot(triangle[...], flags, preferred_element_type=jnp.float32)[:, :1]
        start = (lax.broadcasted_iota(jnp.int32, (many, 1), 0) // count * slots).astype(jnp.float32)
        seat = lax.broadcasted_iota(jnp.int32, (many, group * slots), 1).astype(jnp.float32)
        chosen = live & (seat == order + start)
        chosen = chosen.astype(jnp.float32)
        pick[...] = chosen.astype(jnp.bfloat16)
        pick_t[...] = chosen.T.astype(jnp.bfloat16)
        scale[...] = mine

        @pl.loop(0, width, step=tile)
        def _(column):
            part = pl.ds(pl.multiple_of(column, tile), tile)
            rows = rows_all[pl.ds(base, group), :, part].reshape(many, tile)
            picked[:, part] = jnp.dot(
                pick_t[...], rows, preferred_element_type=jnp.float32
            ).astype(jnp.bfloat16)

        gate_proj = jnp.dot(picked[...], gate_w[...], preferred_element_type=jnp.float32)
        up_proj = jnp.dot(picked[...], up_w[...], preferred_element_type=jnp.float32)
        act[...] = (gate_proj / (1.0 + jnp.exp(-gate_proj)) * up_proj).astype(jnp.bfloat16)

        @pl.loop(0, width, step=tile)
        def _(column):
            part = pl.ds(pl.multiple_of(column, tile), tile)
            produced = jnp.dot(act[...], down_w[:, part], preferred_element_type=jnp.float32)
            back = jnp.dot(pick[...], produced.astype(jnp.bfloat16), preferred_element_type=jnp.float32)
            sums = (back * scale[...]).astype(jnp.bfloat16)
            terms[pl.ds(base, group), :, part] = sums.reshape(group, count, tile)

    def copy_of(source, target, index, lane, chip, device):
        return pltpu.make_async_remote_copy(
            src_ref=source,
            dst_ref=target.at[index],
            send_sem=s_sends.at[lane, chip],
            recv_sem=s_recvs.at[lane, chip],
            device_id=device,
            device_id_type=MESH,
        )

    def to_partner(chip, block_core):
        return copy_of(terms.at[chip * 2 + block_core], near, chip, 0, chip, at.partner())

    def hop(kind, chip, level):
        held = terms.at[chip * 2 + core]
        if kind in (3, 4):
            return copy_of(held, third, chip, 1, chip, at.device(at.chip(z, 3)))
        return copy_of(held, second, level, 2, chip, at.device(at.chip(z, 2)))

    def rise(chip, level):
        return copy_of(terms.at[chip * 2 + core], flow, level, 3, chip, above())

    def fall(chip, level):
        ends = (level == z - 1).astype(jnp.int32)
        slot = level * (1 - ends) + levels * ends
        return copy_of(terms.at[chip * 2 + core], flow, slot, 4, chip, below())

    def fallen(chip):
        return copy_of(terms.at[chip * 2 + core], flow, levels, 4, chip, below())

    def add(chip, extra, last=False):
        @pl.loop(0, count, step=chunk)
        def _(row):
            part = pl.ds(pl.multiple_of(row, chunk), chunk)
            total = terms[chip * 2 + core, part, :].astype(jnp.float32)
            for ref, index in extra:
                total = total + ref[index, part, :].astype(jnp.float32)
            if last:
                out[part, :] = (residual[part, :] + total).astype(out.dtype)
            else:
                terms[chip * 2 + core, part, :] = total.astype(terms.dtype)

    def received(level, kind):
        chip = at.chip(level, kind)
        to_partner(chip, core).wait_recv()
        extra = [(near, chip)]
        if side == 2 and kind in (1, 2):
            hop(3, chip, level).wait_recv()
            extra.append((third, chip))
        if side == 2 and kind == 1:
            hop(2, chip, level).wait_recv()
            extra.append((second, level))
        return chip, extra

    def pass_on(level, kind):
        chip, extra = received(level, kind)
        add(chip, extra)
        hop(kind, chip, level).start()

    def first_along(level):
        @pl.when((z == 0) & (level > z))
        def _():
            chip, extra = received(level, 1)
            add(chip, extra)
            rise(chip, level).start()

        @pl.when((z == levels - 1) & (level < z))
        def _():
            chip, extra = received(level, 1)
            add(chip, extra)
            fall(chip, level).start()

    delay = 2 if side == 2 else 0

    @pl.loop(0, levels + delay)
    def _(step):
        visit(step, 1)
        if side == 2:
            visit(step - 1, 2)
            visit(step - 1, 3)
            visit(step - 2, 4)
        turn = step - delay

        @pl.when((turn >= 0) & (turn < levels))
        def _():
            level = level_of(turn)
            for kind in kinds:
                carry(at.chip(level, kind), 1 - core, 4, at.partner()).wait_recv()

            @pl.when(turn == 0)
            def _():
                for copy in fetch:
                    copy.wait()

            compute(level)
            for kind in kinds:
                to_partner(at.chip(level, kind), 1 - core).start()

    def last_along(level):
        first_along(level)

        @pl.when((z > 0) & (level > z))
        def _():
            chip, extra = received(level, 1)
            rise(chip, level).wait_recv()
            add(chip, extra + [(flow, level)])
            rise(chip, level).start()

        @pl.when((z < levels - 1) & (level < z))
        def _():
            chip, extra = received(level, 1)
            fall(chip, level).wait_recv()
            add(chip, extra + [(flow, level)])
            fall(chip, level).start()

    lag = 1 if side == 2 else 0

    @pl.loop(0, levels + 2 * lag)
    def _(step):
        if side == 2:

            @pl.when(step < levels)
            def _():
                level = level_of(levels - 1 - step)
                pass_on(level, 4)
                pass_on(level, 3)

            @pl.when((step >= lag) & (step < levels + lag))
            def _():
                pass_on(level_of(levels - 1 + lag - step), 2)

        @pl.when((step >= 2 * lag) & (step < levels + 2 * lag - 1))
        def _():
            last_along(level_of(levels - 1 + 2 * lag - step))

    chip, extra = received(z, 1)

    @pl.when(z > 0)
    def _():
        rise(chip, z).wait_recv()

    @pl.when(z < levels - 1)
    def _():
        fallen(chip).wait_recv()

    @pl.when((z > 0) & (z < levels - 1))
    def _():
        add(chip, extra + [(flow, z), (flow, levels)], last=True)

    @pl.when((z > 0) & (z == levels - 1))
    def _():
        add(chip, extra + [(flow, z)], last=True)

    @pl.when((z == 0) & (z < levels - 1))
    def _():
        add(chip, extra + [(flow, levels)], last=True)

    if levels == 1:
        add(chip, extra, last=True)

    @pl.loop(0, levels)
    def _(level):
        for kind in kinds:
            chip = at.chip(level, kind)
            carry(chip, core, 4, at.partner()).wait_send()
            if side == 2 and kind in (1, 2):
                carry(chip, core, 3, at.partner()).wait_send()
            to_partner(chip, 1 - core).wait_send()
            if kind != 1:
                hop(kind, chip, level).wait_send()
            else:
                if side == 2:
                    carry(chip, core, 2, at.partner()).wait_send()

                @pl.when((z < levels - 1) & (level <= z))
                def _():
                    carry(chip, core, 0, at.partner()).wait_send()

                @pl.when((z > 0) & (level >= z))
                def _():
                    carry(chip, core, 1, at.partner()).wait_send()

                @pl.when(level > z)
                def _():
                    rise(chip, level).wait_send()

                @pl.when(level < z)
                def _():
                    fall(chip, level).wait_send()


def run_layer(projected, hidden, gain, weights, w_gate, w_up, w_down, slots, side):
    wide_count = lax.axis_size("wide")
    blocks, chips = 2 * wide_count, side * side
    levels = wide_count // chips
    rows, width = hidden.shape
    block, half = (rows, width), jnp.bfloat16
    inner = w_gate.shape[2]
    seats, many = 2 * chips * slots, 2 * chips * rows
    lateral = wide_count if side == 2 else 1
    return pl.pallas_call(
        functools.partial(layer_kernel, side, wide_count, 16, slots),
        out_shape=jax.ShapeDtypeStruct(block, half),
        in_specs=[pl.BlockSpec(memory_space=pltpu.VMEM)] * 4
        + [pl.BlockSpec(memory_space=pl.ANY)] * 3,
        out_specs=pl.BlockSpec(memory_space=pltpu.VMEM),
        scratch_shapes=[
            pltpu.VMEM((blocks, rows, width + weights.shape[1]), half),
            pltpu.VMEM((blocks,) + block, half),
            pltpu.VMEM(block, jnp.float32),
            pltpu.VMEM(block, jnp.float32),
            pltpu.VMEM((width, inner), half),
            pltpu.VMEM((width, inner), half),
            pltpu.VMEM((inner, width), half),
            pltpu.VMEM((many, many), half),
            pltpu.VMEM((many, seats), half),
            pltpu.VMEM((seats, many), half),
            pltpu.VMEM((many, 1), jnp.float32),
            pltpu.VMEM((seats, width), half),
            pltpu.VMEM((seats, inner), half),
            pltpu.VMEM((wide_count,) + block, half),
            pltpu.VMEM((lateral,) + block, half),
            pltpu.VMEM((levels if side == 2 else 1,) + block, half),
            pltpu.VMEM((levels + 1,) + block, half),
            pltpu.SemaphoreType.DMA((2,)),
            pltpu.SemaphoreType.DMA((3,)),
            pltpu.SemaphoreType.DMA((wide_count, 5)),
            pltpu.SemaphoreType.DMA((blocks,)),
            pltpu.SemaphoreType.DMA((5, wide_count)),
            pltpu.SemaphoreType.DMA((5, wide_count)),
        ],
        compiler_params=pltpu.CompilerParams(
            collective_id=0, has_side_effects=True, vmem_limit_bytes=67043328
        ),
        name="run_layer",
    )(projected, hidden, gain, weights, w_gate, w_up, w_down)


END_PLAN = (
    ("t", 0), ("m1", 4), ("q2", 0), ("m1", 5), ("m1", 8), ("m1", 6), ("m2", 0), ("m2", 1), ("m2", 4), ("qh", 0),
    ("m2", 2), ("m3", 1), ("m2", 5), ("m1", 12), ("q", 4), ("m2", 6), ("q", 5), ("m2", 8), ("m1", 9), ("m2", 12),
    ("m3", 0), ("t", 1), ("m1", 13), ("m4", 1), ("q", 6), ("q", 7), ("m1", 14), ("m2", 9), ("m4", 0), ("m1", 10),
    ("co", 1), ("t", 3), ("m2", 13), ("m2", 14), ("cw", 1), ("q", 12), ("nw", 1), ("q", 13), ("sq", 5), ("m3", 3),
    ("m4", 3), ("sq", 7), ("m3", 2), ("q", 14), ("q", 8), ("q", 15), ("m2", 10), ("sq", 4), ("sq", 6), ("s1", 1),
    ("t", 2), ("co", 3), ("m4", 2), ("cw", 3), ("nw", 3), ("sq", 12), ("q", 9), ("q", 10), ("q", 11), ("sq", 14),
    ("s2", 4), ("s1", 3), ("sq", 13), ("s2", 6), ("sq", 15), ("co", 2), ("cw", 2), ("nw", 2), ("s2", 13), ("sq", 11),
    ("sq", 8), ("s1", 2), ("s2", 12), ("sq", 10), ("co", 0), ("sq", 9), ("s3", 13), ("s2", 14), ("cw", 0), ("s2", 8),
    ("s2", 9), ("nw", 0), ("s2", 5), ("s3", 12), ("s3", 14), ("s2", 10), ("s1", 0), ("s3", 8), ("s3", 9), ("s3", 10),
    ("s3", 4), ("s3", 5), ("sq", 0), ("s3", 6), ("s2", 2), ("s2", 1), ("s2q", 0), ("s2", 0), ("s3q", 0), ("s3", 1),
    ("s3", 2), ("s3", 0),
)
MIDDLE_PLAN = (
    ("q2", 0), ("m1", 8), ("m1", 4), ("t", 0), ("m1", 9), ("m2", 0), ("m2", 1), ("m1", 5), ("t", 2), ("m2", 2),
    ("m1", 10), ("m1", 12), ("qh", 0), ("m2", 8), ("m2", 9), ("q", 8), ("m1", 13), ("m2", 10), ("m2", 4), ("m1", 14),
    ("q", 9), ("m2", 12), ("m1", 6), ("t", 3), ("m4", 0), ("q", 10), ("q", 4), ("m3", 0), ("q", 12), ("q", 11),
    ("co", 0), ("m3", 2), ("q", 13), ("m2", 13), ("q", 14), ("cw", 0), ("nw", 0), ("m4", 2), ("m2", 14), ("q", 15),
    ("t", 1), ("s1", 0), ("m3", 3), ("m2", 5), ("m2", 6), ("co", 2), ("m4", 3), ("q", 5), ("q", 6), ("cw", 2),
    ("q", 7), ("co", 3), ("nw", 2), ("s1", 2), ("m3", 1), ("m4", 1), ("cw", 3), ("nw", 3), ("s1", 3), ("co", 1),
    ("sq", 12), ("cw", 1), ("sq", 13), ("nw", 1), ("s2", 9), ("s1", 1), ("sq", 14), ("sq", 15), ("sq", 7), ("s2", 12),
    ("sq", 8), ("s2", 8), ("sq", 9), ("sq", 4), ("s2", 13), ("s2", 1), ("s2", 10), ("s2", 14), ("sq", 10), ("s2", 4),
    ("s2", 0), ("sq", 6), ("s2", 5), ("sq", 11), ("sq", 5), ("s3", 13), ("s3", 12), ("s3", 14), ("s2", 6), ("sq", 0),
    ("s3", 9), ("s3", 4), ("s3", 8), ("s3", 5), ("s2", 2), ("s2q", 0), ("s3", 10), ("s3", 6), ("s3", 1), ("s3", 0),
    ("s3q", 0), ("s3", 2),
)


class Grid:
    def __init__(self, levels):
        wide = lax.axis_index("wide")
        self.levels, self.core = levels, lax.axis_index("narrow")
        self.z, self.p = wide // 4, wide % 4
        y, x = self.p // 2, self.p % 2
        along_x, along_y = self.p + 1 - 2 * x, self.p + 2 - 4 * y
        c = self.core
        self.a = (1 - c) * along_x + c * along_y
        self.b = c * along_x + (1 - c) * along_y
        self.d = 3 - self.p
        self.has_up, self.has_down = self.z < levels - 1, self.z > 0

    def at(self, level, column):
        return {"wide": level * 4 + column, "narrow": self.core}

    def partner(self):
        return {"wide": self.z * 4 + self.p, "narrow": 1 - self.core}

    def up(self):
        return self.at(self.z + 1, self.p)

    def down(self):
        return self.at(self.z - 1, self.p)

    def greet(self):
        barrier = pltpu.get_barrier_semaphore()

        def hello(device):
            pl.semaphore_signal(barrier, inc=1, device_id=device, device_id_type=MESH)

        hello(self.partner())
        hello(self.at(self.z, self.a))
        hello(self.at(self.z, self.b))
        pl.when(self.has_up)(lambda: hello(self.up()))
        pl.when(self.has_down)(lambda: hello(self.down()))

    def greeted(self):
        ends = self.has_up.astype(jnp.int32) + self.has_down.astype(jnp.int32)
        pl.semaphore_wait(pltpu.get_barrier_semaphore(), 3 + ends)

    def level_of(self, turn):
        low, high = self.z, self.levels - 1 - self.z
        less = (low < high).astype(jnp.int32)
        span = low * less + high * (1 - less)
        paired = (turn <= 2 * span).astype(jnp.int32)
        distance = paired * ((turn + 1) // 2) + (1 - paired) * (turn - span)
        toward = 2 * less - 1
        sign = paired * (2 * (turn % 2) - 1) * toward + (1 - paired) * toward
        return self.z + sign * distance


def fast_kernel(
    levels, draft_len, cache_len, gain, ids, ratios, hidden_hbm, query_hbm, open_hbm, kv_hbm, keys_hbm, values_hbm,
    out_hbm, gate_hbm, up_hbm, down_hbm,
    out, rows_all, terms, near, from_b, from_a, from_b_q, from_a_q, flow_m, flow_q, tables, scale,
    hidden, query, opened, kv, keys, values, out_w, gate_w, up_w, down_w, attended, projected, theirs, residual, act,
    loads, meet, meet_in, t_sends, t_recvs, g_sends, g_recvs, s_sends, s_recvs,
):
    g = Grid(levels)
    z, p, core = g.z, g.p, g.core
    half = jnp.bfloat16
    count, width = hidden.shape
    quarter = count // 4
    main = count - quarter
    tail = 4 * main
    lot = 4 * count
    experts = 8 * levels
    expert = (z * 4 + p) * 2 + core
    tile = projected.shape[3]
    reqs, context_len, head_size = keys.shape
    drafts = query.shape[0] // reqs
    heads = query.shape[1] // head_size
    other = 1 - core

    pairs = (
        (query_hbm, query), (kv_hbm, kv), (keys_hbm, keys), (values_hbm, values), (open_hbm, opened),
        (out_hbm, out_w), (hidden_hbm, hidden), (gate_hbm.at[0], gate_w), (up_hbm.at[0], up_w), (down_hbm.at[0], down_w),
    )
    fetch = [pltpu.make_async_copy(source, target, loads.at[i]) for i, (source, target) in enumerate(pairs)]
    for copy in fetch:
        copy.start()

    g.greet()

    name = lax.broadcasted_iota(jnp.int32, (experts, count), 0)
    weight = jnp.zeros((experts, count), jnp.float32)
    for k in range(ids.shape[0]):
        weight = weight + jnp.where(ids[k : k + 1, :] == name, ratios[k : k + 1, :], 0.0)
    high = weight.astype(half).astype(jnp.float32)
    both = jnp.concatenate([high, weight - high] * 2, axis=0)
    both = jnp.concatenate([both, both], axis=1).T
    lane = lax.broadcasted_iota(jnp.int32, tables.shape[3:], 1)
    tables[z, core, p] = jnp.where(lane < 2 * experts, both[: count // 2], both[count // 2 : count]).astype(half)

    def send(source, target, send_sem, recv_sem, device):
        return pltpu.make_async_remote_copy(
            src_ref=source, dst_ref=target, send_sem=send_sem, recv_sem=recv_sem, device_id=device, device_id_type=MESH
        )

    def table(source, index, recv_index, device):
        return send(source, source, t_sends.at[index], t_recvs.at[recv_index], device)

    def table_near(index, column):
        return table(tables.at[z, core, column], index, index, g.at(z, (g.a, g.b, g.b)[index]))

    def table_far(way, level):
        device = (g.up, g.down, g.partner)[way]()
        return table(tables.at[level, core], 3 + way * levels + level, 3 + (way // 2) * levels + level, device)

    def table_over(level, lane_core):
        return table(tables.at[level, lane_core], 3 + 2 * levels + level, 3 + levels + level, g.partner())

    def attend(first, last):
        for r in range(first, last):
            mine = slice(r * drafts, (r + 1) * drafts)
            q = jnp.concatenate([query[mine, h * head_size : (h + 1) * head_size] for h in range(heads)], axis=0)
            contract = (((1,), (1,)), ((), ()))
            s = lax.dot_general(q, keys[r], contract, preferred_element_type=jnp.float32) * (1.0 / math.sqrt(head_size))
            sd = lax.dot_general(q, kv[0], contract, preferred_element_type=jnp.float32) * (1.0 / math.sqrt(head_size))
            slot = lax.broadcasted_iota(jnp.int32, s.shape, 1)
            column = lax.broadcasted_iota(jnp.int32, sd.shape, 1) - r * drafts
            row = lax.broadcasted_iota(jnp.int32, sd.shape, 0) % drafts
            s = jnp.where(slot < cache_len[r], s, -jnp.inf)
            sd = jnp.where((column >= 0) & (column <= row) & (column < draft_len[r]), sd, -jnp.inf)
            top = jnp.maximum(jnp.max(s, axis=1, keepdims=True), jnp.max(sd, axis=1, keepdims=True))
            probs, probs_d = jnp.exp(s - top), jnp.exp(sd - top)
            total = jnp.sum(probs, axis=1, keepdims=True) + jnp.sum(probs_d, axis=1, keepdims=True)
            context = jnp.dot(probs.astype(half), values[r], preferred_element_type=jnp.float32)
            context = context + jnp.dot(probs_d.astype(half), kv[1], preferred_element_type=jnp.float32)
            context = context / total
            live = lax.broadcasted_iota(jnp.int32, (drafts, head_size), 0) < draft_len[r]
            for h in range(heads):
                part = slice(h * head_size, (h + 1) * head_size)
                shut = 1.0 + jnp.exp(-opened[mine, part].astype(jnp.float32))
                value = context[h * drafts : (h + 1) * drafts] / shut
                attended[mine, part] = jnp.where(live, value, 0.0).astype(half)

    for i in range(5):
        fetch[i].wait()
    attend(0, reqs)
    fetch[5].wait()
    g.greeted()
    table_near(0, p).start()
    table_near(1, p).start()

    def swap(i):
        return send(projected.at[i, other], theirs.at[i], meet.at[i], meet_in.at[i], g.partner())

    tiles = width // tile
    for i in range(tiles):
        product = jnp.dot(attended[...], out_w[:, i * tile : (i + 1) * tile], preferred_element_type=jnp.float32)
        projected[i] = product.reshape(2, count, tile)
        swap(i).start()
    fetch[6].wait()
    table_near(0, g.a).wait_recv()
    table_near(2, g.a).start()
    for i in range(tiles):
        swap(i).wait_recv()

    thirds = main // 16

    def m_rows(column):
        return pl.ds(pl.multiple_of(column * main, 16), main)

    def m_part(column, i):
        return pl.ds(pl.multiple_of(column * main + i * 16, 16), 16)

    def q_rows(column):
        return pl.ds(pl.multiple_of(tail + column * quarter, 16), quarter)

    q_all = pl.ds(tail, count)
    UP, DOWN, A, B, OVER = range(5)
    from_a_slot, from_b_slot, q_slot, over_slot = thirds, 2 * thirds, 2 * thirds + 2, 2 * thirds + 6

    def target(way):
        return (g.up, g.down, lambda: g.at(z, g.a), lambda: g.at(z, g.b), g.partner)[way]()

    def carry(ref, way, level, slot):
        return send(ref, ref, g_sends.at[way, level], g_recvs.at[level, slot], target(way))

    def m_piece(way, level, column, i, slot):
        return carry(rows_all.at[level, core, m_part(column, i)], way, level, slot)

    def m_z(way, level, i):
        return m_piece(way, level, p, i, i)

    def m_a(level, i):
        return m_piece(A, level, p, i, from_a_slot + i)

    def m_b(level, i, passed):
        return m_piece(B, level, g.a if passed else p, i, from_b_slot + passed)

    def m_b_all(level, column, passed):
        return carry(rows_all.at[level, core, m_rows(column)], B, level, from_b_slot + passed)

    def m_over(level, column):
        return carry(rows_all.at[level, core, m_rows(column)], OVER, level, over_slot)

    def q_block(way, column, slot):
        return carry(rows_all.at[z, core, q_rows(column)], way, z, q_slot + slot)

    def q_piece(way, level, i):
        return carry(rows_all.at[level, core, q_rows(i)], way, level, q_slot + i)

    def q_over(level):
        return carry(rows_all.at[level, core, q_all], OVER, level, over_slot)

    def over_all(level, lane_core):
        return carry(rows_all.at[level, lane_core], OVER, level, over_slot)

    def along(level, copy):
        @pl.when(g.has_up & (level <= z))
        def _():
            copy(UP)

        @pl.when(g.has_down & (level >= z))
        def _():
            copy(DOWN)

    def norm(i):
        part = slice(i * 16, (i + 1) * 16)
        total = hidden[part, :].astype(jnp.float32) + jnp.concatenate(
            [projected[t, core, part, :] + theirs[t, part, :] for t in range(tiles)], axis=1
        )
        residual[part, :] = total
        spread = jnp.mean(total * total, axis=-1, keepdims=True)
        normed = (total * lax.rsqrt(spread + 1e-06) * gain[...]).astype(half)
        if i * 16 >= main:
            place = tail + p * quarter + i * 16 - main
        else:
            place = p * main + i * 16
        rows_all[z, core, pl.ds(pl.multiple_of(place, 16), 16), :] = normed

    for i in range(main // 16, count // 16):
        norm(i)
    q_block(A, p, 0).start()
    q_block(B, p, 1).start()
    for i in range(thirds):
        norm(i)
        along(z, lambda way: m_z(way, z, i).start())
        m_a(z, i).start()
        m_b(z, i, 0).start()
    m_over(z, p).start()

    def compute(level, lane_core):
        for column in range(4):
            block = tables[level, lane_core, column].astype(jnp.float32)
            for part in range(2):
                first = 2 * part * experts + expert
                mine = jnp.where((lane == first) | (lane == first + experts), block, 0.0)
                mine = jnp.broadcast_to(jnp.sum(mine, axis=1, keepdims=True), block.shape)
                for i in range(count // 2 // 16):
                    row = part * (count // 2) + i * 16
                    place = column * main + row if row < main else tail + column * quarter + row - main
                    scale[place : place + 16, :] = mine[i * 16 : (i + 1) * 16]
        x = rows_all.at[level, lane_core]
        gate_proj = jnp.dot(x[...], gate_w[...], preferred_element_type=jnp.float32)
        up_proj = jnp.dot(x[...], up_w[...], preferred_element_type=jnp.float32)
        act[...] = (gate_proj / (1.0 + jnp.exp(-gate_proj)) * up_proj).astype(half)

        produced = jnp.dot(act[...], down_w[...], preferred_element_type=jnp.float32)
        terms[level, lane_core] = (produced * scale[:, 0:1]).astype(half)

    plane_slot, q_in = 1 + thirds, 1 + 2 * thirds

    def term(ref, target_ref, way, slot, level, device):
        return send(ref, target_ref, s_sends.at[way, level], s_recvs.at[level, slot], device)

    def term_over(level, lane_core):
        return term(terms.at[level, lane_core], near.at[level], 0, 0, level, g.partner())

    def piece(i):
        return pl.ds(pl.multiple_of(i * 16, 16), 16)

    def b_term(level, column, slot, i):
        source = terms.at[level, core, m_part(column, i)]
        counted = 1 + i if slot else plane_slot + i
        return term(source, from_b.at[level, slot, piece(i)], 1, counted, level, g.at(z, g.b))

    def a_term(level, column, i):
        source = terms.at[level, core, m_part(column, i)]
        return term(source, from_a.at[level, piece(i)], 2, plane_slot + i, level, g.at(z, g.a))

    def flow_m_term(way, level, i, device):
        source = terms.at[level, core, m_part(p, i)]
        return term(source, flow_m.at[way, level, piece(i)], 3, plane_slot + i, level, device)

    def flow_q_term(way, level, i, device):
        source = terms.at[level, core, q_rows(i)]
        return term(source, flow_q.at[way, level, piece(i)], 3, q_in + i, level, device)

    def b_term_q(column, slot):
        source = terms.at[z, core, q_rows(column)]
        return term(source, from_b_q.at[slot], 1, q_in + 4 + slot, z, g.at(z, g.b))

    def a_term_q(column):
        return term(terms.at[z, core, q_rows(column)], from_a_q, 2, q_in + 4, z, g.at(z, g.a))

    def arrived(level, slot, rows):
        ref = near.at[level, pl.ds(0, rows)]
        term(ref, ref, 0, slot, level, g.partner()).wait_recv()

    def left(sems, way, level, rows):
        ref = rows_all.at[level, core, pl.ds(0, rows)]
        send(ref, ref, sems.at[way, level], s_recvs.at[level, 0], g.partner()).wait_send()

    def table_first(turn, mid):
        level = g.level_of(turn)
        if turn == 0:
            table_near(1, g.b).wait_recv()
            table_near(2, g.d).wait_recv()
        else:
            table_far(0, level).wait_recv()
        along(level, lambda way: table_far(way, level).start())
        table_over(level, core).start()

    def q_second(turn, mid):
        q_block(A, g.a, 0).wait_recv()
        q_block(B, g.a, 2).start()

    def q_home(turn, mid):
        q_block(B, g.b, 1).wait_recv()
        q_block(B, g.d, 2).wait_recv()

        @pl.loop(0, 4)
        def _(i):
            along(z, lambda way: q_piece(way, z, i).start())

        q_over(z).start()

    def q_next(turn, mid):
        turn, i = turn // 4, turn % 4
        level = g.level_of(turn)
        q_piece(UP, level, i).wait_recv()
        along(level, lambda way: q_piece(way, level, i).start())
        if i == 3:
            q_over(level).start()

    def m_first(turn, mid):
        turn, i = turn // 4, turn % 4
        level = g.level_of(turn)
        m_z(UP, level, i).wait_recv()
        along(level, lambda way: m_z(way, level, i).start())
        m_a(level, i).start()
        m_b(level, i, 0).start()
        if i == thirds - 1:
            m_over(level, p).start()

    def m_second(turn, mid):
        turn, i = turn // 4, turn % 4
        level = g.level_of(turn)
        m_a(level, i).wait_recv()
        m_b(level, i, 1).start()
        if i == thirds - 1:
            m_over(level, g.a).start()

    def m_third(turn, mid):
        level = g.level_of(turn)
        m_b_all(level, g.b, 0).wait_recv()
        m_over(level, g.b).start()

    def m_fourth(turn, mid):
        level = g.level_of(turn)
        m_b_all(level, g.d, 1).wait_recv()
        m_over(level, g.d).start()

    def rows_over(turn, mid):
        level = g.level_of(turn)
        over_all(level, other).wait_recv()
        table_over(level, other).wait_recv()

    def near_in(turn, mid):
        term_over(g.level_of(turn), other).wait_recv()

    def add(level, start, extra, last=None):
        part = pl.ds(pl.multiple_of(start, 16), 16)

        @pl.loop(0, width, step=512)
        def _(column):
            part_of = pl.ds(pl.multiple_of(column, 512), 512)
            total = terms[level, core, part, part_of].astype(jnp.float32) + near[level, part, part_of].astype(jnp.float32)
            for ref in extra:
                total = total + ref[:, part_of].astype(jnp.float32)
            if last is None:
                terms[level, core, part, part_of] = total.astype(half)
            else:
                rest = slice(last, last + 16)
                out[rest, part_of] = (residual[rest, part_of] + total).astype(half)

    def m_start(column, i):
        return column * main + i * 16

    def q_start(column):
        return tail + column * quarter

    def rising(level):
        return (level > z).astype(jnp.int32)

    def ways_in(turn, mid):
        if turn == 0:
            return (0, 1) if mid else ((z == 0).astype(jnp.int32),)
        return (1 - rising(g.level_of(turn)),) if mid else ()

    def stage_1(turn, mid):
        level = g.level_of(turn)

        @pl.loop(0, thirds)
        def _(i):
            add(level, m_start(g.d, i), [])
            b_term(level, g.d, 1, i).start()
            add(level, m_start(g.b, i), [])
            b_term(level, g.b, 0, i).start()

    def stage_2(turn, mid):
        turn, i = turn // 4, turn % 4
        level = g.level_of(turn)
        b_term(level, g.d, 1, i).wait_recv()
        add(level, m_start(g.a, i), [from_b.at[level, 1, piece(i)]])
        a_term(level, g.a, i).start()

    def stage_q(turn, mid):
        turn, i = turn // 4, turn % 4
        level = g.level_of(turn)
        ways = ways_in(turn, mid)

        def arrive(i):
            if ways:
                arrived(level, q_in + i, 16 * len(ways))

        def sum_of(i):
            add(level, q_start(i), [flow_q.at[way, level, piece(i)] for way in ways])

        if turn == 0:

            @pl.loop(0, 4)
            def _(column):
                arrive(column)
                pl.when((column != p) & (column != g.a))(lambda: sum_of(column))

            b_term_q(g.d, 1).start()
            b_term_q(g.b, 0).start()
        else:
            arrive(i)
            sum_of(i)
            pl.when(level > z)(lambda: flow_q_term(0, level, i, g.up()).start())
            pl.when(level < z)(lambda: flow_q_term(1, level, i, g.down()).start())

    def stage_2q(turn, mid):
        b_term_q(g.d, 1).wait_recv()
        add(z, q_start(g.a), [from_b_q.at[1]] + [flow_q.at[way, z, piece(g.a)] for way in ways_in(0, mid)])
        a_term_q(g.a).start()

    def stage_3q(turn, mid):
        arrived(z, q_in + 4, 2 * quarter)
        add(z, q_start(p), [from_b_q.at[0], from_a_q] + [flow_q.at[way, z, piece(p)] for way in ways_in(0, mid)], last=main)

    def stage_3(turn, mid):
        turn, i = turn // 4, turn % 4
        level = g.level_of(turn)
        ways = ways_in(turn, mid)
        arrived(level, plane_slot + i, 16 * (2 + len(ways)))
        extra = [from_b.at[level, 0, piece(i)], from_a.at[level, piece(i)]]
        extra = extra + [flow_m.at[way, level, piece(i)] for way in ways]
        if turn == 0:
            add(level, m_start(p, i), extra, last=i * 16)
        else:
            add(level, m_start(p, i), extra)
            pl.when(level > z)(lambda: flow_m_term(0, level, i, g.up()).start())
            pl.when(level < z)(lambda: flow_m_term(1, level, i, g.down()).start())

    steps = {
        "t": table_first, "q2": q_second, "qh": q_home, "q": q_next, "m1": m_first, "m2": m_second, "m3": m_third,
        "m4": m_fourth, "co": rows_over, "nw": near_in, "s1": stage_1, "sq": stage_q, "s2": stage_2, "s2q": stage_2q,
        "s3": stage_3, "s3q": stage_3q,
    }
    at_end = (z == 0) | (z == levels - 1)
    is_end = at_end.astype(jnp.int32)

    def parts_of(plan):
        parts, pieces = [[]], []
        for entry in plan:
            if entry[0] == "co":
                parts[-1].append(entry)
            if entry[0] in ("co", "cw"):
                pieces.append(2 * entry[1] + (entry[0] == "cw"))
                parts.append([])
            else:
                parts[-1].append(entry)
        return parts, pieces

    def play(part, mid):
        def run():
            for name, turn in part:
                steps[name](turn, mid)

        return run

    (end_parts, end_pieces), (middle_parts, middle_pieces) = parts_of(END_PLAN), parts_of(MIDDLE_PLAN)

    @pl.loop(0, len(end_parts))
    def _(step):
        piece = 0
        for i in range(len(end_parts)):
            pl.when((step == i) & at_end)(play(end_parts[i], False))
            pl.when((step == i) & jnp.logical_not(at_end))(play(middle_parts[i], True))
            if i < len(end_pieces):
                chosen = is_end * end_pieces[i] + (1 - is_end) * middle_pieces[i]
                piece = piece + (step == i).astype(jnp.int32) * chosen

        @pl.when(step == 0)
        def _():
            for copy in fetch[7:]:
                copy.wait()

        @pl.when(step < len(end_pieces))
        def _():
            level = g.level_of(piece // 2)
            mine = piece % 2
            compute(level, mine * core + (1 - mine) * other)

            @pl.when(mine == 0)
            def _():
                term_over(level, other).start()

    for i in range(3):
        table_near(i, p).wait_send()
    for i in range(tiles):
        swap(i).wait_send()
    @pl.loop(0, levels)
    def _(level):
        table_over(level, core).wait_send()
        along(level, lambda way: table_far(way, level).wait_send())
        along(level, lambda way: left(g_sends, way, level, main + count))
        left(g_sends, OVER, level, lot)
        left(s_sends, 0, level, lot)

        @pl.when(level == z)
        def _():
            for sems, a_way, b_way in ((g_sends, A, B), (s_sends, 2, 1)):
                left(sems, a_way, level, count)
                left(sems, b_way, level, 2 * count)

        @pl.when(level != z)
        def _():
            for sems, a_way, b_way in ((g_sends, A, B), (s_sends, 2, 1)):
                left(sems, a_way, level, main)
                left(sems, b_way, level, 2 * main)
            left(s_sends, 3, level, main + count)


def run_fast(
    hidden, queries, out_gate, draft_kv, cache_keys, cache_values, draft_len, cache_len, o_weight, norm_gain,
    route_ids, route_weights, w_gate, w_up, w_down,
):
    levels = lax.axis_size("wide") // 4
    count, width = hidden.shape
    quarter = count // 4
    main, lot = count - quarter, 4 * count
    inner = w_gate.shape[2]
    half = jnp.bfloat16
    tile = 512
    lanes = max(128, 32 * levels)
    dma = pltpu.SemaphoreType.DMA
    vmem, smem, hbm = (pl.BlockSpec(memory_space=space) for space in (pltpu.VMEM, pltpu.SMEM, pl.ANY))
    return pl.pallas_call(
        functools.partial(fast_kernel, levels),
        out_shape=pltpu.VMEM((count, width), half),
        in_specs=[smem] * 2 + [vmem] * 3 + [hbm] * 10,
        out_specs=vmem,
        scratch_shapes=[
            pltpu.VMEM((levels, 2, lot, width), half),
            pltpu.VMEM((levels, 2, lot, width), half),
            pltpu.VMEM((levels, lot, width), half),
            pltpu.VMEM((levels, 2, main, width), half),
            pltpu.VMEM((levels, main, width), half),
            pltpu.VMEM((2, quarter, width), half),
            pltpu.VMEM((quarter, width), half),
            pltpu.VMEM((2, levels, main, width), half),
            pltpu.VMEM((2, levels, count, width), half),
            pltpu.VMEM((levels, 2, 4, count // 2, lanes), half),
            pltpu.VMEM((lot, lanes), jnp.float32),
            pltpu.VMEM(hidden.shape, half),
            pltpu.VMEM(queries.shape, half),
            pltpu.VMEM(out_gate.shape, half),
            pltpu.VMEM(draft_kv.shape, half),
            pltpu.VMEM(cache_keys.shape, half),
            pltpu.VMEM(cache_values.shape, half),
            pltpu.VMEM(o_weight.shape, half),
            pltpu.VMEM((width, inner), half),
            pltpu.VMEM((width, inner), half),
            pltpu.VMEM((inner, width), half),
            pltpu.VMEM(queries.shape, half),
            pltpu.VMEM((width // tile, 2, count, tile), jnp.float32),
            pltpu.VMEM((width // tile, count, tile), jnp.float32),
            pltpu.VMEM((count, width), jnp.float32),
            pltpu.VMEM((lot, inner), half),
            dma((10,)),
            dma((width // tile,)),
            dma((width // tile,)),
            dma((3 + 3 * levels,)),
            dma((3 + 2 * levels,)),
            dma((5, levels)),
            dma((levels, 7 + main // 8)),
            dma((4, levels)),
            dma((levels, 7 + main // 8)),
        ],
        compiler_params=pltpu.CompilerParams(
            collective_id=0, has_side_effects=True, vmem_limit_bytes=66500000
        ),
        name="run_layer",
    )(
        draft_len, cache_len, norm_gain[None, :], route_ids.T, route_weights.T, hidden, queries, out_gate, draft_kv,
        cache_keys, cache_values, o_weight, w_gate, w_up, w_down,
    )


def fits_fast(hidden_in, queries, cache_keys):
    levels = lax.axis_size("wide") // 4
    drafts = queries.shape[0] // cache_keys.shape[0]
    return (
        plane_of(lax.axis_size("rep"), lax.axis_size("wide")) == 2
        and hidden_in.shape[0] * 2 == 128
        and hidden_in.shape[1] % 512 == 0
        and drafts % 16 == 0
        and cache_keys.shape[0] % 2 == 0
        and levels * 32 == 128
    )


def on_device(
    hidden_in,
    queries,
    out_gate,
    draft_kv,
    cache_keys,
    cache_values,
    draft_len,
    cache_len,
    o_weight,
    norm_gain,
    route_ids,
    route_weights,
    w_gate,
    w_up,
    w_down,
):
    if fits_fast(hidden_in, queries, cache_keys):
        return run_fast(
            hidden_in, queries, out_gate, draft_kv, cache_keys, cache_values, draft_len, cache_len, o_weight,
            norm_gain, route_ids, route_weights, w_gate, w_up, w_down,
        )
    attended = attention_rows(
        queries, out_gate, draft_kv, cache_keys, cache_values, draft_len, cache_len
    )
    own_rows = hidden_in.shape[0]
    width = hidden_in.shape[1]
    projected = jnp.dot(attended, o_weight, preferred_element_type=jnp.float32)
    projected = projected.reshape(2, own_rows, width)
    top_count = route_ids.shape[1]
    experts = lax.axis_size("wide") * lax.axis_size("narrow")
    capacity = max(2, min(own_rows, (3 * own_rows * top_count + 2 * experts - 1) // (2 * experts)))
    slots = -(-capacity // 16) * 16
    chosen = route_ids[:, :, None] == jnp.arange(experts, dtype=jnp.int32)[None, None, :]
    dense = jnp.sum(jnp.where(chosen, route_weights[:, :, None], 0.0), axis=1)
    coarse = lax.reduce_precision(dense, 8, 7)
    weights = jnp.concatenate([coarse, dense - coarse], axis=1).astype(jnp.bfloat16)
    weights = jnp.pad(weights, ((0, 0), (0, -weights.shape[1] % 128)))
    side = plane_of(lax.axis_size("rep"), lax.axis_size("wide"))
    return run_layer(
        projected, hidden_in, norm_gain[None, :], weights, w_gate, w_up, w_down, slots, side
    )


def solution(mesh):
    placed = (
        P(("rep", "wide", "narrow"), None),
        P(("rep", "wide"), "narrow"),
        P(("rep", "wide"), "narrow"),
        P(None, ("rep", "wide"), None),
        P(("rep", "wide"), None, None),
        P(("rep", "wide"), None, None),
        P(("rep", "wide")),
        P(("rep", "wide")),
        P("narrow", None),
        P(),
        P(("rep", "wide", "narrow"), None),
        P(("rep", "wide", "narrow"), None),
        P(("wide", "narrow"), None, None),
        P(("wide", "narrow"), None, None),
        P(("wide", "narrow"), None, None),
    )
    return jax.shard_map(
        on_device,
        mesh=mesh,
        in_specs=placed,
        out_specs=P(("rep", "wide", "narrow"), None),
        check_vma=False,
    )
```

```python
import math

import functools

import jax
import jax.numpy as jnp
from jax import lax
from jax.experimental import pallas as pl
from jax.experimental.pallas import tpu as pltpu
from jax.sharding import PartitionSpec as P

MESH = pl.DeviceIdType.MESH


def attention_rows(queries, out_gate, draft_kv, cache_keys, cache_values, draft_len, cache_len):
    req_count, context_len, head_size = cache_keys.shape
    row_count = queries.shape[0]
    drafts = row_count // req_count
    head_count = queries.shape[1] // head_size
    query_blocks = queries.reshape(req_count, drafts, head_count, head_size)
    draft_keys = draft_kv[0].reshape(req_count, drafts, head_size)
    draft_values = draft_kv[1].reshape(req_count, drafts, head_size)
    score_scale = 1.0 / math.sqrt(head_size)
    cache_scores = (
        jnp.einsum("rjhd,rcd->rjhc", query_blocks, cache_keys, preferred_element_type=jnp.float32)
        * score_scale
    )
    draft_scores = (
        jnp.einsum("rjhd,rid->rjhi", query_blocks, draft_keys, preferred_element_type=jnp.float32)
        * score_scale
    )
    slots = jnp.arange(context_len, dtype=jnp.int32)
    cache_live = slots[None, :] < cache_len[:, None]
    cache_scores = jnp.where(cache_live[:, None, None, :], cache_scores, -jnp.inf)
    positions = jnp.arange(drafts, dtype=jnp.int32)
    causal = positions[None, :] <= positions[:, None]
    draft_live = causal[None, :, :] & (positions[None, None, :] < draft_len[:, None, None])
    draft_scores = jnp.where(draft_live[:, :, None, :], draft_scores, -jnp.inf)
    row_max = jnp.maximum(jnp.max(cache_scores, axis=-1), jnp.max(draft_scores, axis=-1))
    cache_probs = jnp.exp(cache_scores - row_max[..., None])
    draft_probs = jnp.exp(draft_scores - row_max[..., None])
    denominator = jnp.sum(cache_probs, axis=-1) + jnp.sum(draft_probs, axis=-1)
    context = jnp.einsum(
        "rjhc,rcd->rjhd",
        cache_probs.astype(jnp.bfloat16),
        cache_values,
        preferred_element_type=jnp.float32,
    )
    context = context + jnp.einsum(
        "rjhi,rid->rjhd",
        draft_probs.astype(jnp.bfloat16),
        draft_values,
        preferred_element_type=jnp.float32,
    )
    context = context / denominator[..., None]
    gate_open = jax.nn.sigmoid(out_gate.astype(jnp.float32)).reshape(
        req_count, drafts, head_count, head_size
    )
    row_live = (positions[None, :] < draft_len[:, None]).astype(jnp.float32)
    attended = context * gate_open * row_live[:, :, None, None]
    return attended.reshape(row_count, head_count * head_size).astype(jnp.bfloat16)


def plane_of(rep_count, wide_count):
    return 2 if rep_count == 1 and wide_count % 4 == 0 else 1


class Place:
    def __init__(self, side, wide_count):
        self.side, self.levels = side, wide_count // (side * side)
        wide = lax.axis_index("wide")
        self.core = lax.axis_index("narrow")
        self.z = wide // (side * side)
        self.y = (wide // side) % side
        self.x = wide % side
        c = self.core
        if side == 2:
            flip_y, flip_x = 1 - 2 * self.y, 1 - 2 * self.x
            self.y2, self.x2 = self.y + c * flip_y, self.x + (1 - c) * flip_x
            self.y3, self.x3 = self.y + (1 - c) * flip_y, self.x + c * flip_x
            self.y4, self.x4 = self.y + flip_y, self.x + flip_x

    def chip(self, z, kind):
        y, x = {
            1: (self.y, self.x),
            2: (getattr(self, "y2", 0), getattr(self, "x2", 0)),
            3: (getattr(self, "y3", 0), getattr(self, "x3", 0)),
            4: (getattr(self, "y4", 0), getattr(self, "x4", 0)),
        }[kind]
        return (z * self.side + y) * self.side + x

    def device(self, chip):
        return {"wide": chip, "narrow": self.core}

    def partner(self):
        return {"wide": self.chip(self.z, 1), "narrow": 1 - self.core}

    def greet(self):
        barrier = pltpu.get_barrier_semaphore()
        pl.semaphore_signal(barrier, inc=1, device_id=self.partner(), device_id_type=MESH)
        count = 1
        if self.side == 2:
            for kind in (2, 3):
                pl.semaphore_signal(
                    barrier,
                    inc=1,
                    device_id=self.device(self.chip(self.z, kind)),
                    device_id_type=MESH,
                )
            count = 3
        has_up, has_down = self.z < self.levels - 1, self.z > 0

        @pl.when(has_up)
        def _():
            pl.semaphore_signal(
                barrier, inc=1, device_id=self.device(self.chip(self.z + 1, 1)), device_id_type=MESH
            )

        @pl.when(has_down)
        def _():
            pl.semaphore_signal(
                barrier, inc=1, device_id=self.device(self.chip(self.z - 1, 1)), device_id_type=MESH
            )

        ends = has_up.astype(jnp.int32) + has_down.astype(jnp.int32)
        pl.semaphore_wait(barrier, count + ends)


def norm_rows(at, chunk, projected, hidden, gain, residual, rows_ref, theirs, meet):
    count = hidden.shape[0]
    swap = pltpu.make_async_remote_copy(
        src_ref=projected.at[1 - at.core],
        dst_ref=theirs,
        send_sem=meet.at[0],
        recv_sem=meet.at[1],
        device_id=at.partner(),
        device_id_type=MESH,
    )
    swap.start()
    swap.wait()

    @pl.loop(0, count, step=chunk)
    def _(row):
        part = pl.ds(pl.multiple_of(row, chunk), chunk)
        total = hidden[part, :].astype(jnp.float32) + (projected[at.core, part, :] + theirs[part, :])
        residual[part, :] = total
        spread = jnp.mean(total * total, axis=-1, keepdims=True)
        rows_ref[part, : total.shape[1]] = (total * lax.rsqrt(spread + 1e-06) * gain[...]).astype(rows_ref.dtype)


def layer_kernel(
    side, wide_count, chunk, slots, projected, hidden, gain, weights, gate_hbm, up_hbm, down_hbm,
    out, rows_all, terms, residual, theirs, gate_w, up_w, down_w, triangle, pick, pick_t, scale, picked, act,
    near, third, second, flow, meet, loads, g_sends, g_recvs, s_sends, s_recvs,
):
    at = Place(side, wide_count)
    z, levels, core = at.z, at.levels, at.core
    count, width = hidden.shape
    chips = side * side
    kinds = (4, 3, 2, 1) if side == 2 else (1,)
    group = 2 * chips
    experts = 2 * wide_count
    expert = at.chip(z, 1) * 2 + core
    fetch = [
        pltpu.make_async_copy(source.at[0], target, loads.at[i])
        for i, (source, target) in enumerate(((gate_hbm, gate_w), (up_hbm, up_w), (down_hbm, down_w)))
    ]
    for copy in fetch:
        copy.start()
    at.greet()
    own = rows_all.at[expert]
    norm_rows(at, chunk, projected, hidden, gain, residual, own, theirs, meet)
    own[:, width:] = weights[...]

    def carry(chip, block_core, lane, target):
        block = rows_all.at[chip * 2 + block_core]
        return pltpu.make_async_remote_copy(
            src_ref=block,
            dst_ref=block,
            send_sem=g_sends.at[chip, lane],
            recv_sem=g_recvs.at[chip * 2 + block_core],
            device_id=target,
            device_id_type=MESH,
        )

    def above():
        return at.device(at.chip(z + 1, 1))

    def below():
        return at.device(at.chip(z - 1, 1))

    def visit(distance, kind):
        for sign in (1, -1):
            level = z + sign * distance
            present = (distance >= 0) & (level >= 0) & (level < levels)
            if sign < 0:
                present = present & (distance > 0)

            @pl.when(present)
            def _():
                chip = at.chip(level, kind)
                if kind == 1:

                    @pl.when(distance > 0)
                    def _():
                        carry(chip, core, 4, at.partner()).wait_recv()

                    go_up = z < levels - 1
                    go_down = z > 0
                    if sign > 0:
                        go_up = go_up & (distance == 0)
                    else:
                        go_down = go_down & (distance == 0)

                    @pl.when(go_up)
                    def _():
                        carry(chip, core, 0, above()).start()

                    @pl.when(go_down)
                    def _():
                        carry(chip, core, 1, below()).start()

                    if side == 2:
                        carry(chip, core, 2, at.device(at.chip(z, 2))).start()
                else:
                    carry(chip, core, 4, at.partner()).wait_recv()
                if side == 2 and kind in (1, 2):
                    carry(chip, core, 3, at.device(at.chip(z, 3))).start()
                carry(chip, core, 4, at.partner()).start()

    def level_of(turn):
        low, high = z, levels - 1 - z
        less = (low < high).astype(jnp.int32)
        span = low * less + high * (1 - less)
        paired = (turn <= 2 * span).astype(jnp.int32)
        distance = paired * ((turn + 1) // 2) + (1 - paired) * (turn - span)
        sign = paired * (2 * (turn % 2) - 1) + (1 - paired) * (2 * less - 1)
        return z + sign * distance

    many = group * count
    tile = 512

    row = lax.broadcasted_iota(jnp.int32, (many, many), 0)
    other = lax.broadcasted_iota(jnp.int32, (many, many), 1)
    triangle[...] = ((other < row) & (other // count == row // count)).astype(jnp.float32).astype(jnp.bfloat16)

    def compute(level):
        base = level * group
        table = rows_all[pl.ds(base, group), :, width:].reshape(many, weights.shape[1])
        lane = lax.broadcasted_iota(jnp.int32, table.shape, 1)
        mine = jnp.where((lane == expert) | (lane == experts + expert), table.astype(jnp.float32), 0.0)
        mine = jnp.sum(mine, axis=1, keepdims=True)
        live = mine > 0.0
        flags = jnp.broadcast_to(live.astype(jnp.float32), (many, 128)).astype(jnp.bfloat16)
        order = jnp.dot(triangle[...], flags, preferred_element_type=jnp.float32)[:, :1]
        start = (lax.broadcasted_iota(jnp.int32, (many, 1), 0) // count * slots).astype(jnp.float32)
        seat = lax.broadcasted_iota(jnp.int32, (many, group * slots), 1).astype(jnp.float32)
        chosen = live & (seat == order + start)
        chosen = chosen.astype(jnp.float32)
        pick[...] = chosen.astype(jnp.bfloat16)
        pick_t[...] = chosen.T.astype(jnp.bfloat16)
        scale[...] = mine

        @pl.loop(0, width, step=tile)
        def _(column):
            part = pl.ds(pl.multiple_of(column, tile), tile)
            rows = rows_all[pl.ds(base, group), :, part].reshape(many, tile)
            picked[:, part] = jnp.dot(
                pick_t[...], rows, preferred_element_type=jnp.float32
            ).astype(jnp.bfloat16)

        gate_proj = jnp.dot(picked[...], gate_w[...], preferred_element_type=jnp.float32)
        up_proj = jnp.dot(picked[...], up_w[...], preferred_element_type=jnp.float32)
        act[...] = (gate_proj / (1.0 + jnp.exp(-gate_proj)) * up_proj).astype(jnp.bfloat16)

        @pl.loop(0, width, step=tile)
        def _(column):
            part = pl.ds(pl.multiple_of(column, tile), tile)
            produced = jnp.dot(act[...], down_w[:, part], preferred_element_type=jnp.float32)
            back = jnp.dot(pick[...], produced.astype(jnp.bfloat16), preferred_element_type=jnp.float32)
            sums = (back * scale[...]).astype(jnp.bfloat16)
            terms[pl.ds(base, group), :, part] = sums.reshape(group, count, tile)

    def copy_of(source, target, index, lane, chip, device):
        return pltpu.make_async_remote_copy(
            src_ref=source,
            dst_ref=target.at[index],
            send_sem=s_sends.at[lane, chip],
            recv_sem=s_recvs.at[lane, chip],
            device_id=device,
            device_id_type=MESH,
        )

    def to_partner(chip, block_core):
        return copy_of(terms.at[chip * 2 + block_core], near, chip, 0, chip, at.partner())

    def hop(kind, chip, level):
        held = terms.at[chip * 2 + core]
        if kind in (3, 4):
            return copy_of(held, third, chip, 1, chip, at.device(at.chip(z, 3)))
        return copy_of(held, second, level, 2, chip, at.device(at.chip(z, 2)))

    def rise(chip, level):
        return copy_of(terms.at[chip * 2 + core], flow, level, 3, chip, above())

    def fall(chip, level):
        ends = (level == z - 1).astype(jnp.int32)
        slot = level * (1 - ends) + levels * ends
        return copy_of(terms.at[chip * 2 + core], flow, slot, 4, chip, below())

    def fallen(chip):
        return copy_of(terms.at[chip * 2 + core], flow, levels, 4, chip, below())

    def add(chip, extra, last=False):
        @pl.loop(0, count, step=chunk)
        def _(row):
            part = pl.ds(pl.multiple_of(row, chunk), chunk)
            total = terms[chip * 2 + core, part, :].astype(jnp.float32)
            for ref, index in extra:
                total = total + ref[index, part, :].astype(jnp.float32)
            if last:
                out[part, :] = (residual[part, :] + total).astype(out.dtype)
            else:
                terms[chip * 2 + core, part, :] = total.astype(terms.dtype)

    def received(level, kind):
        chip = at.chip(level, kind)
        to_partner(chip, core).wait_recv()
        extra = [(near, chip)]
        if side == 2 and kind in (1, 2):
            hop(3, chip, level).wait_recv()
            extra.append((third, chip))
        if side == 2 and kind == 1:
            hop(2, chip, level).wait_recv()
            extra.append((second, level))
        return chip, extra

    def pass_on(level, kind):
        chip, extra = received(level, kind)
        add(chip, extra)
        hop(kind, chip, level).start()

    def first_along(level):
        @pl.when((z == 0) & (level > z))
        def _():
            chip, extra = received(level, 1)
            add(chip, extra)
            rise(chip, level).start()

        @pl.when((z == levels - 1) & (level < z))
        def _():
            chip, extra = received(level, 1)
            add(chip, extra)
            fall(chip, level).start()

    delay = 2 if side == 2 else 0

    @pl.loop(0, levels + delay)
    def _(step):
        visit(step, 1)
        if side == 2:
            visit(step - 1, 2)
            visit(step - 1, 3)
            visit(step - 2, 4)
        turn = step - delay

        @pl.when((turn >= 0) & (turn < levels))
        def _():
            level = level_of(turn)
            for kind in kinds:
                carry(at.chip(level, kind), 1 - core, 4, at.partner()).wait_recv()

            @pl.when(turn == 0)
            def _():
                for copy in fetch:
                    copy.wait()

            compute(level)
            for kind in kinds:
                to_partner(at.chip(level, kind), 1 - core).start()

    def last_along(level):
        first_along(level)

        @pl.when((z > 0) & (level > z))
        def _():
            chip, extra = received(level, 1)
            rise(chip, level).wait_recv()
            add(chip, extra + [(flow, level)])
            rise(chip, level).start()

        @pl.when((z < levels - 1) & (level < z))
        def _():
            chip, extra = received(level, 1)
            fall(chip, level).wait_recv()
            add(chip, extra + [(flow, level)])
            fall(chip, level).start()

    lag = 1 if side == 2 else 0

    @pl.loop(0, levels + 2 * lag)
    def _(step):
        if side == 2:

            @pl.when(step < levels)
            def _():
                level = level_of(levels - 1 - step)
                pass_on(level, 4)
                pass_on(level, 3)

            @pl.when((step >= lag) & (step < levels + lag))
            def _():
                pass_on(level_of(levels - 1 + lag - step), 2)

        @pl.when((step >= 2 * lag) & (step < levels + 2 * lag - 1))
        def _():
            last_along(level_of(levels - 1 + 2 * lag - step))

    chip, extra = received(z, 1)

    @pl.when(z > 0)
    def _():
        rise(chip, z).wait_recv()

    @pl.when(z < levels - 1)
    def _():
        fallen(chip).wait_recv()

    @pl.when((z > 0) & (z < levels - 1))
    def _():
        add(chip, extra + [(flow, z), (flow, levels)], last=True)

    @pl.when((z > 0) & (z == levels - 1))
    def _():
        add(chip, extra + [(flow, z)], last=True)

    @pl.when((z == 0) & (z < levels - 1))
    def _():
        add(chip, extra + [(flow, levels)], last=True)

    if levels == 1:
        add(chip, extra, last=True)

    @pl.loop(0, levels)
    def _(level):
        for kind in kinds:
            chip = at.chip(level, kind)
            carry(chip, core, 4, at.partner()).wait_send()
            if side == 2 and kind in (1, 2):
                carry(chip, core, 3, at.partner()).wait_send()
            to_partner(chip, 1 - core).wait_send()
            if kind != 1:
                hop(kind, chip, level).wait_send()
            else:
                if side == 2:
                    carry(chip, core, 2, at.partner()).wait_send()

                @pl.when((z < levels - 1) & (level <= z))
                def _():
                    carry(chip, core, 0, at.partner()).wait_send()

                @pl.when((z > 0) & (level >= z))
                def _():
                    carry(chip, core, 1, at.partner()).wait_send()

                @pl.when(level > z)
                def _():
                    rise(chip, level).wait_send()

                @pl.when(level < z)
                def _():
                    fall(chip, level).wait_send()


def run_layer(projected, hidden, gain, weights, w_gate, w_up, w_down, slots, side):
    wide_count = lax.axis_size("wide")
    blocks, chips = 2 * wide_count, side * side
    levels = wide_count // chips
    rows, width = hidden.shape
    block, half = (rows, width), jnp.bfloat16
    inner = w_gate.shape[2]
    seats, many = 2 * chips * slots, 2 * chips * rows
    lateral = wide_count if side == 2 else 1
    return pl.pallas_call(
        functools.partial(layer_kernel, side, wide_count, 16, slots),
        out_shape=jax.ShapeDtypeStruct(block, half),
        in_specs=[pl.BlockSpec(memory_space=pltpu.VMEM)] * 4
        + [pl.BlockSpec(memory_space=pl.ANY)] * 3,
        out_specs=pl.BlockSpec(memory_space=pltpu.VMEM),
        scratch_shapes=[
            pltpu.VMEM((blocks, rows, width + weights.shape[1]), half),
            pltpu.VMEM((blocks,) + block, half),
            pltpu.VMEM(block, jnp.float32),
            pltpu.VMEM(block, jnp.float32),
            pltpu.VMEM((width, inner), half),
            pltpu.VMEM((width, inner), half),
            pltpu.VMEM((inner, width), half),
            pltpu.VMEM((many, many), half),
            pltpu.VMEM((many, seats), half),
            pltpu.VMEM((seats, many), half),
            pltpu.VMEM((many, 1), jnp.float32),
            pltpu.VMEM((seats, width), half),
            pltpu.VMEM((seats, inner), half),
            pltpu.VMEM((wide_count,) + block, half),
            pltpu.VMEM((lateral,) + block, half),
            pltpu.VMEM((levels if side == 2 else 1,) + block, half),
            pltpu.VMEM((levels + 1,) + block, half),
            pltpu.SemaphoreType.DMA((2,)),
            pltpu.SemaphoreType.DMA((3,)),
            pltpu.SemaphoreType.DMA((wide_count, 5)),
            pltpu.SemaphoreType.DMA((blocks,)),
            pltpu.SemaphoreType.DMA((5, wide_count)),
            pltpu.SemaphoreType.DMA((5, wide_count)),
        ],
        compiler_params=pltpu.CompilerParams(
            collective_id=0, has_side_effects=True, vmem_limit_bytes=67043328
        ),
        name="run_layer",
    )(projected, hidden, gain, weights, w_gate, w_up, w_down)


END_PLAN = (
    ("t", 0), ("m1", 4), ("q2", 0), ("m1", 5), ("m1", 6), ("m2", 4), ("m1", 8), ("qh", 0), ("m2", 5), ("m2", 6),
    ("m1", 12), ("m2", 0), ("m1", 9), ("m3", 0), ("q", 4), ("m1", 13), ("t", 1), ("m2", 12), ("m2", 13), ("m4", 1),
    ("m3", 1), ("q", 5), ("m1", 14), ("q", 6), ("m2", 8), ("q", 7), ("m1", 10), ("co", 1), ("m2", 14), ("t", 3),
    ("cw", 1), ("nw", 1), ("sq", 5), ("m2", 9), ("m3", 2), ("q", 12), ("sq", 6), ("m2", 1), ("m3", 3), ("q", 13),
    ("q", 14), ("m4", 3), ("sq", 4), ("q", 15), ("m2", 10), ("s1", 1), ("sq", 7), ("co", 3), ("m2", 2), ("q", 8),
    ("q", 9), ("m4", 2), ("cw", 3), ("s2", 4), ("nw", 3), ("sq", 13), ("q", 10), ("q", 11), ("sq", 12), ("t", 2),
    ("s2", 5), ("s1", 3), ("sq", 14), ("sq", 15), ("co", 2), ("cw", 2), ("s2", 13), ("nw", 2), ("m4", 0), ("sq", 11),
    ("sq", 8), ("sq", 10), ("s2", 12), ("s1", 2), ("co", 0), ("s2", 14), ("sq", 9), ("cw", 0), ("s3", 13), ("s2", 8),
    ("s2", 6), ("s3", 12), ("nw", 0), ("s2", 9), ("s3", 14), ("s1", 0), ("s2", 10), ("s3", 8), ("s3", 9), ("s3", 10),
    ("s3", 5), ("s3", 4), ("sq", 0), ("s3", 6), ("s2", 2), ("s2", 1), ("s2", 0), ("s2q", 0), ("s3", 0), ("s3", 1),
    ("s3", 2), ("s3q", 0),
)
MIDDLE_PLAN = (
    ("q2", 0), ("m1", 8), ("m1", 4), ("m2", 0), ("m1", 9), ("m1", 5), ("t", 0), ("m2", 1), ("t", 2), ("m1", 12),
    ("m1", 10), ("m1", 13), ("m2", 2), ("qh", 0), ("m1", 14), ("m2", 12), ("q", 8), ("m1", 6), ("m3", 0), ("q", 9),
    ("q", 10), ("t", 3), ("q", 11), ("m2", 13), ("m2", 14), ("m2", 8), ("q", 12), ("q", 13), ("q", 14), ("m4", 0),
    ("m2", 4), ("q", 15), ("q", 4), ("co", 0), ("m2", 9), ("q", 5), ("q", 6), ("m3", 3), ("m4", 3), ("m2", 10),
    ("m2", 5), ("cw", 0), ("m3", 1), ("nw", 0), ("q", 7), ("s1", 0), ("t", 1), ("co", 3), ("m3", 2), ("m4", 2),
    ("m2", 6), ("cw", 3), ("nw", 3), ("s1", 3), ("co", 2), ("cw", 2), ("m4", 1), ("s2", 2), ("s2", 12), ("nw", 2),
    ("sq", 13), ("s2", 13), ("s1", 2), ("sq", 12), ("co", 1), ("sq", 14), ("s2", 14), ("sq", 15), ("cw", 1), ("nw", 1),
    ("sq", 7), ("sq", 8), ("s1", 1), ("sq", 4), ("s2", 9), ("sq", 10), ("sq", 6), ("sq", 9), ("sq", 5), ("s2", 8),
    ("s2", 4), ("s2", 10), ("sq", 11), ("s3", 13), ("s2", 5), ("s3", 12), ("s3", 14), ("s2", 6), ("s2", 1), ("sq", 0),
    ("s3", 9), ("s3", 4), ("s2", 0), ("s3", 8), ("s3", 5), ("s3", 10), ("s3", 6), ("s2q", 0), ("s3", 1), ("s3", 0),
    ("s3q", 0), ("s3", 2),
)


class Grid:
    def __init__(self, levels):
        wide = lax.axis_index("wide")
        self.levels, self.core = levels, lax.axis_index("narrow")
        self.z, self.p = wide // 4, wide % 4
        y, x = self.p // 2, self.p % 2
        along_x, along_y = self.p + 1 - 2 * x, self.p + 2 - 4 * y
        c = self.core
        self.a = (1 - c) * along_x + c * along_y
        self.b = c * along_x + (1 - c) * along_y
        self.d = 3 - self.p
        self.has_up, self.has_down = self.z < levels - 1, self.z > 0

    def at(self, level, column):
        return {"wide": level * 4 + column, "narrow": self.core}

    def partner(self):
        return {"wide": self.z * 4 + self.p, "narrow": 1 - self.core}

    def up(self):
        return self.at(self.z + 1, self.p)

    def down(self):
        return self.at(self.z - 1, self.p)

    def greet(self):
        barrier = pltpu.get_barrier_semaphore()

        def hello(device):
            pl.semaphore_signal(barrier, inc=1, device_id=device, device_id_type=MESH)

        hello(self.partner())
        hello(self.at(self.z, self.a))
        hello(self.at(self.z, self.b))
        pl.when(self.has_up)(lambda: hello(self.up()))
        pl.when(self.has_down)(lambda: hello(self.down()))

    def greeted(self):
        ends = self.has_up.astype(jnp.int32) + self.has_down.astype(jnp.int32)
        pl.semaphore_wait(pltpu.get_barrier_semaphore(), 3 + ends)

    def level_of(self, turn):
        low, high = self.z, self.levels - 1 - self.z
        less = (low < high).astype(jnp.int32)
        span = low * less + high * (1 - less)
        paired = (turn <= 2 * span).astype(jnp.int32)
        distance = paired * ((turn + 1) // 2) + (1 - paired) * (turn - span)
        toward = 2 * less - 1
        sign = paired * (2 * (turn % 2) - 1) * toward + (1 - paired) * toward
        return self.z + sign * distance


def fast_kernel(
    levels, draft_len, cache_len, gain, ids, ratios, hidden_hbm, query_hbm, open_hbm, kv_hbm, keys_hbm, values_hbm,
    out_hbm, gate_hbm, up_hbm, down_hbm,
    out, rows_all, terms, near, from_b, from_a, from_b_q, from_a_q, flow_m, flow_q, tables, scale,
    hidden, query, opened, kv, keys, values, out_w, gate_w, up_w, down_w, attended, projected, theirs, residual, act,
    loads, meet, meet_in, t_sends, t_recvs, g_sends, g_recvs, s_sends, s_recvs,
):
    g = Grid(levels)
    z, p, core = g.z, g.p, g.core
    half = jnp.bfloat16
    count, width = hidden.shape
    quarter = count // 4
    main = count - quarter
    tail = 4 * main
    lot = 4 * count
    experts = 8 * levels
    expert = (z * 4 + p) * 2 + core
    tile = projected.shape[3]
    reqs, context_len, head_size = keys.shape
    drafts = query.shape[0] // reqs
    heads = query.shape[1] // head_size
    other = 1 - core

    pairs = (
        (query_hbm, query), (kv_hbm, kv), (keys_hbm, keys), (values_hbm, values), (open_hbm, opened),
        (out_hbm, out_w), (hidden_hbm, hidden), (gate_hbm.at[0], gate_w), (up_hbm.at[0], up_w), (down_hbm.at[0], down_w),
    )
    fetch = [pltpu.make_async_copy(source, target, loads.at[i]) for i, (source, target) in enumerate(pairs)]
    for copy in fetch:
        copy.start()

    g.greet()

    name = lax.broadcasted_iota(jnp.int32, (experts, count), 0)
    weight = jnp.zeros((experts, count), jnp.float32)
    for k in range(ids.shape[0]):
        weight = weight + jnp.where(ids[k : k + 1, :] == name, ratios[k : k + 1, :], 0.0)
    high = weight.astype(half).astype(jnp.float32)
    both = jnp.concatenate([high, weight - high] * 2, axis=0)
    both = jnp.concatenate([both, both], axis=1).T
    lane = lax.broadcasted_iota(jnp.int32, tables.shape[3:], 1)
    tables[z, core, p] = jnp.where(lane < 2 * experts, both[: count // 2], both[count // 2 : count]).astype(half)

    def send(source, target, send_sem, recv_sem, device):
        return pltpu.make_async_remote_copy(
            src_ref=source, dst_ref=target, send_sem=send_sem, recv_sem=recv_sem, device_id=device, device_id_type=MESH
        )

    def table(source, index, recv_index, device):
        return send(source, source, t_sends.at[index], t_recvs.at[recv_index], device)

    def table_near(index, column):
        return table(tables.at[z, core, column], index, index, g.at(z, (g.a, g.b, g.b)[index]))

    def table_far(way, level):
        device = (g.up, g.down, g.partner)[way]()
        return table(tables.at[level, core], 3 + way * levels + level, 3 + (way // 2) * levels + level, device)

    def table_over(level, lane_core):
        return table(tables.at[level, lane_core], 3 + 2 * levels + level, 3 + levels + level, g.partner())

    def attend(first, last):
        for r in range(first, last):
            mine = slice(r * drafts, (r + 1) * drafts)
            q = jnp.concatenate([query[mine, h * head_size : (h + 1) * head_size] for h in range(heads)], axis=0)
            contract = (((1,), (1,)), ((), ()))
            s = lax.dot_general(q, keys[r], contract, preferred_element_type=jnp.float32) * (1.0 / math.sqrt(head_size))
            sd = lax.dot_general(q, kv[0], contract, preferred_element_type=jnp.float32) * (1.0 / math.sqrt(head_size))
            slot = lax.broadcasted_iota(jnp.int32, s.shape, 1)
            column = lax.broadcasted_iota(jnp.int32, sd.shape, 1) - r * drafts
            row = lax.broadcasted_iota(jnp.int32, sd.shape, 0) % drafts
            s = jnp.where(slot < cache_len[r], s, -jnp.inf)
            sd = jnp.where((column >= 0) & (column <= row) & (column < draft_len[r]), sd, -jnp.inf)
            top = jnp.maximum(jnp.max(s, axis=1, keepdims=True), jnp.max(sd, axis=1, keepdims=True))
            probs, probs_d = jnp.exp(s - top), jnp.exp(sd - top)
            total = jnp.sum(probs, axis=1, keepdims=True) + jnp.sum(probs_d, axis=1, keepdims=True)
            context = jnp.dot(probs.astype(half), values[r], preferred_element_type=jnp.float32)
            context = context + jnp.dot(probs_d.astype(half), kv[1], preferred_element_type=jnp.float32)
            context = context / total
            live = lax.broadcasted_iota(jnp.int32, (drafts, head_size), 0) < draft_len[r]
            for h in range(heads):
                part = slice(h * head_size, (h + 1) * head_size)
                shut = 1.0 + jnp.exp(-opened[mine, part].astype(jnp.float32))
                value = context[h * drafts : (h + 1) * drafts] / shut
                attended[mine, part] = jnp.where(live, value, 0.0).astype(half)

    for i in range(5):
        fetch[i].wait()
    attend(0, reqs)
    fetch[5].wait()
    g.greeted()
    table_near(0, p).start()
    table_near(1, p).start()

    def swap(i):
        return send(projected.at[i, other], theirs.at[i], meet.at[i], meet_in.at[i], g.partner())

    tiles = width // tile
    for i in range(tiles):
        product = jnp.dot(attended[...], out_w[:, i * tile : (i + 1) * tile], preferred_element_type=jnp.float32)
        projected[i] = product.reshape(2, count, tile)
        swap(i).start()
    fetch[6].wait()
    table_near(0, g.a).wait_recv()
    table_near(2, g.a).start()
    for i in range(tiles):
        swap(i).wait_recv()

    thirds = main // 16

    def m_rows(column):
        return pl.ds(pl.multiple_of(column * main, 16), main)

    def m_part(column, i):
        return pl.ds(pl.multiple_of(column * main + i * 16, 16), 16)

    def q_rows(column):
        return pl.ds(pl.multiple_of(tail + column * quarter, 16), quarter)

    q_all = pl.ds(tail, count)
    UP, DOWN, A, B, OVER = range(5)
    from_a_slot, from_b_slot, q_slot, over_slot = thirds, 2 * thirds, 2 * thirds + 2, 2 * thirds + 6

    def target(way):
        return (g.up, g.down, lambda: g.at(z, g.a), lambda: g.at(z, g.b), g.partner)[way]()

    def carry(ref, way, level, slot):
        return send(ref, ref, g_sends.at[way, level], g_recvs.at[level, slot], target(way))

    def m_piece(way, level, column, i, slot):
        return carry(rows_all.at[level, core, m_part(column, i)], way, level, slot)

    def m_z(way, level, i):
        return m_piece(way, level, p, i, i)

    def m_a(level, i):
        return m_piece(A, level, p, i, from_a_slot + i)

    def m_b(level, i, passed):
        return m_piece(B, level, g.a if passed else p, i, from_b_slot + passed)

    def m_b_all(level, column, passed):
        return carry(rows_all.at[level, core, m_rows(column)], B, level, from_b_slot + passed)

    def m_over(level, column):
        return carry(rows_all.at[level, core, m_rows(column)], OVER, level, over_slot)

    def q_block(way, column, slot):
        return carry(rows_all.at[z, core, q_rows(column)], way, z, q_slot + slot)

    def q_piece(way, level, i):
        return carry(rows_all.at[level, core, q_rows(i)], way, level, q_slot + i)

    def q_over(level):
        return carry(rows_all.at[level, core, q_all], OVER, level, over_slot)

    def over_all(level, lane_core):
        return carry(rows_all.at[level, lane_core], OVER, level, over_slot)

    def along(level, copy):
        @pl.when(g.has_up & (level <= z))
        def _():
            copy(UP)

        @pl.when(g.has_down & (level >= z))
        def _():
            copy(DOWN)

    def norm(i):
        part = slice(i * 16, (i + 1) * 16)
        total = hidden[part, :].astype(jnp.float32) + jnp.concatenate(
            [projected[t, core, part, :] + theirs[t, part, :] for t in range(tiles)], axis=1
        )
        residual[part, :] = total
        spread = jnp.mean(total * total, axis=-1, keepdims=True)
        normed = (total * lax.rsqrt(spread + 1e-06) * gain[...]).astype(half)
        if i * 16 >= main:
            place = tail + p * quarter + i * 16 - main
        else:
            place = p * main + i * 16
        rows_all[z, core, pl.ds(pl.multiple_of(place, 16), 16), :] = normed

    for i in range(main // 16, count // 16):
        norm(i)
    q_block(A, p, 0).start()
    q_block(B, p, 1).start()
    for i in range(thirds):
        norm(i)
        along(z, lambda way: m_z(way, z, i).start())
        m_a(z, i).start()
        m_b(z, i, 0).start()
    m_over(z, p).start()

    def compute(level, lane_core):
        for column in range(4):
            block = tables[level, lane_core, column].astype(jnp.float32)
            for part in range(2):
                first = 2 * part * experts + expert
                mine = jnp.where((lane == first) | (lane == first + experts), block, 0.0)
                mine = jnp.broadcast_to(jnp.sum(mine, axis=1, keepdims=True), block.shape)
                for i in range(count // 2 // 16):
                    row = part * (count // 2) + i * 16
                    place = column * main + row if row < main else tail + column * quarter + row - main
                    scale[place : place + 16, :] = mine[i * 16 : (i + 1) * 16]
        x = rows_all.at[level, lane_core]
        gate_proj = jnp.dot(x[...], gate_w[...], preferred_element_type=jnp.float32)
        up_proj = jnp.dot(x[...], up_w[...], preferred_element_type=jnp.float32)
        act[...] = (gate_proj / (1.0 + jnp.exp(-gate_proj)) * up_proj).astype(half)

        produced = jnp.dot(act[...], down_w[...], preferred_element_type=jnp.float32)
        terms[level, lane_core] = (produced * scale[:, 0:1]).astype(half)

    plane_slot, q_in = 1 + thirds, 1 + 2 * thirds

    def term(ref, target_ref, way, slot, level, device):
        return send(ref, target_ref, s_sends.at[way, level], s_recvs.at[level, slot], device)

    def term_over(level, lane_core):
        return term(terms.at[level, lane_core], near.at[level], 0, 0, level, g.partner())

    def piece(i):
        return pl.ds(pl.multiple_of(i * 16, 16), 16)

    def b_term(level, column, slot, i):
        source = terms.at[level, core, m_part(column, i)]
        counted = 1 + i if slot else plane_slot + i
        return term(source, from_b.at[level, slot, piece(i)], 1, counted, level, g.at(z, g.b))

    def a_term(level, column, i):
        source = terms.at[level, core, m_part(column, i)]
        return term(source, from_a.at[level, piece(i)], 2, plane_slot + i, level, g.at(z, g.a))

    def flow_m_term(way, level, i, device):
        source = terms.at[level, core, m_part(p, i)]
        return term(source, flow_m.at[way, level, piece(i)], 3, plane_slot + i, level, device)

    def flow_q_term(way, level, i, device):
        source = terms.at[level, core, q_rows(i)]
        return term(source, flow_q.at[way, level, piece(i)], 3, q_in + i, level, device)

    def b_term_q(column, slot):
        source = terms.at[z, core, q_rows(column)]
        return term(source, from_b_q.at[slot], 1, q_in + 4 + slot, z, g.at(z, g.b))

    def a_term_q(column):
        return term(terms.at[z, core, q_rows(column)], from_a_q, 2, q_in + 4, z, g.at(z, g.a))

    def arrived(level, slot, rows):
        ref = near.at[level, pl.ds(0, rows)]
        term(ref, ref, 0, slot, level, g.partner()).wait_recv()

    def left(sems, way, level, rows):
        ref = rows_all.at[level, core, pl.ds(0, rows)]
        send(ref, ref, sems.at[way, level], s_recvs.at[level, 0], g.partner()).wait_send()

    def table_first(turn, mid):
        level = g.level_of(turn)
        if turn == 0:
            table_near(1, g.b).wait_recv()
            table_near(2, g.d).wait_recv()
        else:
            table_far(0, level).wait_recv()
        along(level, lambda way: table_far(way, level).start())
        table_over(level, core).start()

    def q_second(turn, mid):
        q_block(A, g.a, 0).wait_recv()
        q_block(B, g.a, 2).start()

    def q_home(turn, mid):
        q_block(B, g.b, 1).wait_recv()
        q_block(B, g.d, 2).wait_recv()

        @pl.loop(0, 4)
        def _(i):
            along(z, lambda way: q_piece(way, z, i).start())

        q_over(z).start()

    def q_next(turn, mid):
        turn, i = turn // 4, turn % 4
        level = g.level_of(turn)
        q_piece(UP, level, i).wait_recv()
        along(level, lambda way: q_piece(way, level, i).start())
        if i == 3:
            q_over(level).start()

    def m_first(turn, mid):
        turn, i = turn // 4, turn % 4
        level = g.level_of(turn)
        m_z(UP, level, i).wait_recv()
        along(level, lambda way: m_z(way, level, i).start())
        m_a(level, i).start()
        m_b(level, i, 0).start()
        if i == thirds - 1:
            m_over(level, p).start()

    def m_second(turn, mid):
        turn, i = turn // 4, turn % 4
        level = g.level_of(turn)
        m_a(level, i).wait_recv()
        m_b(level, i, 1).start()
        if i == thirds - 1:
            m_over(level, g.a).start()

    def m_third(turn, mid):
        level = g.level_of(turn)
        m_b_all(level, g.b, 0).wait_recv()
        m_over(level, g.b).start()

    def m_fourth(turn, mid):
        level = g.level_of(turn)
        m_b_all(level, g.d, 1).wait_recv()
        m_over(level, g.d).start()

    def rows_over(turn, mid):
        level = g.level_of(turn)
        over_all(level, other).wait_recv()
        table_over(level, other).wait_recv()

    def near_in(turn, mid):
        term_over(g.level_of(turn), other).wait_recv()

    def add(level, start, extra, last=None):
        part = pl.ds(pl.multiple_of(start, 16), 16)

        @pl.loop(0, width, step=512)
        def _(column):
            part_of = pl.ds(pl.multiple_of(column, 512), 512)
            total = terms[level, core, part, part_of].astype(jnp.float32) + near[level, part, part_of].astype(jnp.float32)
            for ref in extra:
                total = total + ref[:, part_of].astype(jnp.float32)
            if last is None:
                terms[level, core, part, part_of] = total.astype(half)
            else:
                rest = slice(last, last + 16)
                out[rest, part_of] = (residual[rest, part_of] + total).astype(half)

    def m_start(column, i):
        return column * main + i * 16

    def q_start(column):
        return tail + column * quarter

    def rising(level):
        return (level > z).astype(jnp.int32)

    def ways_in(turn, mid):
        if turn == 0:
            return (0, 1) if mid else ((z == 0).astype(jnp.int32),)
        return (1 - rising(g.level_of(turn)),) if mid else ()

    def stage_1(turn, mid):
        level = g.level_of(turn)

        @pl.loop(0, thirds)
        def _(i):
            add(level, m_start(g.d, i), [])
            b_term(level, g.d, 1, i).start()
            add(level, m_start(g.b, i), [])
            b_term(level, g.b, 0, i).start()

    def stage_2(turn, mid):
        turn, i = turn // 4, turn % 4
        level = g.level_of(turn)
        b_term(level, g.d, 1, i).wait_recv()
        add(level, m_start(g.a, i), [from_b.at[level, 1, piece(i)]])
        a_term(level, g.a, i).start()

    def stage_q(turn, mid):
        turn, i = turn // 4, turn % 4
        level = g.level_of(turn)
        ways = ways_in(turn, mid)

        def arrive(i):
            if ways:
                arrived(level, q_in + i, 16 * len(ways))

        def sum_of(i):
            add(level, q_start(i), [flow_q.at[way, level, piece(i)] for way in ways])

        if turn == 0:

            @pl.loop(0, 4)
            def _(column):
                arrive(column)
                pl.when((column != p) & (column != g.a))(lambda: sum_of(column))

            b_term_q(g.d, 1).start()
            b_term_q(g.b, 0).start()
        else:
            arrive(i)
            sum_of(i)
            pl.when(level > z)(lambda: flow_q_term(0, level, i, g.up()).start())
            pl.when(level < z)(lambda: flow_q_term(1, level, i, g.down()).start())

    def stage_2q(turn, mid):
        b_term_q(g.d, 1).wait_recv()
        add(z, q_start(g.a), [from_b_q.at[1]] + [flow_q.at[way, z, piece(g.a)] for way in ways_in(0, mid)])
        a_term_q(g.a).start()

    def stage_3q(turn, mid):
        arrived(z, q_in + 4, 2 * quarter)
        add(z, q_start(p), [from_b_q.at[0], from_a_q] + [flow_q.at[way, z, piece(p)] for way in ways_in(0, mid)], last=main)

    def stage_3(turn, mid):
        turn, i = turn // 4, turn % 4
        level = g.level_of(turn)
        ways = ways_in(turn, mid)
        arrived(level, plane_slot + i, 16 * (2 + len(ways)))
        extra = [from_b.at[level, 0, piece(i)], from_a.at[level, piece(i)]]
        extra = extra + [flow_m.at[way, level, piece(i)] for way in ways]
        if turn == 0:
            add(level, m_start(p, i), extra, last=i * 16)
        else:
            add(level, m_start(p, i), extra)
            pl.when(level > z)(lambda: flow_m_term(0, level, i, g.up()).start())
            pl.when(level < z)(lambda: flow_m_term(1, level, i, g.down()).start())

    steps = {
        "t": table_first, "q2": q_second, "qh": q_home, "q": q_next, "m1": m_first, "m2": m_second, "m3": m_third,
        "m4": m_fourth, "co": rows_over, "nw": near_in, "s1": stage_1, "sq": stage_q, "s2": stage_2, "s2q": stage_2q,
        "s3": stage_3, "s3q": stage_3q,
    }
    at_end = (z == 0) | (z == levels - 1)
    is_end = at_end.astype(jnp.int32)

    def parts_of(plan):
        parts, pieces = [[]], []
        for entry in plan:
            if entry[0] == "co":
                parts[-1].append(entry)
            if entry[0] in ("co", "cw"):
                pieces.append(2 * entry[1] + (entry[0] == "cw"))
                parts.append([])
            else:
                parts[-1].append(entry)
        return parts, pieces

    def play(part, mid):
        def run():
            for name, turn in part:
                steps[name](turn, mid)

        return run

    (end_parts, end_pieces), (middle_parts, middle_pieces) = parts_of(END_PLAN), parts_of(MIDDLE_PLAN)

    @pl.loop(0, len(end_parts))
    def _(step):
        piece = 0
        for i in range(len(end_parts)):
            pl.when((step == i) & at_end)(play(end_parts[i], False))
            pl.when((step == i) & jnp.logical_not(at_end))(play(middle_parts[i], True))
            if i < len(end_pieces):
                chosen = is_end * end_pieces[i] + (1 - is_end) * middle_pieces[i]
                piece = piece + (step == i).astype(jnp.int32) * chosen

        @pl.when(step == 0)
        def _():
            for copy in fetch[7:]:
                copy.wait()

        @pl.when(step < len(end_pieces))
        def _():
            level = g.level_of(piece // 2)
            mine = piece % 2
            compute(level, mine * core + (1 - mine) * other)

            @pl.when(mine == 0)
            def _():
                term_over(level, other).start()

    for i in range(3):
        table_near(i, p).wait_send()
    for i in range(tiles):
        swap(i).wait_send()
    @pl.loop(0, levels)
    def _(level):
        table_over(level, core).wait_send()
        along(level, lambda way: table_far(way, level).wait_send())
        along(level, lambda way: left(g_sends, way, level, main + count))
        left(g_sends, OVER, level, lot)
        left(s_sends, 0, level, lot)

        @pl.when(level == z)
        def _():
            for sems, a_way, b_way in ((g_sends, A, B), (s_sends, 2, 1)):
                left(sems, a_way, level, count)
                left(sems, b_way, level, 2 * count)

        @pl.when(level != z)
        def _():
            for sems, a_way, b_way in ((g_sends, A, B), (s_sends, 2, 1)):
                left(sems, a_way, level, main)
                left(sems, b_way, level, 2 * main)
            left(s_sends, 3, level, main + count)


def run_fast(
    hidden, queries, out_gate, draft_kv, cache_keys, cache_values, draft_len, cache_len, o_weight, norm_gain,
    route_ids, route_weights, w_gate, w_up, w_down,
):
    levels = lax.axis_size("wide") // 4
    count, width = hidden.shape
    quarter = count // 4
    main, lot = count - quarter, 4 * count
    inner = w_gate.shape[2]
    half = jnp.bfloat16
    tile = 512
    lanes = max(128, 32 * levels)
    dma = pltpu.SemaphoreType.DMA
    vmem, smem, hbm = (pl.BlockSpec(memory_space=space) for space in (pltpu.VMEM, pltpu.SMEM, pl.ANY))
    return pl.pallas_call(
        functools.partial(fast_kernel, levels),
        out_shape=pltpu.VMEM((count, width), half),
        in_specs=[smem] * 2 + [vmem] * 3 + [hbm] * 10,
        out_specs=vmem,
        scratch_shapes=[
            pltpu.VMEM((levels, 2, lot, width), half),
            pltpu.VMEM((levels, 2, lot, width), half),
            pltpu.VMEM((levels, lot, width), half),
            pltpu.VMEM((levels, 2, main, width), half),
            pltpu.VMEM((levels, main, width), half),
            pltpu.VMEM((2, quarter, width), half),
            pltpu.VMEM((quarter, width), half),
            pltpu.VMEM((2, levels, main, width), half),
            pltpu.VMEM((2, levels, count, width), half),
            pltpu.VMEM((levels, 2, 4, count // 2, lanes), half),
            pltpu.VMEM((lot, lanes), jnp.float32),
            pltpu.VMEM(hidden.shape, half),
            pltpu.VMEM(queries.shape, half),
            pltpu.VMEM(out_gate.shape, half),
            pltpu.VMEM(draft_kv.shape, half),
            pltpu.VMEM(cache_keys.shape, half),
            pltpu.VMEM(cache_values.shape, half),
            pltpu.VMEM(o_weight.shape, half),
            pltpu.VMEM((width, inner), half),
            pltpu.VMEM((width, inner), half),
            pltpu.VMEM((inner, width), half),
            pltpu.VMEM(queries.shape, half),
            pltpu.VMEM((width // tile, 2, count, tile), jnp.float32),
            pltpu.VMEM((width // tile, count, tile), jnp.float32),
            pltpu.VMEM((count, width), jnp.float32),
            pltpu.VMEM((lot, inner), half),
            dma((10,)),
            dma((width // tile,)),
            dma((width // tile,)),
            dma((3 + 3 * levels,)),
            dma((3 + 2 * levels,)),
            dma((5, levels)),
            dma((levels, 7 + main // 8)),
            dma((4, levels)),
            dma((levels, 7 + main // 8)),
        ],
        compiler_params=pltpu.CompilerParams(
            collective_id=0, has_side_effects=True, vmem_limit_bytes=66500000
        ),
        name="run_layer",
    )(
        draft_len, cache_len, norm_gain[None, :], route_ids.T, route_weights.T, hidden, queries, out_gate, draft_kv,
        cache_keys, cache_values, o_weight, w_gate, w_up, w_down,
    )


def fits_fast(hidden_in, queries, cache_keys):
    levels = lax.axis_size("wide") // 4
    drafts = queries.shape[0] // cache_keys.shape[0]
    return (
        plane_of(lax.axis_size("rep"), lax.axis_size("wide")) == 2
        and hidden_in.shape[0] * 2 == 128
        and hidden_in.shape[1] % 512 == 0
        and drafts % 16 == 0
        and cache_keys.shape[0] % 2 == 0
        and levels * 32 == 128
    )


def on_device(
    hidden_in,
    queries,
    out_gate,
    draft_kv,
    cache_keys,
    cache_values,
    draft_len,
    cache_len,
    o_weight,
    norm_gain,
    route_ids,
    route_weights,
    w_gate,
    w_up,
    w_down,
):
    if fits_fast(hidden_in, queries, cache_keys):
        return run_fast(
            hidden_in, queries, out_gate, draft_kv, cache_keys, cache_values, draft_len, cache_len, o_weight,
            norm_gain, route_ids, route_weights, w_gate, w_up, w_down,
        )
    attended = attention_rows(
        queries, out_gate, draft_kv, cache_keys, cache_values, draft_len, cache_len
    )
    own_rows = hidden_in.shape[0]
    width = hidden_in.shape[1]
    projected = jnp.dot(attended, o_weight, preferred_element_type=jnp.float32)
    projected = projected.reshape(2, own_rows, width)
    top_count = route_ids.shape[1]
    experts = lax.axis_size("wide") * lax.axis_size("narrow")
    capacity = max(2, min(own_rows, (3 * own_rows * top_count + 2 * experts - 1) // (2 * experts)))
    slots = -(-capacity // 16) * 16
    chosen = route_ids[:, :, None] == jnp.arange(experts, dtype=jnp.int32)[None, None, :]
    dense = jnp.sum(jnp.where(chosen, route_weights[:, :, None], 0.0), axis=1)
    coarse = lax.reduce_precision(dense, 8, 7)
    weights = jnp.concatenate([coarse, dense - coarse], axis=1).astype(jnp.bfloat16)
    weights = jnp.pad(weights, ((0, 0), (0, -weights.shape[1] % 128)))
    side = plane_of(lax.axis_size("rep"), lax.axis_size("wide"))
    return run_layer(
        projected, hidden_in, norm_gain[None, :], weights, w_gate, w_up, w_down, slots, side
    )


def solution(mesh):
    placed = (
        P(("rep", "wide", "narrow"), None),
        P(("rep", "wide"), "narrow"),
        P(("rep", "wide"), "narrow"),
        P(None, ("rep", "wide"), None),
        P(("rep", "wide"), None, None),
        P(("rep", "wide"), None, None),
        P(("rep", "wide")),
        P(("rep", "wide")),
        P("narrow", None),
        P(),
        P(("rep", "wide", "narrow"), None),
        P(("rep", "wide", "narrow"), None),
        P(("wide", "narrow"), None, None),
        P(("wide", "narrow"), None, None),
        P(("wide", "narrow"), None, None),
    )
    return jax.shard_map(
        on_device,
        mesh=mesh,
        in_specs=placed,
        out_specs=P(("rep", "wide", "narrow"), None),
        check_vma=False,
    )
```
